32 devices in a mesh: dp: 8 (over z, x), fsdp: 4 (over y, core).
Axes of the slice: x: 2, y: 2, z: 4, core: 2. Of those that a mesh axis runs over, the one named last changes fastest.
Arguments:
- tokens: bfloat16 [32768, 768], P(('dp', 'fsdp')), may hold values from -6 to 6
- seg_lengths: int32 [32, 8], P(('dp', 'fsdp')), may hold values from 1 to 768, 1024 in all within a row
- cotangent: bfloat16 [32768, 768], P(('dp', 'fsdp')), may hold values from -6 to 6
- in_gain: bfloat16 [768], P(('dp', 'fsdp')), may hold values from 0.5 to 1.5
- in_bias: bfloat16 [768], P(('dp', 'fsdp')), may hold values from -1 to 1
- qkv_weight: bfloat16 [768, 2304], P(('dp', 'fsdp')), may hold values from -0.21875 to 0.21875
- qv_bias: bfloat16 [1536], P(('dp', 'fsdp')), may hold values from -1 to 1
- mid_gain: bfloat16 [768], P(('dp', 'fsdp')), may hold values from 0.5 to 1.5
- mid_bias: bfloat16 [768], P(('dp', 'fsdp')), may hold values from -1 to 1
- out_weight: bfloat16 [768, 768], P(('dp', 'fsdp')), may hold values from -0.21875 to 0.21875
- out_bias: bfloat16 [768], P(('dp', 'fsdp')), may hold values from -1 to 1
- ffn_gain: bfloat16 [768], P(('dp', 'fsdp')), may hold values from 0.5 to 1.5
- ffn_bias: bfloat16 [768], P(('dp', 'fsdp')), may hold values from -1 to 1
- up_weight: bfloat16 [768, 3072], P(('dp', 'fsdp')), may hold values from -0.21875 to 0.21875
- up_bias: bfloat16 [3072], P(('dp', 'fsdp')), may hold values from -1 to 1
- hid_gain: bfloat16 [3072], P(('dp', 'fsdp')), may hold values from 0.5 to 1.5
- hid_bias: bfloat16 [3072], P(('dp', 'fsdp')), may hold values from -1 to 1
- down_weight: bfloat16 [3072, 768], P(('dp', 'fsdp')), may hold values from -0.109375 to 0.109375
- down_bias: bfloat16 [768], P(('dp', 'fsdp')), may hold values from -1 to 1
Outputs:
- out_tokens: bfloat16 [32768, 768], P(('dp', 'fsdp'))
- grad_tokens: float32 [32768, 768], P(('dp', 'fsdp'))
- grad_in_gain: float32 [768], P(('dp', 'fsdp'))
- grad_in_bias: float32 [768], P(('dp', 'fsdp'))
- grad_qkv_weight: float32 [768, 2304], P(('dp', 'fsdp'))
- grad_qv_bias: float32 [1536], P(('dp', 'fsdp'))
- grad_mid_gain: float32 [768], P(('dp', 'fsdp'))
- grad_mid_bias: float32 [768], P(('dp', 'fsdp'))
- grad_out_weight: float32 [768, 768], P(('dp', 'fsdp'))
- grad_out_bias: float32 [768], P(('dp', 'fsdp'))
- grad_ffn_gain: float32 [768], P(('dp', 'fsdp'))
- grad_ffn_bias: float32 [768], P(('dp', 'fsdp'))
- grad_up_weight: float32 [768, 3072], P(('dp', 'fsdp'))
- grad_up_bias: float32 [3072], P(('dp', 'fsdp'))
- grad_hid_gain: float32 [3072], P(('dp', 'fsdp'))
- grad_hid_bias: float32 [3072], P(('dp', 'fsdp'))
- grad_down_weight: float32 [3072, 768], P(('dp', 'fsdp'))
- grad_down_bias: float32 [768], P(('dp', 'fsdp'))
The draws below stay inside these ranges and needn't reach their ends.
Inputs may be any that keep to these rules, and one draw needn't show every extreme that they name: `seg_lengths`: each row's 8 entries are the lengths of its packed sequences in slot order, the last entry being the padding run at the row's end; they sum to 1024, and some entry equals 768.
All inputs are finite; a program needn't handle non-finite values.
Results may differ from the reference program's by a relative error of at most 0.012.
Values may be sent and summed in bfloat16 or wider, within the bound.
No kernel may reach another device: no remote copies, remote signals or barrier semaphores. Data moves between devices by JAX's collectives and lax.ppermute only.
A program may use at most 256 MiB of HBM per device.

```python
import math
import jax
import jax.numpy as jnp
import numpy as np
from jax import lax

D = 768
FF = 3072
H = 12
HD = 64
ROW = 1024
BLOCK = 512
SEGS = 8
MOST = 768
ROWS = 32
TOKENS = 32768


def raised(drawn, key, source, target, shards_of, factor):
    def block_of(position):
        return (jnp.arange(drawn.shape[position]) // (drawn.shape[position] // shards_of)).reshape((-1,) + (1,) * (drawn.ndim - 1 - position))

    near = jax.random.permutation(key, shards_of)[block_of(target)]
    second = (block_of(target) + shards_of // 2) % shards_of
    return jnp.where((block_of(source) == near) | (block_of(source) == second), factor * drawn, drawn)


def block_scale(rng, shape, shards, least, top_value):
    def one(dim, blocks):
        heights = jax.random.uniform(jax.random.fold_in(jax.random.fold_in(rng, 6), dim), (blocks,), jnp.float32, least / len(shards), top_value / len(shards))
        return jnp.repeat(jnp.exp(heights), shape[dim] // blocks).reshape((-1,) + (1,) * (len(shape) - dim - 1))

    loudness = one(*shards[0])
    for cut in shards[1:]:
        loudness = loudness * one(*cut)
    return loudness


def split_up(number_of, total, reach, slope):
    portions = [(1 << 20) // math.isqrt(standing ** slope) + 1 for standing in range(2, number_of + 1)]
    spare, counts = total - reach - (number_of - 1), [1] * (number_of - 1)
    while spare > 0:
        movable = [i for i in range(number_of - 1) if counts[i] < reach]
        pool, remaining = sum([portions[i] for i in movable]), spare
        for i in movable:
            more = min(reach - counts[i], max(1, remaining * portions[i] // pool), spare)
            counts[i] = counts[i] + more
            spare = spare - more
    return np.array([reach] + counts)


def ragged(stream_key, number_of, total, bound, lean):
    if number_of == 2:
        one = jax.random.randint(stream_key, (), max(1, total - bound), min(bound, total - 1) + 1)
        return jnp.stack([one, total - one])
    tallies = jnp.asarray(split_up(number_of, total, bound, lean), jnp.int32)
    pairs = (number_of - 1) // 2
    giver, receiver = tallies[1:1 + 2 * pairs:2], tallies[2:2 + 2 * pairs:2]
    margin = jnp.minimum(giver - 1, bound - receiver)
    moved = jax.random.randint(jax.random.fold_in(stream_key, 1), (pairs,), 0, 1 << 20) % (margin + 1)
    tallies = tallies.at[1:1 + 2 * pairs:2].set(giver - moved).at[2:2 + 2 * pairs:2].set(receiver + moved)
    return tallies[jax.random.permutation(jax.random.fold_in(stream_key, 2), number_of)]


def gaussian(own_key, shape, width, most, pieces=(), kind=jnp.bfloat16):
    loudness = block_scale(own_key, shape, pieces, -0.22, 0.18) if pieces else 1.0
    entries = jax.random.normal(own_key, shape, jnp.float32) * width * loudness
    return jnp.minimum(jnp.maximum(entries, -most), most).astype(kind)


def gaussian_with(rng, dims, width, reach, split, heavy, kind=jnp.bfloat16):
    values = width * jax.random.normal(rng, dims, jnp.float32)
    if split:
        values = values * block_scale(rng, dims, split, -0.22, 0.18)
    return jnp.clip(raised(values, jax.random.fold_in(rng, 3), *heavy), -reach, reach).astype(kind)


def setup_inputs(seed: int = 0) -> dict:
    splits = jax.random.split(jax.random.key(seed), 20)
    return {
        "tokens": gaussian_with(splits[0], (TOKENS, D), 1.0, 6.0, ((0, 32),), (0, 1, 32, 2.75)),
        "seg_lengths": jax.vmap(lambda own: ragged(own, SEGS, ROW, MOST, 2))(jax.random.split(splits[1], ROWS)).reshape((ROWS, SEGS)).astype(jnp.int32),
        "cotangent": gaussian_with(splits[2], (TOKENS, D), 1.0, 6.0, ((0, 32),), (0, 1, 32, 2.75)),
        "in_gain": jnp.clip(1.0 + 0.1 * jax.random.normal(splits[3], (D,), jnp.float32), 0.5, 1.5).astype(jnp.bfloat16),
        "in_bias": gaussian(splits[4], (D,), 0.2, 1.0, ((0, 32),)),
        "qkv_weight": gaussian(splits[5], (D, 3 * D), D ** -0.5, 0.21875, ((0, 32),)),
        "qv_bias": gaussian(splits[6], (2 * D,), 0.2, 1.0, ((0, 32),)),
        "mid_gain": jnp.clip(1.0 + 0.1 * jax.random.normal(splits[7], (D,), jnp.float32), 0.5, 1.5).astype(jnp.bfloat16),
        "mid_bias": gaussian(splits[8], (D,), 0.2, 1.0, ((0, 32),)),
        "out_weight": gaussian(splits[9], (D, D), D ** -0.5, 0.21875, ((0, 32),)),
        "out_bias": gaussian(splits[10], (D,), 0.2, 1.0, ((0, 32),)),
        "ffn_gain": jnp.clip(1.0 + 0.1 * jax.random.normal(splits[11], (D,), jnp.float32), 0.5, 1.5).astype(jnp.bfloat16),
        "ffn_bias": gaussian(splits[12], (D,), 0.2, 1.0, ((0, 32),)),
        "up_weight": gaussian(splits[13], (D, FF), D ** -0.5, 0.21875, ((0, 32),)),
        "up_bias": gaussian(splits[14], (FF,), 0.2, 1.0, ((0, 32),)),
        "hid_gain": jnp.clip(1.0 + 0.1 * jax.random.normal(splits[15], (FF,), jnp.float32), 0.5, 1.5).astype(jnp.bfloat16),
        "hid_bias": gaussian(splits[16], (FF,), 0.2, 1.0, ((0, 32),)),
        "down_weight": gaussian(splits[17], (FF, D), FF ** -0.5, 0.109375, ((0, 32),)),
        "down_bias": gaussian(splits[18], (D,), 0.2, 1.0, ((0, 32),)),
    }


EPSILON = 1e-05
NEGATIVE = -1e+30

@jax.custom_vjp
def low(v):
    return lax.optimization_barrier(v.astype(jnp.bfloat16)).astype(jnp.float32)

@jax.custom_vjp
def low_back(v):
    return v

def low_keep(v):
    return (low(v), None)

def low_pass(kept, grad):
    return (grad,)

def back_keep(v):
    return (v, None)

def back_low(kept, grad):
    return (low(grad),)
low.defvjp(low_keep, low_pass)
low_back.defvjp(back_keep, back_low)

def layer_norm(inputs, norm_gain, norm_bias):
    center = inputs - lax.optimization_barrier(jnp.mean(inputs, axis=-1, keepdims=True))
    spread = lax.optimization_barrier(jnp.mean(center * center, axis=-1, keepdims=True))
    return center * lax.rsqrt(spread + EPSILON) * norm_gain + norm_bias

def matrix(left, right):
    return jnp.dot(left, right, precision=lax.Precision.HIGHEST)

def segment_ids(lengths):
    segment_ends = jnp.cumsum(lengths)[:-1]
    token_positions = jnp.arange(ROW, dtype=jnp.int32)
    return lax.optimization_barrier(jnp.sum((token_positions[:, None] >= segment_ends[None, :]).astype(jnp.int32), axis=1))

def attention(query_rows, key_row_slice, value_row_slice, document_ids):
    factor = 1.0 / math.sqrt(HD)
    token_positions = jnp.arange(ROW, dtype=jnp.int32)
    block_count = ROW // BLOCK
    query_blocks = query_rows.reshape(block_count, BLOCK, H, HD)
    segment_blocks = document_ids.reshape(block_count, BLOCK)
    position_blocks = token_positions.reshape(block_count, BLOCK)

    def one_block(inputs_block):
        query_block, segment_block, position_block = inputs_block
        products = jnp.einsum('qhd,khd->hqk', query_block, key_row_slice, precision=lax.Precision.HIGHEST)
        scores = low_back(products * factor)
        permitted_pairs_mask = (segment_block[:, None] == document_ids[None, :]) & (token_positions[None, :] <= position_block[:, None])
        scores = jnp.where(permitted_pairs_mask[None], scores, NEGATIVE)
        attn_probs = low(jax.nn.softmax(scores, axis=-1))
        return jnp.einsum('hqk,khd->qhd', attn_probs, value_row_slice, precision=lax.Precision.HIGHEST)
    outputs = lax.map(jax.checkpoint(one_block), (query_blocks, segment_blocks, position_blocks))
    return outputs.reshape(ROW, H, HD)

def row_forward(inputs, params, document_ids):
    in_gain, in_bias, qkv_weight, qv_bias, mid_gain, mid_bias, out_weight, out_bias, ffn_gain, ffn_bias, up_weight, up_bias, hid_gain, hid_bias, down_weight, down_bias = params
    hidden_one = low(layer_norm(inputs, in_gain, in_bias))
    qkv_bias = jnp.concatenate([qv_bias[:D], jnp.zeros((D,), jnp.float32), qv_bias[D:]])
    projected = low(low_back(matrix(hidden_one, qkv_weight) + qkv_bias))
    query_rows = projected[:, :D].reshape(ROW, H, HD)
    key_row_slice = projected[:, D:2 * D].reshape(ROW, H, HD)
    value_row_slice = projected[:, 2 * D:].reshape(ROW, H, HD)
    attended = low_back(attention(query_rows, key_row_slice, value_row_slice, document_ids)).reshape(ROW, D)
    hidden_two = low(layer_norm(attended, mid_gain, mid_bias))
    middle = inputs + low_back(matrix(hidden_two, out_weight) + out_bias)
    hidden_three = low(layer_norm(middle, ffn_gain, ffn_bias))
    upward = low_back(matrix(hidden_three, up_weight) + up_bias)
    hidden_four = low(layer_norm(jax.nn.gelu(upward, approximate=False), hid_gain, hid_bias))
    return middle + low_back(matrix(hidden_four, down_weight) + down_bias)

def reference(tokens, seg_lengths, cotangent, in_gain, in_bias, qkv_weight, qv_bias, mid_gain, mid_bias, out_weight, out_bias, ffn_gain, ffn_bias, up_weight, up_bias, hid_gain, hid_bias, down_weight, down_bias):
    params = tuple((param.astype(jnp.float32) for param in (in_gain, in_bias, qkv_weight, qv_bias, mid_gain, mid_bias, out_weight, out_bias, ffn_gain, ffn_bias, up_weight, up_bias, hid_gain, hid_bias, down_weight, down_bias)))
    inputs = tokens.astype(jnp.float32).reshape(ROWS, ROW, D)
    cotangents = cotangent.astype(jnp.float32).reshape(ROWS, ROW, D)

    def one_row(totals, entry):
        row_inputs, row_cotangent, row_lengths = entry
        document_ids = segment_ids(row_lengths)
        outputs, pullback = jax.vjp(lambda values_in, params_in: row_forward(values_in, params_in, document_ids), row_inputs, params)
        grad_inputs, grad_params = pullback(row_cotangent)
        totals = jax.tree.map(lambda left, right: left + right, totals, grad_params)
        return (totals, (outputs.astype(jnp.bfloat16), grad_inputs))
    initial = tuple((jnp.zeros_like(param) for param in params))
    grads, (outputs, grad_inputs) = lax.scan(one_row, initial, (inputs, cotangents, seg_lengths))
    return (outputs.reshape(TOKENS, D), grad_inputs.reshape(TOKENS, D), grads[0], grads[1], grads[2], grads[3], grads[4], grads[5], grads[6], grads[7], grads[8], grads[9], grads[10], grads[11], grads[12], grads[13], grads[14], grads[15])
```

```python
import functools
import math

import jax
import jax.numpy as jnp
from jax import lax
from jax.experimental import pallas as pl
from jax.experimental.pallas import tpu as pltpu
from jax.sharding import PartitionSpec as P

HD = 64
ROW = 1024
BLOCK = 512


EPSILON = 1e-05
NEGATIVE = -1e30


def layer_norm(inputs, norm_gain, norm_bias):
    center = inputs - jnp.mean(inputs, axis=-1, keepdims=True)
    spread = jnp.mean(center * center, axis=-1, keepdims=True)
    return center * lax.rsqrt(spread + EPSILON) * norm_gain + norm_bias


def gelu_norm(inputs, norm_gain, norm_bias):
    return layer_norm(jax.nn.gelu(inputs, approximate=False), norm_gain, norm_bias)


def product(left, right):
    return jnp.dot(left, right, preferred_element_type=jnp.float32)


def product_tn(left, right):
    return lax.dot_general(
        left, right, (((0,), (0,)), ((), ())), preferred_element_type=jnp.float32
    )


def product_nt(left, right):
    return lax.dot_general(
        left, right, (((1,), (1,)), ((), ())), preferred_element_type=jnp.float32
    )


def segment_ids(lengths, slots):
    order = jnp.arange(lengths.shape[0], dtype=jnp.int32)
    segment_ends = jnp.sum(jnp.where(order[None, :] <= order[:, None], lengths[None, :], 0), axis=1)[:-1]
    token_positions = jnp.arange(slots, dtype=jnp.int32)
    return jnp.sum((token_positions[:, None] >= segment_ends[None, :]).astype(jnp.int32), axis=1)


def visible_pair_grid(document_ids, query_position_index, key_position_index, window_extent):
    token_positions = jnp.arange(window_extent, dtype=jnp.int32)
    query_segment = document_ids[
        query_position_index * window_extent : (query_position_index + 1) * window_extent
    ]
    key_document_ids = document_ids[
        key_position_index * window_extent : (key_position_index + 1) * window_extent
    ]
    same = query_segment[:, None] == key_document_ids[None, :]
    causal_ordering = (
        key_position_index * window_extent + token_positions[None, :]
        <= query_position_index * window_extent + token_positions[:, None]
    )
    return (same & causal_ordering)[None]


def block_scores(query_block, key_tile_rows, factor):
    return (
        jnp.einsum("qhd,khd->hqk", query_block, key_tile_rows, preferred_element_type=jnp.float32)
        * factor
    )


def attend_forward(query_rows, key_row_slice, value_row_slice, document_ids, window_extent):
    factor = 1.0 / math.sqrt(query_rows.shape[2])
    block_count = query_rows.shape[0] // window_extent
    head_count = query_rows.shape[1]
    outputs = []
    totals = []
    for query_position_index in range(block_count):
        query_block = query_rows[
            query_position_index * window_extent : (query_position_index + 1) * window_extent
        ]
        top = jnp.full((head_count, window_extent), NEGATIVE, jnp.float32)
        mass = jnp.zeros((head_count, window_extent), jnp.float32)
        for key_position_index in range(query_position_index + 1):
            key_tile_rows = key_row_slice[
                key_position_index * window_extent : (key_position_index + 1) * window_extent
            ]
            scores = block_scores(query_block, key_tile_rows, factor)
            permitted_pairs_mask = visible_pair_grid(
                document_ids, query_position_index, key_position_index, window_extent
            )
            masked = jnp.where(permitted_pairs_mask, scores, NEGATIVE)
            newest = jnp.maximum(top, jnp.max(masked, axis=-1))
            fresh = jnp.where(permitted_pairs_mask, jnp.exp(masked - newest[:, :, None]), 0.0)
            mass = mass * jnp.exp(top - newest) + jnp.sum(fresh, axis=-1)
            top = newest
        log_total = top + jnp.log(mass)
        accum = jnp.zeros((window_extent, head_count, query_rows.shape[2]), jnp.float32)
        for key_position_index in range(query_position_index + 1):
            key_tile_rows = key_row_slice[
                key_position_index * window_extent : (key_position_index + 1) * window_extent
            ]
            value_tile_rows = value_row_slice[
                key_position_index * window_extent : (key_position_index + 1) * window_extent
            ]
            scores = block_scores(query_block, key_tile_rows, factor)
            permitted_pairs_mask = visible_pair_grid(
                document_ids, query_position_index, key_position_index, window_extent
            )
            soft_low = jnp.where(
                permitted_pairs_mask, jnp.exp(scores - log_total[:, :, None]), 0.0
            ).astype(jnp.bfloat16)
            accum = accum + jnp.einsum(
                "hqk,khd->qhd", soft_low, value_tile_rows, preferred_element_type=jnp.float32
            )
        outputs.append(accum)
        totals.append(log_total)
    return (jnp.concatenate(outputs, axis=0), totals)


def attend_backward(
    query_rows,
    key_row_slice,
    value_row_slice,
    document_ids,
    totals,
    grad_out,
    attended,
    window_extent,
):
    factor = 1.0 / math.sqrt(query_rows.shape[2])
    block_count = query_rows.shape[0] // window_extent
    row_delta = jnp.einsum("qhd,qhd->hq", grad_out.astype(jnp.float32), attended)
    zero_block = jnp.zeros((window_extent,) + query_rows.shape[1:], jnp.float32)
    grad_query = [zero_block for index in range(block_count)]
    key_gradient = [zero_block for index in range(block_count)]
    value_gradient = [zero_block for index in range(block_count)]
    for query_position_index in range(block_count):
        query_block = query_rows[
            query_position_index * window_extent : (query_position_index + 1) * window_extent
        ]
        grad_block = grad_out[
            query_position_index * window_extent : (query_position_index + 1) * window_extent
        ]
        delta_block = row_delta[
            :, query_position_index * window_extent : (query_position_index + 1) * window_extent
        ]
        for key_position_index in range(query_position_index + 1):
            key_tile_rows = key_row_slice[
                key_position_index * window_extent : (key_position_index + 1) * window_extent
            ]
            value_tile_rows = value_row_slice[
                key_position_index * window_extent : (key_position_index + 1) * window_extent
            ]
            scores = block_scores(query_block, key_tile_rows, factor)
            permitted_pairs_mask = visible_pair_grid(
                document_ids, query_position_index, key_position_index, window_extent
            )
            soft = jnp.where(
                permitted_pairs_mask,
                jnp.exp(scores - totals[query_position_index][:, :, None]),
                0.0,
            )
            value_gradient[key_position_index] = value_gradient[key_position_index] + jnp.einsum(
                "hqk,qhd->khd",
                soft.astype(jnp.bfloat16),
                grad_block,
                preferred_element_type=jnp.float32,
            )
            grad_soft = jnp.einsum(
                "qhd,khd->hqk", grad_block, value_tile_rows, preferred_element_type=jnp.float32
            )
            grad_scores = (soft * (grad_soft - delta_block[:, :, None])).astype(jnp.bfloat16)
            grad_query[query_position_index] = (
                grad_query[query_position_index]
                + jnp.einsum(
                    "hqk,khd->qhd", grad_scores, key_tile_rows, preferred_element_type=jnp.float32
                )
                * factor
            )
            key_gradient[key_position_index] = (
                key_gradient[key_position_index]
                + jnp.einsum(
                    "hqk,qhd->khd", grad_scores, query_block, preferred_element_type=jnp.float32
                )
                * factor
            )
    return (
        jnp.concatenate(grad_query, axis=0),
        jnp.concatenate(key_gradient, axis=0),
        jnp.concatenate(value_gradient, axis=0),
    )


AXES = ("dp", "fsdp")


def place():
    outer, inner = lax.axis_index("dp"), lax.axis_index("fsdp")
    return outer // 2, outer % 2, inner // 2, inner % 2


def send(values, dz=0, dx=0, dy=0, dc=0):
    pairs = []
    for z in range(4):
        for x in range(2):
            for y in range(2):
                for c in range(2):
                    here = ((z * 2 + x) * 2 + y) * 2 + c
                    there = ((((z + dz) % 4) * 2 + (x ^ dx)) * 2 + (y ^ dy)) * 2 + (c ^ dc)
                    pairs.append((here, there))
    return lax.ppermute(values, AXES, pairs)


def assemble_kernel(spot_ref, *refs):
    sources, target, sem = refs[:8], refs[8], refs[9]
    copies = []
    for part in range(8):
        for step in range(4):
            copies.append(
                pltpu.make_async_copy(
                    sources[part].at[step],
                    target.at[spot_ref[part * 4 + step]],
                    sem.at[part * 4 + step],
                )
            )
    for copy in copies:
        copy.start()
    for copy in copies:
        copy.wait()


def assemble(parts):
    rows, columns = parts[0].shape[1:]
    z, x, y, c = place()
    spots = []
    for part in range(8):
        dx, dy, dc = part >> 2 & 1, part >> 1 & 1, part & 1
        for step in range(4):
            spots.append(((((z - step) % 4) * 2 + (x ^ dx)) * 2 + (y ^ dy)) * 2 + (c ^ dc))
    whole = pl.pallas_call(
        assemble_kernel,
        out_shape=jax.ShapeDtypeStruct((32, rows, columns), parts[0].dtype),
        in_specs=[pl.BlockSpec(memory_space=pltpu.SMEM)] + [pl.BlockSpec(memory_space=pl.ANY)] * 8,
        out_specs=pl.BlockSpec(memory_space=pltpu.VMEM),
        scratch_shapes=[pltpu.SemaphoreType.DMA((32,))],
        compiler_params=pltpu.CompilerParams(vmem_limit_bytes=16 << 20),
        cost_estimate=pl.CostEstimate(flops=0, transcendentals=0, bytes_accessed=64 * rows * columns * 2),
        name="assemble",
    )(jnp.stack(spots).astype(jnp.int32), *parts)
    return whole.reshape(32 * rows, columns)


def gather(shard, way):
    near = [shard] + [send(shard, dz=step) for step in (1, 2, 3)]
    own = jnp.stack(near)
    across_x, across_y = send(own, dx=1), send(own, dy=1)
    if way == "x":
        diagonal = send(across_x, dy=1)
    elif way == "y":
        diagonal = send(across_y, dx=1)
    else:
        diagonal = send(own, dx=1, dy=1)
    parts = [own, across_y, across_x, diagonal]
    both = []
    for part in parts:
        both += [part, send(part, dc=1)]
    return assemble(both)


def wide(values):
    return values.astype(jnp.float32)


def scatter_sum(partial, way):
    rows, columns = partial.shape[0] // 32, partial.shape[1]
    z, x, y, c = place()
    view = partial.reshape(4, 2, 2, 2, rows, columns)
    pick = lax.dynamic_index_in_dim
    got = send(pick(view, 1 - c, 3, keepdims=False), dc=1)
    total = (wide(pick(view, c, 3, keepdims=False)) + wide(got)).astype(jnp.bfloat16)
    if way == "x":
        got = send(pick(total, 1 - x, 1, keepdims=False), dx=1)
        total = (wide(pick(total, x, 1, keepdims=False)) + wide(got)).astype(jnp.bfloat16)
        got = send(pick(total, 1 - y, 1, keepdims=False), dy=1)
        total = (wide(pick(total, y, 1, keepdims=False)) + wide(got)).astype(jnp.bfloat16)
    else:
        got = send(pick(total, 1 - y, 2, keepdims=False), dy=1)
        total = (wide(pick(total, y, 2, keepdims=False)) + wide(got)).astype(jnp.bfloat16)
        got = send(pick(total, 1 - x, 1, keepdims=False), dx=1)
        total = (wide(pick(total, x, 1, keepdims=False)) + wide(got)).astype(jnp.bfloat16)
    result = wide(pick(total, z, 0, keepdims=False))
    for step in (1, 2, 3):
        result = result + wide(send(pick(total, (z + step) % 4, 0, keepdims=False), dz=step))
    return result


def gather_vectors(shards):
    sizes = [shard.shape[0] for shard in shards]
    packed = jnp.concatenate(shards)
    count = packed.shape[0]
    packed = jnp.pad(packed, (0, -count % 128)).reshape(1, -1)
    z, x, y, c = place()
    first = [packed] + [
        lax.ppermute(packed, "fsdp", [(i, i ^ flip) for i in range(4)]) for flip in (1, 2, 3)
    ]
    inner = lax.axis_index("fsdp")
    ranked = jnp.stack([_choose(first, inner ^ spot) for spot in range(4)])
    outer = lax.axis_index("dp")
    second = [ranked] + [
        lax.ppermute(ranked, "dp", [(i, i ^ flip) for i in range(8)]) for flip in range(1, 8)
    ]
    everything = jnp.stack([_choose(second, outer ^ spot) for spot in range(8)]).reshape(32, -1)
    full, start = [], 0
    for size in sizes:
        full.append(everything[:, start : start + size].reshape(-1))
        start += size
    return full


def _choose(options, index):
    picked = options[0]
    for number, option in enumerate(options[1:], 1):
        picked = jnp.where(index == number, option, picked)
    return picked


def sum_vectors(vectors):
    sizes = [vector.shape[0] for vector in vectors]
    packed = jnp.concatenate(vectors).reshape(-1, 128)
    for flip in (1, 2):
        packed = packed + lax.ppermute(packed, "fsdp", [(i, i ^ flip) for i in range(4)])
    for flip in (1, 2, 4):
        packed = packed + lax.ppermute(packed, "dp", [(i, i ^ flip) for i in range(8)])
    flat = packed.reshape(-1)
    here = lax.axis_index("dp") * 4 + lax.axis_index("fsdp")
    out, start = [], 0
    for size in sizes:
        out.append(lax.dynamic_slice(flat, (start + here * (size // 32),), (size // 32,)))
        start += size
    return out


def gather_all(staged, shards):
    if not staged:
        return [lax.all_gather(shard, AXES, axis=0, tiled=True) for shard in shards]
    full = [None] * 16
    small = [index for index in range(16) if index not in (2, 6, 10, 14)]
    for index, whole in zip(small, gather_vectors([shards[index] for index in small])):
        full[index] = whole
    full[2] = gather(shards[2], "both")
    full[6] = gather(shards[6], "both")
    full[10] = gather(shards[10], "x")
    full[14] = gather(shards[14], "y")
    return full


def sum_all(staged, parts):
    if not staged:
        return [lax.psum_scatter(part, AXES, scatter_dimension=0, tiled=True) for part in parts]
    out = [None] * 16
    last = [0, 1, 3]
    early = [index for index in range(16) if index not in (2, 6, 10, 14) and index not in last]
    for group in (early, last):
        for index, total in zip(group, sum_vectors([parts[index] for index in group])):
            out[index] = total
    for index, way in ((14, "x"), (10, "y"), (6, "x"), (2, "y")):
        out[index] = scatter_sum(parts[index].astype(jnp.bfloat16), way)
    return out


def body(
    staged,
    tokens,
    seg_lengths,
    cotangent,
    in_gain,
    in_bias,
    qkv_weight,
    qv_bias,
    mid_gain,
    mid_bias,
    out_weight,
    out_bias,
    ffn_gain,
    ffn_bias,
    up_weight,
    up_bias,
    hid_gain,
    hid_bias,
    down_weight,
    down_bias,
):
    gathered = gather_all(staged, (
        in_gain, in_bias, qkv_weight, qv_bias, mid_gain, mid_bias, out_weight, out_bias, ffn_gain, ffn_bias, up_weight, up_bias, hid_gain, hid_bias, down_weight, down_bias
    ))
    model_width = tokens.shape[1]
    head_count = model_width // HD
    block_count = ROW // BLOCK
    in_gain_full = gathered[0].astype(jnp.float32)
    in_bias_full = gathered[1].astype(jnp.float32)
    qv_full = gathered[3].astype(jnp.float32)
    mid_gain_full = gathered[4].astype(jnp.float32)
    mid_bias_full = gathered[5].astype(jnp.float32)
    out_bias_full = gathered[7].astype(jnp.float32)
    ffn_gain_full = gathered[8].astype(jnp.float32)
    ffn_bias_full = gathered[9].astype(jnp.float32)
    up_bias_full = gathered[11].astype(jnp.float32)
    hid_gain_full = gathered[12].astype(jnp.float32)
    hid_bias_full = gathered[13].astype(jnp.float32)
    down_bias_full = gathered[15].astype(jnp.float32)
    qkv_bias_full = jnp.concatenate(
        [qv_full[:model_width], jnp.zeros((model_width,), jnp.float32), qv_full[model_width:]]
    )
    row_index = 0
    row_inputs = tokens.astype(jnp.float32)
    document_ids = segment_ids(seg_lengths[row_index], ROW)
    normed_one, in_back = jax.vjp(layer_norm, row_inputs, in_gain_full, in_bias_full)
    hidden_one = normed_one.astype(jnp.bfloat16)
    projected = (product(hidden_one, gathered[2]) + qkv_bias_full).astype(jnp.bfloat16)
    query_rows = projected[:, :model_width].reshape(ROW, head_count, HD)
    key_row_slice = projected[:, model_width : 2 * model_width].reshape(ROW, head_count, HD)
    value_row_slice = projected[:, 2 * model_width :].reshape(ROW, head_count, HD)
    attended, totals = attend_forward(
        query_rows, key_row_slice, value_row_slice, document_ids, BLOCK
    )
    normed_two, mid_back = jax.vjp(
        layer_norm, attended.reshape(ROW, model_width), mid_gain_full, mid_bias_full
    )
    hidden_two = normed_two.astype(jnp.bfloat16)
    middle = row_inputs + product(hidden_two, gathered[6]) + out_bias_full
    ffn_kept = []
    out_blocks = []
    for bindex in range(block_count):
        middle_block = middle[bindex * BLOCK : (bindex + 1) * BLOCK]
        normed_three, ffn_back = jax.vjp(layer_norm, middle_block, ffn_gain_full, ffn_bias_full)
        hidden_three = normed_three.astype(jnp.bfloat16)
        upward = product(hidden_three, gathered[10]) + up_bias_full
        normed_four, hid_back = jax.vjp(gelu_norm, upward, hid_gain_full, hid_bias_full)
        hidden_four = normed_four.astype(jnp.bfloat16)
        out_blocks.append(middle_block + product(hidden_four, gathered[14]) + down_bias_full)
        ffn_kept.append((ffn_back, hidden_three, hid_back, hidden_four))
    out_rows = jnp.concatenate(out_blocks, axis=0).astype(jnp.bfloat16)
    kept_rows = [
        (
            in_back,
            hidden_one,
            query_rows,
            key_row_slice,
            value_row_slice,
            document_ids,
            totals,
            attended,
            mid_back,
            hidden_two,
            ffn_kept,
        )
    ]
    weights_back = gathered
    acc_ffn_gain = jnp.zeros(ffn_gain_full.shape, jnp.float32)
    acc_ffn_bias = jnp.zeros(ffn_gain_full.shape, jnp.float32)
    acc_up_weight = jnp.zeros(gathered[10].shape, jnp.float32)
    acc_up_bias = jnp.zeros(up_bias_full.shape, jnp.float32)
    acc_hid_gain = jnp.zeros(hid_gain_full.shape, jnp.float32)
    acc_hid_bias = jnp.zeros(hid_gain_full.shape, jnp.float32)
    acc_down_weight = jnp.zeros(gathered[14].shape, jnp.float32)
    acc_down_bias = jnp.zeros(down_bias_full.shape, jnp.float32)
    row_index = 0
    ffn_kept = kept_rows[row_index][10]
    grad_blocks = []
    for bindex in range(block_count):
        ffn_back, hidden_three, hid_back, hidden_four = ffn_kept[bindex]
        start = row_index * ROW + bindex * BLOCK
        grad_final = cotangent[start : start + BLOCK].astype(jnp.float32)
        grad_low = grad_final.astype(jnp.bfloat16)
        acc_down_bias = acc_down_bias + jnp.sum(grad_low.astype(jnp.float32), axis=0)
        acc_down_weight = acc_down_weight + product_tn(hidden_four, grad_low)
        grad_four = product_nt(grad_low, weights_back[14])
        grad_up, part_gain, part_bias = hid_back(grad_four)
        acc_hid_gain = acc_hid_gain + part_gain
        acc_hid_bias = acc_hid_bias + part_bias
        grad_up_low = grad_up.astype(jnp.bfloat16)
        acc_up_bias = acc_up_bias + jnp.sum(grad_up_low.astype(jnp.float32), axis=0)
        acc_up_weight = acc_up_weight + product_tn(hidden_three, grad_up_low)
        grad_three = product_nt(grad_up_low, weights_back[10])
        grad_mid_part, part_gain, part_bias = ffn_back(grad_three)
        acc_ffn_gain = acc_ffn_gain + part_gain
        acc_ffn_bias = acc_ffn_bias + part_bias
        grad_blocks.append(grad_final + grad_mid_part)
    grad_middle_rows = [jnp.concatenate(grad_blocks, axis=0)]
    row_index = 0
    (
        in_back,
        hidden_one,
        query_rows,
        key_row_slice,
        value_row_slice,
        document_ids,
        totals,
        attended,
        mid_back,
        hidden_two,
        ffn_kept,
    ) = kept_rows[row_index]
    grad_middle = grad_middle_rows[row_index]
    grad_branch = grad_middle.astype(jnp.bfloat16)
    acc_out_bias = jnp.sum(grad_branch.astype(jnp.float32), axis=0)
    acc_out_weight = product_tn(hidden_two, grad_branch)
    grad_two = product_nt(grad_branch, weights_back[6])
    grad_attended, part_gain, part_bias = mid_back(grad_two)
    acc_mid_gain = part_gain
    acc_mid_bias = part_bias
    grad_att_low = grad_attended.astype(jnp.bfloat16).reshape(ROW, head_count, HD)
    grad_query, key_gradient, value_gradient = attend_backward(
        query_rows,
        key_row_slice,
        value_row_slice,
        document_ids,
        totals,
        grad_att_low,
        attended,
        BLOCK,
    )
    grad_projected = jnp.concatenate(
        [
            grad_query.reshape(ROW, model_width),
            key_gradient.reshape(ROW, model_width),
            value_gradient.reshape(ROW, model_width),
        ],
        axis=1,
    ).astype(jnp.bfloat16)
    column_sums = jnp.sum(grad_projected.astype(jnp.float32), axis=0)
    acc_qv_bias = jnp.concatenate([column_sums[:model_width], column_sums[2 * model_width :]])
    acc_qkv_weight = product_tn(hidden_one, grad_projected)
    grad_one = product_nt(grad_projected, weights_back[2])
    grad_input_part, part_gain, part_bias = in_back(grad_one)
    grad_rows = grad_middle + grad_input_part
    summed = sum_all(staged, (
        part_gain, part_bias, acc_qkv_weight, acc_qv_bias, acc_mid_gain, acc_mid_bias, acc_out_weight, acc_out_bias, acc_ffn_gain, acc_ffn_bias, acc_up_weight, acc_up_bias, acc_hid_gain, acc_hid_bias, acc_down_weight, acc_down_bias
    ))
    return (
        out_rows,
        grad_rows,
        summed[0],
        summed[1],
        summed[2],
        summed[3],
        summed[4],
        summed[5],
        summed[6],
        summed[7],
        summed[8],
        summed[9],
        summed[10],
        summed[11],
        summed[12],
        summed[13],
        summed[14],
        summed[15],
    )


def solution(mesh):
    in_specs = (
        P(("dp", "fsdp"), None),
        P(("dp", "fsdp"), None),
        P(("dp", "fsdp"), None),
        P(("dp", "fsdp")),
        P(("dp", "fsdp")),
        P(("dp", "fsdp"), None),
        P(("dp", "fsdp")),
        P(("dp", "fsdp")),
        P(("dp", "fsdp")),
        P(("dp", "fsdp"), None),
        P(("dp", "fsdp")),
        P(("dp", "fsdp")),
        P(("dp", "fsdp")),
        P(("dp", "fsdp"), None),
        P(("dp", "fsdp")),
        P(("dp", "fsdp")),
        P(("dp", "fsdp")),
        P(("dp", "fsdp"), None),
        P(("dp", "fsdp")),
    )
    out_specs = (
        P(("dp", "fsdp"), None),
        P(("dp", "fsdp"), None),
        P(("dp", "fsdp")),
        P(("dp", "fsdp")),
        P(("dp", "fsdp"), None),
        P(("dp", "fsdp")),
        P(("dp", "fsdp")),
        P(("dp", "fsdp")),
        P(("dp", "fsdp"), None),
        P(("dp", "fsdp")),
        P(("dp", "fsdp")),
        P(("dp", "fsdp")),
        P(("dp", "fsdp"), None),
        P(("dp", "fsdp")),
        P(("dp", "fsdp")),
        P(("dp", "fsdp")),
        P(("dp", "fsdp"), None),
        P(("dp", "fsdp")),
    )
    staged = (mesh.shape["dp"], mesh.shape["fsdp"]) == (8, 4)
    return jax.shard_map(functools.partial(body, staged), mesh=mesh, in_specs=in_specs, out_specs=out_specs, check_vma=False)
```

```python
import functools
import math

import jax
import jax.numpy as jnp
from jax import lax
from jax.experimental import pallas as pl
from jax.experimental.pallas import tpu as pltpu
from jax.sharding import PartitionSpec as P

HD = 64
EPSILON = 1e-05
NEGATIVE = -1e30
TILE = 256
CHUNK = 512
NT = (((1,), (1,)), ((), ()))
TN = (((0,), (0,)), ((), ()))
NN = (((1,), (0,)), ((), ()))
ANY = pl.BlockSpec(memory_space=pl.ANY)
SCALARS = pl.BlockSpec(memory_space=pltpu.SMEM)
GRANT = pltpu.CompilerParams(vmem_limit_bytes=58 << 20)


def dot(left, right, dims=NN):
    return lax.dot_general(left, right, dims, preferred_element_type=jnp.float32)


def wide(values):
    return values.astype(jnp.float32)


def low(values):
    return values.astype(jnp.bfloat16)


def cost(flops, size):
    return pl.CostEstimate(flops=int(0.4 * flops), transcendentals=0, bytes_accessed=int(0.4 * size))


def standardize(values):
    center = values - jnp.mean(values, axis=1, keepdims=True)
    scale = lax.rsqrt(jnp.mean(center * center, axis=1, keepdims=True) + EPSILON)
    return center * scale, scale


def standardize_back(grads, normal, scale, gain):
    inner = grads * gain
    return (
        inner
        - jnp.mean(inner, axis=1, keepdims=True)
        - normal * jnp.mean(inner * normal, axis=1, keepdims=True)
    ) * scale


def fold_rows(values):
    return jnp.sum(values.reshape(-1, 8, values.shape[1]), axis=0)


def fetch(spots_ref, sources, target, sem, start=0):
    stop = start + target.shape[1]
    if len(sources) == 1:
        return [pltpu.make_async_copy(sources[0].at[:, pl.ds(start, stop - start)], target, sem.at[0])]
    rows = sources[0].shape[1]
    left = sources[6].shape[2] if len(sources) > 8 else 0
    copies = []
    for part, source in enumerate(sources):
        begin = left if part >= 8 else 0
        low_end, high_end = max(start, begin), min(stop, begin + source.shape[2])
        if low_end >= high_end:
            continue
        for step in range(4):
            spot = pl.multiple_of(spots_ref[(part - 2 if part >= 8 else part) * 4 + step] * rows, math.gcd(rows, 128))
            copies.append(
                pltpu.make_async_copy(
                    source.at[step, :, pl.ds(low_end - begin, high_end - low_end)],
                    target.at[pl.ds(spot, rows), pl.ds(low_end - start, high_end - low_end)],
                    sem.at[len(copies)],
                )
            )
    return copies


def run_all(copies):
    for copy in copies:
        copy.start()
    for copy in copies:
        copy.wait()


def first():
    return pl.program_id(0) == 0


def rows_of(columns):
    return pl.BlockSpec((TILE, columns), lambda block: (block, 0))


def whole(shape):
    return pl.BlockSpec(shape, lambda block: (0,) * len(shape))


def project_kernel(count, spots_ref, x_ref, vectors_ref, bias_ref, *refs):
    sources, (hidden_ref, out_ref, weight_ref, sem) = refs[:count], refs[count:]

    @pl.when(first())
    def _():
        run_all(fetch(spots_ref, sources, weight_ref, sem))

    normal, _ = standardize(wide(x_ref[...]))
    hidden = low(normal * vectors_ref[6:7, :] + vectors_ref[7:8, :])
    hidden_ref[...] = hidden
    width = hidden.shape[1]
    for part in range(3):
        columns = slice(part * width, (part + 1) * width)
        out_ref[:, columns] = low(dot(hidden, weight_ref[:, columns]) + bias_ref[:, columns])


def project(spots, tokens, vectors, bias, weight):
    slots, width = tokens.shape
    return pl.pallas_call(
        functools.partial(project_kernel, len(weight)),
        grid=(slots // TILE,),
        out_shape=(
            jax.ShapeDtypeStruct((slots, width), jnp.bfloat16),
            jax.ShapeDtypeStruct((slots, 3 * width), jnp.bfloat16),
        ),
        in_specs=[SCALARS, rows_of(width), whole(vectors.shape), whole((1, 3 * width))]
        + [ANY] * len(weight),
        out_specs=(rows_of(width), rows_of(3 * width)),
        scratch_shapes=[pltpu.VMEM((width, 3 * width), jnp.bfloat16), pltpu.SemaphoreType.DMA((40,))],
        compiler_params=GRANT,
        cost_estimate=cost(6 * slots * width * width, 20 * slots * width),
        name="project",
    )(spots, tokens, vectors, bias, *weight)


def bell(values):
    square = jnp.exp(values * values * -0.5)
    step = 1.0 / (1.0 + jnp.abs(values) * (0.3275911 * math.sqrt(0.5)))
    series = step * (
        0.5 * 0.254829592
        + step
        * (
            0.5 * -0.284496736
            + step * (0.5 * 1.421413741 + step * (0.5 * -1.453152027 + step * (0.5 * 1.061405429)))
        )
    )
    tail = series * square
    below = jnp.where(values > 0, 1.0 - tail, tail)
    return values * below, below + values * square * (1.0 / math.sqrt(2.0 * math.pi))


def lift_kernel(count, spots_ref, attended_ref, x_ref, vectors_ref, up_bias_ref, gain_ref, shift_ref, *refs):
    sources = refs[:count]
    (two_ref, middle_ref, three_ref, four_ref, normal_ref, slope_ref, out_ref, up_ref, active, out_sem, up_sem) = refs[count:]

    @pl.when(first())
    def _():
        run_all(
            fetch(spots_ref, sources, out_ref, out_sem)
            + fetch(spots_ref, sources, up_ref, up_sem, out_ref.shape[1])
        )

    mid_gain, mid_bias, out_bias, ffn_gain, ffn_bias = [vectors_ref[row : row + 1, :] for row in range(5)]
    normal, _ = standardize(attended_ref[...])
    two = low(normal * mid_gain + mid_bias)
    two_ref[...] = two
    middle = wide(x_ref[...]) + dot(two, out_ref[...]) + out_bias
    middle_ref[...] = middle
    normal, _ = standardize(middle)
    three = low(normal * ffn_gain + ffn_bias)
    three_ref[...] = three
    units = up_ref.shape[1]
    spans = [slice(start, start + CHUNK) for start in range(0, units, CHUNK)]
    raise_up = lambda span: dot(three, up_ref[:, span]) + up_bias_ref[:, span]
    ahead = raise_up(spans[0])
    total = jnp.zeros((TILE, 1), jnp.float32)
    slopes = []
    for number, span in enumerate(spans):
        upward = ahead
        if number + 1 < len(spans):
            ahead = raise_up(spans[number + 1])
        value, slope = bell(upward)
        active[:, span] = value
        slope_ref[:, span] = low(slope)
        total = total + jnp.sum(value, axis=1, keepdims=True)
    mean = total * (1.0 / units)
    spread = jnp.zeros((TILE, 1), jnp.float32)
    for span in spans:
        center = active[:, span] - mean
        spread = spread + jnp.sum(center * center, axis=1, keepdims=True)
    scale = lax.rsqrt(spread * (1.0 / units) + EPSILON)
    for span in spans:
        normal = (active[:, span] - mean) * scale
        normal_ref[:, span] = low(normal)
        four_ref[:, span] = low(normal * gain_ref[:, span] + shift_ref[:, span])
        slope_ref[:, span] = low(wide(slope_ref[:, span]) * scale)


def lift(spots, attended, tokens, vectors, up_bias, gain, shift, weight):
    slots, width = tokens.shape
    units = up_bias.shape[1]
    shape = jax.ShapeDtypeStruct
    return pl.pallas_call(
        functools.partial(lift_kernel, len(weight)),
        grid=(slots // TILE,),
        out_shape=(
            shape((slots, width), jnp.bfloat16),
            shape((slots, width), jnp.float32),
            shape((slots, width), jnp.bfloat16),
            shape((slots, units), jnp.bfloat16),
            shape((slots, units), jnp.bfloat16),
            shape((slots, units), jnp.bfloat16),
        ),
        in_specs=[SCALARS, rows_of(width), rows_of(width), whole(vectors.shape)]
        + [whole((1, units))] * 3
        + [ANY] * len(weight),
        out_specs=(rows_of(width),) * 3 + (rows_of(units),) * 3,
        scratch_shapes=[
            pltpu.VMEM((width, width), jnp.bfloat16),
            pltpu.VMEM((width, units), jnp.bfloat16),
            pltpu.VMEM((TILE, units), jnp.float32),
            pltpu.SemaphoreType.DMA((40,)),
            pltpu.SemaphoreType.DMA((40,)),
        ],
        compiler_params=GRANT,
        cost_estimate=cost(2 * slots * width * (width + units), 40 * slots * width),
        name="lift",
    )(spots, attended, tokens, vectors, up_bias, gain, shift, *weight)


def drop_kernel(count, spots_ref, middle_ref, four_ref, normal_ref, slope_ref, grad_ref, gain_ref, bias_ref, *refs):
    sources = refs[:count]
    out_ref, up_ref, sums_ref, weight_ref, keep, gain_acc, shift_acc, up_acc, down_acc, sem = refs[count:]

    @pl.when(first())
    def _():
        run_all(fetch(spots_ref, sources, weight_ref, sem))
        for acc in (gain_acc, shift_acc, up_acc, down_acc):
            acc[...] = jnp.zeros_like(acc)

    units = four_ref.shape[1]
    width = middle_ref.shape[1]
    grads = grad_ref[...]
    spans = [slice(start, start + CHUNK) for start in range(0, units, CHUNK)]
    back = lambda span: dot(grads, weight_ref[span, :], NT)
    ahead = back(spans[0])
    total = jnp.zeros((TILE, 1), jnp.float32)
    cross = jnp.zeros((TILE, 1), jnp.float32)
    for number, span in enumerate(spans):
        hidden = ahead
        if number + 1 < len(spans):
            ahead = back(spans[number + 1])
        normal = wide(normal_ref[:, span])
        shift_acc[:, span] += fold_rows(hidden)
        gain_acc[:, span] += fold_rows(hidden * normal)
        inner = hidden * gain_ref[:, span]
        keep[:, span] = inner
        total = total + jnp.sum(inner, axis=1, keepdims=True)
        cross = cross + jnp.sum(inner * normal, axis=1, keepdims=True)
    out_ref[...] = low(middle_ref[...] + dot(four_ref[...], weight_ref[...]) + bias_ref[...])
    total = total * (1.0 / units)
    cross = cross * (1.0 / units)
    for span in spans:
        up = (keep[:, span] - total - wide(normal_ref[:, span]) * cross) * wide(slope_ref[:, span])
        up = low(up)
        up_ref[:, span] = up
        up_acc[:, span] += fold_rows(wide(up))
    down_acc[...] += fold_rows(wide(grads))

    @pl.when(pl.program_id(0) == pl.num_programs(0) - 1)
    def _():
        sums_ref[...] = jnp.zeros_like(sums_ref)
        row = 0
        for acc in (gain_acc, shift_acc, up_acc, down_acc):
            for start in range(0, acc.shape[1], width):
                sums_ref[row : row + 1, :] = jnp.sum(acc[:, start : start + width], axis=0, keepdims=True)
                row += 1


def drop(spots, middle, four, normal, slope, grads, gain, bias, weight):
    slots, width = middle.shape
    units = four.shape[1]
    rows = 3 * units // width + 1
    return pl.pallas_call(
        functools.partial(drop_kernel, len(weight)),
        grid=(slots // TILE,),
        out_shape=(
            jax.ShapeDtypeStruct((slots, width), jnp.bfloat16),
            jax.ShapeDtypeStruct((slots, units), jnp.bfloat16),
            jax.ShapeDtypeStruct((rows, width), jnp.float32),
        ),
        in_specs=[SCALARS, rows_of(width)]
        + [rows_of(units)] * 3
        + [rows_of(width), whole((1, units)), whole((1, width))]
        + [ANY] * len(weight),
        out_specs=(rows_of(width), rows_of(units), whole((rows, width))),
        scratch_shapes=[
            pltpu.VMEM((units, width), jnp.bfloat16),
            pltpu.VMEM((TILE, units), jnp.float32),
            pltpu.VMEM((8, units), jnp.float32),
            pltpu.VMEM((8, units), jnp.float32),
            pltpu.VMEM((8, units), jnp.float32),
            pltpu.VMEM((8, width), jnp.float32),
            pltpu.SemaphoreType.DMA((40,)),
        ],
        compiler_params=GRANT,
        cost_estimate=cost(4 * slots * width * units, 40 * slots * width),
        name="drop",
    )(spots, middle, four, normal, slope, grads, gain, bias, *weight)


def settle_kernel(count, spots_ref, up_ref, middle_ref, grad_ref, attended_ref, ffn_gain_ref, mid_gain_ref, *refs):
    sources = refs[:count]
    (total_ref, branch_ref, back_ref, sums_ref, up_weight, out_weight, acc, up_sem, out_sem) = refs[count:]

    @pl.when(first())
    def _():
        run_all(
            fetch(spots_ref, sources, out_weight, out_sem)
            + fetch(spots_ref, sources, up_weight, up_sem, out_weight.shape[1])
        )
        acc[...] = jnp.zeros_like(acc)

    three = dot(up_ref[...], up_weight[...], NT)
    normal, scale = standardize(middle_ref[...])
    acc[0] += fold_rows(three * normal)
    acc[1] += fold_rows(three)
    total = wide(grad_ref[...]) + standardize_back(three, normal, scale, ffn_gain_ref[...])
    total_ref[...] = total
    branch = low(total)
    branch_ref[...] = branch
    acc[2] += fold_rows(wide(branch))
    two = dot(branch, out_weight[...], NT)
    normal, scale = standardize(attended_ref[...])
    acc[3] += fold_rows(two * normal)
    acc[4] += fold_rows(two)
    back_ref[...] = low(standardize_back(two, normal, scale, mid_gain_ref[...]))

    @pl.when(pl.program_id(0) == pl.num_programs(0) - 1)
    def _():
        sums_ref[...] = jnp.zeros_like(sums_ref)
        for row in range(5):
            sums_ref[row : row + 1, :] = jnp.sum(acc[row], axis=0, keepdims=True)


def settle(spots, up, middle, grads, attended, ffn_gain, mid_gain, weight):
    slots, width = middle.shape
    units = up.shape[1]
    return pl.pallas_call(
        functools.partial(settle_kernel, len(weight)),
        grid=(slots // TILE,),
        out_shape=(
            jax.ShapeDtypeStruct((slots, width), jnp.float32),
            jax.ShapeDtypeStruct((slots, width), jnp.bfloat16),
            jax.ShapeDtypeStruct((slots, width), jnp.bfloat16),
            jax.ShapeDtypeStruct((8, width), jnp.float32),
        ),
        in_specs=[SCALARS, rows_of(units)]
        + [rows_of(width)] * 3
        + [whole((1, width))] * 2
        + [ANY] * len(weight),
        out_specs=(rows_of(width),) * 3 + (whole((8, width)),),
        scratch_shapes=[
            pltpu.VMEM((width, units), jnp.bfloat16),
            pltpu.VMEM((width, width), jnp.bfloat16),
            pltpu.VMEM((5, 8, width), jnp.float32),
            pltpu.SemaphoreType.DMA((40,)),
            pltpu.SemaphoreType.DMA((40,)),
        ],
        compiler_params=GRANT,
        cost_estimate=cost(2 * slots * width * (units + width), 30 * slots * width),
        name="settle",
    )(spots, up, middle, grads, attended, ffn_gain, mid_gain, *weight)


def finish_kernel(count, spots_ref, q_ref, k_ref, v_ref, x_ref, total_ref, gain_ref, *refs):
    sources, (out_ref, sums_ref, weight_ref, acc, sem) = refs[:count], refs[count:]

    @pl.when(first())
    def _():
        run_all(fetch(spots_ref, sources, weight_ref, sem))
        acc[...] = jnp.zeros_like(acc)

    width = x_ref.shape[1]
    one = dot(q_ref[...], weight_ref[:, :width], NT)
    one = one + dot(k_ref[...], weight_ref[:, width : 2 * width], NT)
    one = one + dot(v_ref[...], weight_ref[:, 2 * width :], NT)
    normal, scale = standardize(wide(x_ref[...]))
    acc[0] += fold_rows(one * normal)
    acc[1] += fold_rows(one)
    acc[2] += fold_rows(wide(q_ref[...]))
    acc[3] += fold_rows(wide(v_ref[...]))
    out_ref[...] = total_ref[...] + standardize_back(one, normal, scale, gain_ref[...])

    @pl.when(pl.program_id(0) == pl.num_programs(0) - 1)
    def _():
        sums_ref[...] = jnp.zeros_like(sums_ref)
        for row in range(4):
            sums_ref[row : row + 1, :] = jnp.sum(acc[row], axis=0, keepdims=True)


def finish(spots, grad_q, grad_k, grad_v, tokens, total, gain, weight):
    slots, width = tokens.shape
    return pl.pallas_call(
        functools.partial(finish_kernel, len(weight)),
        grid=(slots // TILE,),
        out_shape=(
            jax.ShapeDtypeStruct((slots, width), jnp.float32),
            jax.ShapeDtypeStruct((8, width), jnp.float32),
        ),
        in_specs=[SCALARS]
        + [rows_of(width)] * 5
        + [whole((1, width))]
        + [ANY] * len(weight),
        out_specs=(rows_of(width), whole((8, width))),
        scratch_shapes=[
            pltpu.VMEM((width, 3 * width), jnp.bfloat16),
            pltpu.VMEM((4, 8, width), jnp.float32),
            pltpu.SemaphoreType.DMA((40,)),
        ],
        compiler_params=GRANT,
        cost_estimate=cost(6 * slots * width * width, 24 * slots * width),
        name="finish",
    )(spots, grad_q, grad_k, grad_v, tokens, total, gain, *weight)


def outer_kernel(rows, core_ref, left_ref, right_ref, *out_refs):
    product = dot(left_ref[...], right_ref[...], TN)
    if rows is None:
        out_refs[0][...] = product.astype(out_refs[0].dtype)
        return
    near = core_ref[0] == 0
    for chip in range(product.shape[0] // (2 * rows)):
        one = low(product[chip * 2 * rows : chip * 2 * rows + rows, :])
        two = low(product[chip * 2 * rows + rows : (chip + 1) * 2 * rows, :])
        out_refs[0][chip] = jnp.where(near, one, two)
        out_refs[1][chip] = jnp.where(near, two, one)


def outer(core, left, right, rows, name, dtype=jnp.float32):
    slots, height = left.shape
    columns = right.shape[1]
    step = min(height, columns)
    tall = height > columns
    left_spec = pl.BlockSpec((slots, step), (lambda block: (0, block)) if tall else (lambda block: (0, 0)))
    right_spec = pl.BlockSpec((slots, step), (lambda block: (0, 0)) if tall else (lambda block: (0, block)))
    if rows is None:
        out_shape = (jax.ShapeDtypeStruct((height, columns), dtype),)
        out_specs = (pl.BlockSpec((step, step), (lambda block: (block, 0)) if tall else (lambda block: (0, block))),)
    else:
        out_shape = (jax.ShapeDtypeStruct((height // (2 * rows), rows, columns), jnp.bfloat16),) * 2
        out_specs = (
            pl.BlockSpec(
                (step // (2 * rows), rows, step),
                (lambda block: (block, 0, 0)) if tall else (lambda block: (0, 0, block)),
            ),
        ) * 2
    return pl.pallas_call(
        functools.partial(outer_kernel, rows),
        grid=(max(height, columns) // step,),
        out_shape=out_shape,
        in_specs=[SCALARS, left_spec, right_spec],
        out_specs=out_specs,
        compiler_params=GRANT,
        cost_estimate=cost(2 * slots * height * columns, 2 * slots * (height + columns) + 4 * height * columns),
        name=name,
    )(core, left, right)


def outer_three_kernel(rows, core_ref, left_ref, q_ref, k_ref, v_ref, *out_refs):
    width = q_ref.shape[1]
    for part, right_ref in enumerate((q_ref, k_ref, v_ref)):
        columns = slice(part * width, (part + 1) * width)
        product = dot(left_ref[...], right_ref[...], TN)
        if rows is None:
            out_refs[0][:, columns] = product
            continue
        near = core_ref[0] == 0
        for chip in range(product.shape[0] // (2 * rows)):
            first_rows = low(product[chip * 2 * rows : chip * 2 * rows + rows, :])
            second_rows = low(product[chip * 2 * rows + rows : (chip + 1) * 2 * rows, :])
            out_refs[0][chip, :, columns] = jnp.where(near, first_rows, second_rows)
            out_refs[1][chip, :, columns] = jnp.where(near, second_rows, first_rows)


def outer_three(core, left, grads, rows):
    slots, width = left.shape
    if rows is None:
        out_shape = (jax.ShapeDtypeStruct((width, 3 * width), jnp.float32),)
    else:
        out_shape = (jax.ShapeDtypeStruct((width // (2 * rows), rows, 3 * width), jnp.bfloat16),) * 2
    return pl.pallas_call(
        functools.partial(outer_three_kernel, rows),
        out_shape=out_shape,
        in_specs=[SCALARS] + [pl.BlockSpec(memory_space=pltpu.VMEM)] * 4,
        out_specs=(pl.BlockSpec(memory_space=pltpu.VMEM),) * len(out_shape),
        compiler_params=GRANT,
        cost_estimate=cost(6 * slots * width * width, 8 * slots * width + 12 * width * width),
        name="outer_three",
    )(core, left, *grads)


def halves(values):
    lane = lax.broadcasted_iota(jnp.int32, values.shape, 1)
    zero = jnp.zeros_like(values)
    return jnp.where(lane < HD, values, zero), jnp.where(lane >= HD, values, zero)


def segment_starts(lengths_ref, position):
    start = jnp.zeros_like(position)
    end = jnp.int32(0)
    for index in range(lengths_ref.shape[1] - 1):
        end = end + lengths_ref[0, index]
        start = jnp.where(position >= end, end, start)
    return start


def fill_bias(tile, slots, lengths_ref, bias_ref):
    for block in range(slots // tile):
        reach = (block + 1) * tile
        spot = block * (block + 1) // 2 * tile
        query = lax.broadcasted_iota(jnp.int32, (reach, tile), 1) + block * tile
        key = lax.broadcasted_iota(jnp.int32, (reach, tile), 0)
        start = segment_starts(lengths_ref, lax.broadcasted_iota(jnp.int32, (1, tile), 1) + block * tile)
        bias_ref[spot : spot + reach, :] = jnp.where((key <= query) & (key >= start), 0.0, NEGATIVE)


def attend_kernel(tile, lengths_ref, q_ref, k_ref, v_ref, out_ref, total_ref, bias_ref):
    slots = q_ref.shape[0]

    @pl.when(pl.program_id(0) == 0)
    def _():
        fill_bias(tile, slots, lengths_ref, bias_ref)

    values = halves(v_ref[...])
    steps = [(block, head) for block in range(slots // tile) for head in range(2)]

    def score(block, head):
        reach = (block + 1) * tile
        spot = block * (block + 1) // 2 * tile
        query = halves(q_ref[block * tile : reach, :] * jnp.bfloat16(1.0 / math.sqrt(HD)))[head]
        return dot(k_ref[:reach, :], query, NT) + bias_ref[spot : spot + reach, :]

    ahead = score(*steps[0])
    for number, (block, head) in enumerate(steps):
        reach = (block + 1) * tile
        rows = slice(block * tile, reach)
        scores = ahead
        if number + 1 < len(steps):
            ahead = score(*steps[number + 1])
        top = jnp.max(scores, axis=0, keepdims=True)
        fresh = jnp.exp(scores - top)
        mass = jnp.sum(fresh, axis=0, keepdims=True)
        part = dot(values[head][:reach, :], fresh.astype(jnp.bfloat16), TN) * (1.0 / mass)
        mixed = part if head == 0 else mixed + part
        total_ref[0, head : head + 1, rows] = top + jnp.log(mass)
        if head:
            out_ref[rows, :] = mixed.T


def attend_forward(lengths, projected, begin, pairs, tile=256):
    slots, every = projected.shape[0], projected.shape[1] // (6 * HD)
    blocks = slots // tile
    column = lambda offset: pl.BlockSpec((slots, 2 * HD), lambda pair: (0, offset + pair))
    return pl.pallas_call(
        functools.partial(attend_kernel, tile),
        grid=(pairs,),
        out_shape=(
            jax.ShapeDtypeStruct((slots, 2 * HD * pairs), jnp.float32),
            jax.ShapeDtypeStruct((pairs, 8, slots), jnp.float32),
        ),
        in_specs=[pl.BlockSpec(memory_space=pltpu.SMEM), *[column(begin + part * every) for part in range(3)]],
        out_specs=(column(0), pl.BlockSpec((1, 8, slots), lambda pair: (pair, 0, 0))),
        scratch_shapes=[pltpu.VMEM((tile * blocks * (blocks + 1) // 2, tile), jnp.float32)],
        compiler_params=GRANT,
        cost_estimate=cost(20 * 10**9, 8 * 10**6),
        name="attend_forward",
    )(lengths, projected, projected, projected)


def attend_back_kernel(tile, lengths_ref, q_ref, k_ref, v_ref, g_ref, out_ref, total_ref, gq_ref, gk_ref, gv_ref, bias_ref, gk_acc, gv_acc):
    slots = q_ref.shape[0]

    @pl.when(pl.program_id(0) == 0)
    def _():
        fill_bias(tile, slots, lengths_ref, bias_ref)

    weighed = (g_ref[...].astype(jnp.float32) * out_ref[...]).T
    deltas = [
        jnp.sum(weighed[:HD, :], axis=0, keepdims=True),
        jnp.sum(weighed[HD:, :], axis=0, keepdims=True),
    ]
    keys = halves(k_ref[...])
    steps = [(block, head) for block in reversed(range(slots // tile)) for head in range(2)]

    def begin(block, head):
        reach = (block + 1) * tile
        spot = block * (block + 1) // 2 * tile
        rows = slice(block * tile, reach)
        query = halves(q_ref[rows, :] * jnp.bfloat16(1.0 / math.sqrt(HD)))[head]
        grad = halves(g_ref[rows, :])[head]
        scores = dot(k_ref[:reach, :], query, NT) + bias_ref[spot : spot + reach, :]
        return query, grad, scores, dot(v_ref[:reach, :], grad, NT)

    ahead = begin(*steps[0])
    for number, (block, head) in enumerate(steps):
        reach = (block + 1) * tile
        rows = slice(block * tile, reach)
        query, grad, scores, grad_soft = ahead
        if number + 1 < len(steps):
            ahead = begin(*steps[number + 1])
        soft = jnp.exp(scores - total_ref[0, head : head + 1, rows])
        grad_scores = (soft * (grad_soft - deltas[head][:, rows])).astype(jnp.bfloat16)
        gv = dot(soft.astype(jnp.bfloat16), grad)
        gk = dot(grad_scores, query)
        if number == 0:
            gk_acc[...] = gk
            gv_acc[...] = gv
        else:
            gk_acc[:reach, :] += gk
            gv_acc[:reach, :] += gv
        part = dot(keys[head][:reach, :], grad_scores, TN)
        gq = part if head == 0 else gq + part
        if head:
            gq_ref[rows, :] = (gq.T * (1.0 / math.sqrt(HD))).astype(jnp.bfloat16)
    gk_ref[...] = gk_acc[...].astype(jnp.bfloat16)
    gv_ref[...] = gv_acc[...].astype(jnp.bfloat16)


def attend_backward(lengths, projected, grad_out, attended, totals, begin, tile=256):
    slots, width = attended.shape
    pairs, every = width // (2 * HD), projected.shape[1] // (6 * HD)
    blocks = slots // tile
    column = lambda offset: pl.BlockSpec((slots, 2 * HD), lambda pair: (0, offset + pair))
    return pl.pallas_call(
        functools.partial(attend_back_kernel, tile),
        grid=(pairs,),
        out_shape=(jax.ShapeDtypeStruct((slots, width), jnp.bfloat16),) * 3,
        in_specs=[
            pl.BlockSpec(memory_space=pltpu.SMEM),
            *[column(begin + part * every) for part in range(3)],
            column(begin),
            column(0),
            pl.BlockSpec((1, 8, slots), lambda pair: (pair, 0, 0)),
        ],
        out_specs=(column(0),) * 3,
        scratch_shapes=[
            pltpu.VMEM((tile * blocks * (blocks + 1) // 2, tile), jnp.float32),
            pltpu.VMEM((slots, 2 * HD), jnp.float32),
            pltpu.VMEM((slots, 2 * HD), jnp.float32),
        ],
        compiler_params=GRANT,
        cost_estimate=cost(28 * 10**9, 12 * 10**6),
        name="attend_backward",
    )(lengths, projected, projected, projected, grad_out, attended, totals)


AXES = ("dp", "fsdp")


def place():
    outer_index, inner_index = lax.axis_index("dp"), lax.axis_index("fsdp")
    return outer_index // 2, outer_index % 2, inner_index // 2, inner_index % 2


def send(values, dz=0, dx=0, dy=0, dc=0):
    pairs = []
    for z in range(4):
        for x in range(2):
            for y in range(2):
                for c in range(2):
                    here = ((z * 2 + x) * 2 + y) * 2 + c
                    there = ((((z + dz) % 4) * 2 + (x ^ dx)) * 2 + (y ^ dy)) * 2 + (c ^ dc)
                    pairs.append((here, there))
    return lax.ppermute(values, AXES, pairs)


def index_of(z, x, y, c):
    return ((z * 2 + x) * 2 + y) * 2 + c


COLUMNS_Z = [[index_of(z, x, y, c) for z in range(4)] for x in range(2) for y in range(2) for c in range(2)]


def part_spots():
    z, x, y, c = place()
    spots = []
    for part in range(8):
        dx, dy, dc = part >> 2 & 1, part >> 1 & 1, part & 1
        for step in range(4):
            spots.append(((((z - step) % 4) * 2 + (x ^ dx)) * 2 + (y ^ dy)) * 2 + (c ^ dc))
    return jnp.stack(spots).astype(jnp.int32)


def after(value, *others):
    return lax.optimization_barrier((value, *others))[0]


def send_z(shard):
    return [shard] + [send(shard, dz=step) for step in (1, 2, 3)]


def gather_z(shards, *gate):
    return jnp.stack(after(shards, *gate))


def gather_near(own):
    return own, send(own, dy=1), send(own, dx=1), send(own, dx=1, dy=1)


def gather_core(parts):
    both = []
    for part in parts:
        both += [part, send(part, dc=1)]
    return both


def chips_kernel(way, place_ref, *refs):
    x, y = place_ref[1], place_ref[2]
    count = 4 if way == "both" else 2
    sources, out_refs = refs[:-count], refs[-count:]
    start = 0
    for kept_ref, got_ref in zip(sources[::2], sources[1::2]):
        columns = slice(start, start + kept_ref.shape[2])
        start = columns.stop
        total = lambda z, x, y: low(wide(kept_ref[(z * 2 + x) * 2 + y]) + wide(got_ref[(z * 2 + x) * 2 + y]))
        for z in range(4):
            for flip, out_ref in enumerate(out_refs):
                if way == "x":
                    for other in range(2):
                        out_ref[z * 2 + other, :, columns] = total(z, x ^ flip, other)
                elif way == "y":
                    for other in range(2):
                        out_ref[z * 2 + other, :, columns] = total(z, other, y ^ flip)
                else:
                    out_ref[z, :, columns] = total(z, x ^ (flip >> 1), y ^ (flip & 1))


def lines_kernel(axis, place_ref, kept_ref, got_ref, stay_ref, go_ref):
    for z in range(4):
        for flip, out_ref in enumerate((stay_ref, go_ref)):
            spot = z * 2 + (place_ref[axis] ^ flip)
            out_ref[z] = low(wide(kept_ref[spot]) + wide(got_ref[spot]))


def planes_kernel(count, place_ref, *refs):
    sources, mine_ref, out_refs = refs[:count], refs[count], refs[count + 1 :]
    for step in range(4):
        z = (place_ref[0] + step) & 3
        total = wide(sources[0][z])
        for source in sources[1:]:
            total = total + wide(source[z])
        if step == 0:
            mine_ref[...] = total
        else:
            out_refs[step - 1][...] = low(total)


def plane_kernel(count, place_ref, *refs):
    sources, out_ref = refs[:count], refs[count]
    for z in range(4):
        total = wide(sources[0][z])
        for source in sources[1:]:
            total = total + wide(source[z])
        out_ref[z] = low(total)


def small_call(kernel, spot, arrays, out_shapes, name):
    vmem = pl.BlockSpec(memory_space=pltpu.VMEM)
    moved = sum(math.prod(a.shape) * a.dtype.itemsize for a in (*arrays, *out_shapes))
    return pl.pallas_call(
        kernel,
        out_shape=tuple(out_shapes),
        in_specs=[SCALARS] + [vmem] * len(arrays),
        out_specs=(vmem,) * len(out_shapes),
        compiler_params=GRANT,
        cost_estimate=cost(0, moved),
        name=name,
    )(spot, *arrays)


class Sum:
    def __init__(self, spot, kept, given, way, name):
        self.spot, self.way, self.name = spot, way, name
        self.rows, self.columns = kept.shape[1], 0
        self.arrays = []
        self.add(kept, given)

    def add(self, kept, given):
        self.kept = kept
        self.columns += kept.shape[2]
        self.arrays += [kept, send(given, dc=1)]

    def shapes(self, blocks, count):
        return [jax.ShapeDtypeStruct((blocks, self.rows, self.columns), jnp.bfloat16)] * count

    def chips(self, *gate):
        kernel = functools.partial(chips_kernel, self.way)
        out = self.shapes(4, 4) if self.way == "both" else self.shapes(8, 2)
        out = small_call(kernel, self.spot, (after(self.arrays[0], *gate), *self.arrays[1:]), out, "chips_" + self.name)
        if self.way == "both":
            own, to_y, to_x, to_xy = out
            self.parts = [own, send(to_y, dy=1), send(to_x, dx=1), send(to_xy, dx=1, dy=1)]
        else:
            self.pair = out[0], send(out[1], dx=int(self.way == "x"), dy=int(self.way == "y"))
        return out[0]

    def lines(self, *gate):
        kernel = functools.partial(lines_kernel, 2 if self.way == "x" else 1)
        kept, got = self.pair
        own, go = small_call(kernel, self.spot, (after(kept, *gate), got), self.shapes(4, 2), "lines_" + self.name)
        self.parts = [own, send(go, dx=int(self.way == "y"), dy=int(self.way == "x"))]
        return own

    def planes(self, *gate):
        self.parts[0] = after(self.parts[0], *gate)
        shape = (self.rows, self.columns)
        out = [jax.ShapeDtypeStruct(shape, jnp.float32)] + [jax.ShapeDtypeStruct(shape, jnp.bfloat16)] * 3
        kernel = functools.partial(planes_kernel, len(self.parts))
        mine, *others = small_call(kernel, self.spot, self.parts, out, "planes_" + self.name)
        self.others = [send(other, dz=step + 1) for step, other in enumerate(others)]
        self.mine = mine
        return mine

    def done(self):
        return self.mine + sum(wide(other) for other in self.others)

    def plane(self, *gate):
        self.parts[0] = after(self.parts[0], *gate)
        kernel = functools.partial(plane_kernel, len(self.parts))
        (total,) = small_call(kernel, self.spot, self.parts, self.shapes(4, 1), "plane_" + self.name)
        flat = total.reshape(4 * self.rows, self.columns)
        mine = lax.psum_scatter(flat, AXES, scatter_dimension=0, axis_index_groups=COLUMNS_Z, tiled=True)
        return total, wide(mine)


WIDE = ("mid_gain", "mid_bias", "out_bias", "ffn_gain", "ffn_bias", "down_bias", "in_gain", "in_bias")
DEEP = ("up_bias", "hid_gain", "hid_bias")


def spread_row(packed, width, count):
    lane = lax.broadcasted_iota(jnp.int32, (1, count), 1)
    owner = jnp.zeros_like(lane)
    for device in range(1, 32):
        owner = owner + (lane >= device * width).astype(jnp.int32)
    inside = lane - owner * width
    pick = lax.broadcasted_iota(jnp.int32, (128, count), 0) == inside
    everyone = dot(packed, low(jnp.where(pick, 1.0, 0.0)))
    owned = lax.broadcasted_iota(jnp.int32, (32, count), 0) == owner
    return jnp.sum(jnp.where(owned, everyone, 0.0), axis=0, keepdims=True)


def vectors_kernel(spots_ref, *refs):
    sources, (wide_ref, qkv_ref, deep_ref, weight_ref, landed, everything, sem, weight_sem) = refs[:8], refs[8:]
    lanes = landed.shape[3]
    copies = [
        pltpu.make_async_copy(
            source.at[:, :, pl.ds(source.shape[2] - lanes, lanes)], landed.at[part], sem.at[part]
        )
        for part, source in enumerate(sources)
    ]
    laid = [
        pltpu.make_async_copy(
            source.at[step, :, pl.ds(0, weight_ref.shape[2])],
            weight_ref.at[spots_ref[part * 4 + step]],
            weight_sem.at[part * 4 + step],
        )
        for part, source in enumerate(sources)
        for step in range(4)
    ]
    for copy in laid:
        copy.start()
    run_all(copies)
    for part in range(8):
        for step in range(4):
            everything[spots_ref[part * 4 + step]] = wide(landed[part, step])
    row = lambda number: low(everything[:, number, :])
    width = wide_ref.shape[1]
    for number in range(8):
        wide_ref[number : number + 1, :] = spread_row(row(number), width // 32, width)
    both = spread_row(row(8), width // 16, 2 * width)
    qkv_ref[:, :width] = both[:, :width]
    qkv_ref[:, width : 2 * width] = jnp.zeros((1, width), jnp.float32)
    qkv_ref[:, 2 * width :] = both[:, width:]
    units = deep_ref.shape[2]
    for number in range(3):
        deep_ref[number] = spread_row(row(9 + number), units // 32, units)
    for copy in laid:
        copy.wait()


def pack_vectors(shards, rows):
    listed = [shards[name] for name in WIDE + ("qv_bias",) + DEEP]
    packed = jnp.stack([jnp.pad(entry, (0, 128 - entry.shape[0])) for entry in listed])
    return jnp.pad(packed, ((0, rows - packed.shape[0]), (0, 0)))


def unpack_first(spots, parts, width, units):
    vmem = pl.BlockSpec(memory_space=pltpu.VMEM)
    rows = parts[0].shape[1]
    *vectors, weight = pl.pallas_call(
        vectors_kernel,
        out_shape=(
            jax.ShapeDtypeStruct((8, width), jnp.float32),
            jax.ShapeDtypeStruct((1, 3 * width), jnp.float32),
            jax.ShapeDtypeStruct((3, 1, units), jnp.float32),
            jax.ShapeDtypeStruct((32, rows, 3 * width), jnp.bfloat16),
        ),
        in_specs=[SCALARS] + [ANY] * 8,
        out_specs=(vmem,) * 4,
        scratch_shapes=[
            pltpu.VMEM((8, 4, rows, 128), jnp.bfloat16),
            pltpu.VMEM((32, rows, 128), jnp.float32),
            pltpu.SemaphoreType.DMA((8,)),
            pltpu.SemaphoreType.DMA((32,)),
        ],
        compiler_params=GRANT,
        cost_estimate=cost(10**8, 10**7),
        name="unpack",
    )(spots, *parts)
    return vectors, weight.reshape(32 * rows, 3 * width)


def sum_rows_core(rows):
    return rows + send(rows, dc=1)


def sum_rows_near(rows):
    return rows + send(rows, dy=1) + (send(rows, dx=1) + send(rows, dx=1, dy=1))


def sum_rows_z(rows):
    return rows + send(rows, dz=1) + (send(rows, dz=2) + send(rows, dz=3))


def owners_kernel(core_ref, deep_ref, mid_ref, end_ref, *out_refs):
    near = core_ref[0] == 0
    width = mid_ref.shape[1]
    per = (deep_ref.shape[0] - 1) // 3
    row = lambda ref, number: ref[number : number + 1, :]
    narrow = [row(deep_ref, 3 * per)] + [row(mid_ref, number) for number in range(5)] + [row(end_ref, number) for number in range(2)]
    broad = [
        jnp.concatenate([row(deep_ref, number * per + part) for part in range(per)], axis=1) for number in range(3)
    ]
    pair = [jnp.concatenate([row(end_ref, 2), row(end_ref, 3)], axis=1)]
    start = 0
    for group in (narrow, broad, pair):
        group = group + [jnp.zeros_like(group[0])] * (8 - len(group))
        stacked = jnp.concatenate(group, axis=0)
        share = stacked.shape[1] // 32
        stacked = jnp.concatenate([stacked, jnp.zeros((8, 128), jnp.float32)], axis=1)
        blocks = [stacked[:, owner * share : owner * share + 128] for owner in range(32)]
        for chip in range(16):
            one, two = blocks[2 * chip], blocks[2 * chip + 1]
            out_refs[0][chip, start : start + 8, :] = jnp.where(near, one, two)
            out_refs[1][chip, start : start + 8, :] = jnp.where(near, two, one)
        start += 8


SUMMED = {
    "down_bias": 0,
    "ffn_gain": 1,
    "ffn_bias": 2,
    "out_bias": 3,
    "mid_gain": 4,
    "mid_bias": 5,
    "in_gain": 6,
    "in_bias": 7,
    "hid_gain": 8,
    "hid_bias": 9,
    "up_bias": 10,
    "qv_bias": 16,
}


def lay_vectors(core, deep, mid, end):
    vmem = pl.BlockSpec(memory_space=pltpu.VMEM)
    return pl.pallas_call(
        owners_kernel,
        out_shape=(jax.ShapeDtypeStruct((16, 24, 128), jnp.float32),) * 2,
        in_specs=[SCALARS] + [vmem] * 3,
        out_specs=(vmem,) * 2,
        compiler_params=GRANT,
        cost_estimate=cost(0, 10**6),
        name="owners",
    )(core, deep, mid, end)


def halve(values, axis, place_index):
    pick = functools.partial(lax.dynamic_index_in_dim, values, axis=axis, keepdims=False)
    return pick(place_index), pick(1 - place_index)


def sum_vectors(kept, got):
    z, x, y, _ = place()
    stay, go = halve((kept + got).reshape(4, 2, 2, *kept.shape[1:]), 1, x)
    stay, go = halve(stay + send(go, dx=1), 1, y)
    plane = stay + send(go, dy=1)
    turns = [lax.dynamic_index_in_dim(plane, (z + step) % 4, keepdims=False) for step in range(4)]
    return turns[0] + sum(send(turns[step], dz=step) for step in (1, 2, 3))


WEIGHTS = ("qkv_weight", "out_weight", "up_weight", "down_weight")
PARAMS = (
    "in_gain",
    "in_bias",
    "qkv_weight",
    "qv_bias",
    "mid_gain",
    "mid_bias",
    "out_weight",
    "out_bias",
    "ffn_gain",
    "ffn_bias",
    "up_weight",
    "up_bias",
    "hid_gain",
    "hid_bias",
    "down_weight",
    "down_bias",
)


def forward_staged(spots, tokens, lengths, shards):
    width = tokens.shape[1]
    units = 32 * shards["up_bias"].shape[0]
    rows = shards["qkv_weight"].shape[0]
    whole_piece = lambda shard: [lax.all_gather(shard, AXES, axis=0, tiled=True)]
    second_piece = whole_piece(jnp.concatenate([shards["out_weight"], shards["up_weight"]], axis=1))
    first_piece = jnp.concatenate([shards["qkv_weight"], pack_vectors(shards, rows)], axis=1)
    near_first = gather_near(gather_z(send_z(first_piece)))
    vectors, weight = unpack_first(spots, gather_core(near_first), width, units)
    third_piece = send_z(after(shards["down_weight"], near_first))
    return ([weight], second_piece, third_piece), vectors


def forward_plain(spots, tokens, lengths, shards):
    width = tokens.shape[1]
    full = {name: lax.all_gather(shards[name], AXES, axis=0, tiled=True) for name in PARAMS}
    pieces = (
        [full["qkv_weight"]],
        [jnp.concatenate([full["out_weight"], full["up_weight"]], axis=1)],
        [full["down_weight"]],
    )
    full = {name: wide(full[name]) for name in PARAMS if name not in WEIGHTS}
    rows = jnp.stack([full[name] for name in WIDE])
    bias = full["qv_bias"]
    qkv_bias = jnp.concatenate([bias[:width], jnp.zeros((width,), jnp.float32), bias[width:]])[None]
    return pieces, (rows, qkv_bias, jnp.stack([full[name][None] for name in DEEP]))


def body(staged, tokens, lengths, cotangent, *params):
    shards = dict(zip(PARAMS, params))
    width = tokens.shape[1]
    pairs = width // (2 * HD)
    if staged:
        spot = jnp.stack(place()).astype(jnp.int32)
        core, spots = spot[3:4], part_spots()
    else:
        spots = core = jnp.zeros((1,), jnp.int32)
    run = forward_staged if staged else forward_plain
    pieces, (rows, qkv_bias, deep) = run(spots, tokens, lengths, shards)
    owned = {name: shards[name].shape[0] if staged else None for name in WEIGHTS}

    one, projected = project(spots, tokens, rows, qkv_bias, pieces[0])
    attended, totals = attend_forward(lengths, projected, 0, pairs)
    third_piece = pieces[2]
    if staged:
        third_piece = gather_z(third_piece, projected)
        near_third = gather_near(third_piece)
        attended = after(attended, third_piece)
    two, middle, three, four, normal, slope = lift(
        spots, attended, tokens, rows, deep[0], deep[1], deep[2], pieces[1]
    )
    if staged:
        third_piece = gather_core(after(near_third, four))
        four = after(four, near_third)
    (down,) = outer(core, four, cotangent, None, "outer_down", jnp.bfloat16)
    if staged:
        middle = after(middle, down)
    out_tokens, up, deep_sums = drop(
        spots, middle, four, normal, slope, cotangent, deep[1], rows[5:6], third_piece
    )
    up_sum = outer(core, three, up, owned["up_weight"], "outer_up")
    if staged:
        up_sum = Sum(spot, *up_sum, "both", "up")
        up = after(up, up_sum.kept)
    total, branch, back, mid_sums = settle(
        spots, up, middle, cotangent, attended, rows[3:4], rows[0:1], pieces[1]
    )
    out_sum = outer(core, two, branch, owned["out_weight"], "outer_out")
    if staged:
        up_sum.add(*out_sum)
        back = after(back, up_sum.chips(back))
    grads = attend_backward(lengths, projected, back, attended, totals, 0)
    qkv_sum = outer_three(core, one, grads, owned["qkv_weight"])
    if staged:
        kept, given = qkv_sum
        flag, up_total = up_sum.plane(kept)
        qkv_sum = Sum(spot, kept, after(given, flag), "both", "qkv")
        total = after(total, qkv_sum.chips())
    grad_tokens, end_sums = finish(spots, *grads, tokens, total, rows[6:7], pieces[0])
    down = lax.psum_scatter(down, AXES, scatter_dimension=0, tiled=True)
    summed = {"down_weight": wide(down)}
    if staged:
        units = 32 * shards["up_bias"].shape[0]
        kept, given = lay_vectors(core, deep_sums, mid_sums, end_sums)
        got = send(given, dc=1)
        flag = qkv_sum.planes(kept, down)
        summed["up_weight"], summed["out_weight"] = jnp.split(up_total, (units,), axis=1)
        summed["qkv_weight"] = qkv_sum.done()
        block = sum_vectors(kept, after(got, flag))
        summed.update({name: block[row, : shards[name].shape[0]] for name, row in SUMMED.items()})
    else:
        deep_rows = 3 * deep.shape[2] // width
        flat = deep_sums[:deep_rows].reshape(3, -1)
        vectors = dict(zip(("hid_gain", "hid_bias", "up_bias"), flat))
        vectors["down_bias"] = deep_sums[deep_rows]
        vectors.update(zip(("ffn_gain", "ffn_bias", "out_bias", "mid_gain", "mid_bias"), mid_sums))
        vectors.update(in_gain=end_sums[0], in_bias=end_sums[1], qv_bias=end_sums[2:4].reshape(-1))
        vectors.update(up_weight=up_sum[0], out_weight=out_sum[0], qkv_weight=qkv_sum[0])
        for name, vector in vectors.items():
            summed[name] = lax.psum_scatter(vector, AXES, scatter_dimension=0, tiled=True)
    return (out_tokens, grad_tokens) + tuple(summed[name] for name in PARAMS)


def solution(mesh):
    staged = (mesh.shape["dp"], mesh.shape["fsdp"]) == (8, 4)
    matrix, vector = P(AXES, None), P(AXES)
    placed = tuple(matrix if name in WEIGHTS else vector for name in PARAMS)
    return jax.shard_map(
        functools.partial(body, staged),
        mesh=mesh,
        in_specs=(matrix,) * 3 + placed,
        out_specs=(matrix,) * 2 + placed,
        check_vma=False,
    )
```

```python
import functools
import math

import jax
import jax.numpy as jnp
from jax import lax
from jax.experimental import pallas as pl
from jax.experimental.pallas import tpu as pltpu
from jax.sharding import PartitionSpec as P

HD = 64
EPSILON = 1e-05
NEGATIVE = -1e30
TILE = 256
CHUNK = 512
NT = (((1,), (1,)), ((), ()))
TN = (((0,), (0,)), ((), ()))
NN = (((1,), (0,)), ((), ()))
ANY = pl.BlockSpec(memory_space=pl.ANY)
SCALARS = pl.BlockSpec(memory_space=pltpu.SMEM)
def grant(size):
    return pltpu.CompilerParams(vmem_limit_bytes=size << 20)


def dot(left, right, dims=NN):
    return lax.dot_general(left, right, dims, preferred_element_type=jnp.float32)


def wide(values):
    return values.astype(jnp.float32)


def low(values):
    return values.astype(jnp.bfloat16)


def cost(flops, size):
    return pl.CostEstimate(flops=int(0.4 * flops), transcendentals=0, bytes_accessed=int(0.4 * size))


def standardize(values):
    center = values - jnp.mean(values, axis=1, keepdims=True)
    scale = lax.rsqrt(jnp.mean(center * center, axis=1, keepdims=True) + EPSILON)
    return center * scale, scale


def standardize_back(grads, normal, scale, gain):
    inner = grads * gain
    return (
        inner
        - jnp.mean(inner, axis=1, keepdims=True)
        - normal * jnp.mean(inner * normal, axis=1, keepdims=True)
    ) * scale


def fold_rows(values):
    return jnp.sum(values.reshape(-1, 8, values.shape[1]), axis=0)


def fetch(spots_ref, sources, target, sem, start=0):
    stop = start + target.shape[1]
    if len(sources) == 1:
        return [pltpu.make_async_copy(sources[0].at[:, pl.ds(start, stop - start)], target, sem.at[0])]
    rows = sources[0].shape[1]
    left = sources[6].shape[2] if len(sources) > 8 else 0
    copies = []
    for part, source in enumerate(sources):
        begin = left if part >= 8 else 0
        low_end, high_end = max(start, begin), min(stop, begin + source.shape[2])
        if low_end >= high_end:
            continue
        for step in range(4):
            spot = pl.multiple_of(spots_ref[(part - 2 if part >= 8 else part) * 4 + step] * rows, math.gcd(rows, 128))
            copies.append(
                pltpu.make_async_copy(
                    source.at[step, :, pl.ds(low_end - begin, high_end - low_end)],
                    target.at[pl.ds(spot, rows), pl.ds(low_end - start, high_end - low_end)],
                    sem.at[len(copies)],
                )
            )
    return copies


def run_all(copies):
    for copy in copies:
        copy.start()
    for copy in copies:
        copy.wait()


def first():
    return pl.program_id(0) == 0


def rows_of(columns):
    return pl.BlockSpec((TILE, columns), lambda block: (block, 0))


def whole(shape):
    return pl.BlockSpec(shape, lambda block: (0,) * len(shape))


def project_kernel(count, spots_ref, x_ref, vectors_ref, bias_ref, *refs):
    sources, (hidden_ref, out_ref, weight_ref, sem) = refs[:count], refs[count:]

    @pl.when(first())
    def _():
        run_all(fetch(spots_ref, sources, weight_ref, sem))

    normal, _ = standardize(wide(x_ref[...]))
    hidden = low(normal * vectors_ref[6:7, :] + vectors_ref[7:8, :])
    hidden_ref[...] = hidden
    width = hidden.shape[1]
    for part in range(3):
        columns = slice(part * width, (part + 1) * width)
        out_ref[:, columns] = low(dot(hidden, weight_ref[:, columns]) + bias_ref[:, columns])


def project(spots, tokens, vectors, bias, weight):
    slots, width = tokens.shape
    return pl.pallas_call(
        functools.partial(project_kernel, len(weight)),
        grid=(slots // TILE,),
        out_shape=(
            jax.ShapeDtypeStruct((slots, width), jnp.bfloat16),
            jax.ShapeDtypeStruct((slots, 3 * width), jnp.bfloat16),
        ),
        in_specs=[SCALARS, rows_of(width), whole(vectors.shape), whole((1, 3 * width))]
        + [ANY] * len(weight),
        out_specs=(rows_of(width), rows_of(3 * width)),
        scratch_shapes=[pltpu.VMEM((width, 3 * width), jnp.bfloat16), pltpu.SemaphoreType.DMA((40,))],
        compiler_params=grant(20),
        cost_estimate=cost(6 * slots * width * width, 20 * slots * width),
        name="project",
    )(spots, tokens, vectors, bias, *weight)


def bell(values):
    square = jnp.exp(values * values * -0.5)
    step = 1.0 / (1.0 + jnp.abs(values) * (0.3275911 * math.sqrt(0.5)))
    series = step * (
        0.5 * 0.254829592
        + step
        * (
            0.5 * -0.284496736
            + step * (0.5 * 1.421413741 + step * (0.5 * -1.453152027 + step * (0.5 * 1.061405429)))
        )
    )
    tail = series * square
    below = jnp.where(values > 0, 1.0 - tail, tail)
    return values * below, below + values * square * (1.0 / math.sqrt(2.0 * math.pi))


def lift_kernel(count, spots_ref, attended_ref, x_ref, vectors_ref, up_bias_ref, gain_ref, shift_ref, *refs):
    sources = refs[:count]
    (two_ref, middle_ref, three_ref, four_ref, normal_ref, slope_ref, scale_ref, out_ref, up_ref, active, out_sem, up_sem) = refs[count:]

    copies = fetch(spots_ref, sources, out_ref, out_sem) + fetch(spots_ref, sources, up_ref, up_sem, out_ref.shape[1])

    @pl.when(first())
    def _():
        for copy in copies:
            copy.start()
        copies[0].wait()

    mid_gain, mid_bias, out_bias, ffn_gain, ffn_bias = [vectors_ref[row : row + 1, :] for row in range(5)]
    normal, _ = standardize(attended_ref[...])
    two = low(normal * mid_gain + mid_bias)
    two_ref[...] = two
    middle = wide(x_ref[...]) + dot(two, out_ref[...]) + out_bias
    middle_ref[...] = middle
    normal, _ = standardize(middle)
    three = low(normal * ffn_gain + ffn_bias)
    three_ref[...] = three

    @pl.when(first())
    def _():
        copies[1].wait()

    units = up_ref.shape[1]
    spans = [slice(start, start + CHUNK) for start in range(0, units, CHUNK)]
    raise_up = lambda span: dot(three, up_ref[:, span]) + up_bias_ref[:, span]
    ahead = raise_up(spans[0])
    total = jnp.zeros((TILE, 1), jnp.float32)
    slopes = []
    for number, span in enumerate(spans):
        upward = ahead
        if number + 1 < len(spans):
            ahead = raise_up(spans[number + 1])
        value, slope = bell(upward)
        active[:, span] = value
        slope_ref[:, span] = low(slope)
        total = total + jnp.sum(value, axis=1, keepdims=True)
    mean = total * (1.0 / units)
    spread = jnp.zeros((TILE, 1), jnp.float32)
    for span in spans:
        center = active[:, span] - mean
        spread = spread + jnp.sum(center * center, axis=1, keepdims=True)
    scale = lax.rsqrt(spread * (1.0 / units) + EPSILON)
    scale_ref[...] = jnp.broadcast_to(scale, scale_ref.shape)
    for span in spans:
        normal = (active[:, span] - mean) * scale
        normal_ref[:, span] = low(normal)
        four_ref[:, span] = low(normal * gain_ref[:, span] + shift_ref[:, span])


def lift(spots, attended, tokens, vectors, up_bias, gain, shift, weight):
    slots, width = tokens.shape
    units = up_bias.shape[1]
    shape = jax.ShapeDtypeStruct
    return pl.pallas_call(
        functools.partial(lift_kernel, len(weight)),
        grid=(slots // TILE,),
        out_shape=(
            shape((slots, width), jnp.bfloat16),
            shape((slots, width), jnp.float32),
            shape((slots, width), jnp.bfloat16),
            shape((slots, units), jnp.bfloat16),
            shape((slots, units), jnp.bfloat16),
            shape((slots, units), jnp.bfloat16),
            shape((slots, 128), jnp.float32),
        ),
        in_specs=[SCALARS, rows_of(width), rows_of(width), whole(vectors.shape)]
        + [whole((1, units))] * 3
        + [ANY] * len(weight),
        out_specs=(rows_of(width),) * 3 + (rows_of(units),) * 3 + (rows_of(128),),
        scratch_shapes=[
            pltpu.VMEM((width, width), jnp.bfloat16),
            pltpu.VMEM((width, units), jnp.bfloat16),
            pltpu.VMEM((TILE, units), jnp.float32),
            pltpu.SemaphoreType.DMA((40,)),
            pltpu.SemaphoreType.DMA((40,)),
        ],
        compiler_params=grant(58),
        cost_estimate=cost(2 * slots * width * (width + units), 40 * slots * width),
        name="lift",
    )(spots, attended, tokens, vectors, up_bias, gain, shift, *weight)


def drop_kernel(count, spots_ref, middle_ref, four_ref, normal_ref, slope_ref, scale_ref, grad_ref, gain_ref, bias_ref, *refs):
    sources = refs[:count]
    out_ref, up_ref, sums_ref, weight_ref, keep, gain_acc, shift_acc, up_acc, down_acc, sem = refs[count:]

    @pl.when(first())
    def _():
        run_all(fetch(spots_ref, sources, weight_ref, sem))
        for acc in (gain_acc, shift_acc, up_acc, down_acc):
            acc[...] = jnp.zeros_like(acc)

    units = four_ref.shape[1]
    width = middle_ref.shape[1]
    grads = grad_ref[...]
    spans = [slice(start, start + CHUNK) for start in range(0, units, CHUNK)]
    back = lambda span: dot(grads, weight_ref[span, :], NT)
    scale = scale_ref[:, :1]
    ahead = back(spans[0])
    total = jnp.zeros((TILE, 1), jnp.float32)
    cross = jnp.zeros((TILE, 1), jnp.float32)
    for number, span in enumerate(spans):
        hidden = ahead
        if number + 1 < len(spans):
            ahead = back(spans[number + 1])
        normal = wide(normal_ref[:, span])
        shift_acc[:, span] += fold_rows(hidden)
        gain_acc[:, span] += fold_rows(hidden * normal)
        inner = hidden * gain_ref[:, span] * scale
        keep[:, span] = inner
        total = total + jnp.sum(inner, axis=1, keepdims=True)
        cross = cross + jnp.sum(inner * normal, axis=1, keepdims=True)
    out_ref[...] = low(middle_ref[...] + dot(four_ref[...], weight_ref[...]) + bias_ref[...])
    total = total * (1.0 / units)
    cross = cross * (1.0 / units)
    for span in spans:
        up = (keep[:, span] - total - wide(normal_ref[:, span]) * cross) * wide(slope_ref[:, span])
        up = low(up)
        up_ref[:, span] = up
        up_acc[:, span] += fold_rows(wide(up))
    down_acc[...] += fold_rows(wide(grads))

    @pl.when(pl.program_id(0) == pl.num_programs(0) - 1)
    def _():
        sums_ref[...] = jnp.zeros_like(sums_ref)
        row = 0
        for acc in (gain_acc, shift_acc, up_acc, down_acc):
            for start in range(0, acc.shape[1], width):
                sums_ref[row : row + 1, :] = jnp.sum(acc[:, start : start + width], axis=0, keepdims=True)
                row += 1


def drop(spots, middle, four, normal, slope, scale, grads, gain, bias, weight):
    slots, width = middle.shape
    units = four.shape[1]
    rows = 3 * units // width + 1
    return pl.pallas_call(
        functools.partial(drop_kernel, len(weight)),
        grid=(slots // TILE,),
        out_shape=(
            jax.ShapeDtypeStruct((slots, width), jnp.bfloat16),
            jax.ShapeDtypeStruct((slots, units), jnp.bfloat16),
            jax.ShapeDtypeStruct((rows, width), jnp.float32),
        ),
        in_specs=[SCALARS, rows_of(width)]
        + [rows_of(units)] * 3
        + [rows_of(128), rows_of(width), whole((1, units)), whole((1, width))]
        + [ANY] * len(weight),
        out_specs=(rows_of(width), rows_of(units), whole((rows, width))),
        scratch_shapes=[
            pltpu.VMEM((units, width), jnp.bfloat16),
            pltpu.VMEM((TILE, units), jnp.float32),
            pltpu.VMEM((8, units), jnp.float32),
            pltpu.VMEM((8, units), jnp.float32),
            pltpu.VMEM((8, units), jnp.float32),
            pltpu.VMEM((8, width), jnp.float32),
            pltpu.SemaphoreType.DMA((40,)),
        ],
        compiler_params=grant(58),
        cost_estimate=cost(4 * slots * width * units, 40 * slots * width),
        name="drop",
    )(spots, middle, four, normal, slope, scale, grads, gain, bias, *weight)


def settle_kernel(count, rows, spots_ref, up_ref, middle_ref, grad_ref, attended_ref, ffn_gain_ref, mid_gain_ref, core_ref, three_ref, columns_ref, *refs):
    sources = refs[:count]
    (total_ref, branch_ref, back_ref, sums_ref), refs = refs[count : count + 4], refs[count + 4 :]
    outer_refs, (up_weight, out_weight, acc, up_sem, out_sem) = refs[:-5], refs[-5:]

    @pl.when(first())
    def _():
        run_all(
            fetch(spots_ref, sources, out_weight, out_sem)
            + fetch(spots_ref, sources, up_weight, up_sem, out_weight.shape[1])
        )
        acc[...] = jnp.zeros_like(acc)

    three = dot(up_ref[...], up_weight[...], NT)
    outer_kernel(rows, core_ref, three_ref, columns_ref, *outer_refs)
    normal, scale = standardize(middle_ref[...])
    acc[0] += fold_rows(three * normal)
    acc[1] += fold_rows(three)
    total = wide(grad_ref[...]) + standardize_back(three, normal, scale, ffn_gain_ref[...])
    total_ref[...] = total
    branch = low(total)
    branch_ref[...] = branch
    acc[2] += fold_rows(wide(branch))
    two = dot(branch, out_weight[...], NT)
    normal, scale = standardize(attended_ref[...])
    acc[3] += fold_rows(two * normal)
    acc[4] += fold_rows(two)
    back_ref[...] = low(standardize_back(two, normal, scale, mid_gain_ref[...]))

    @pl.when(pl.program_id(0) == pl.num_programs(0) - 1)
    def _():
        sums_ref[...] = jnp.zeros_like(sums_ref)
        for row in range(5):
            sums_ref[row : row + 1, :] = jnp.sum(acc[row], axis=0, keepdims=True)


def settle(spots, core, up, middle, grads, attended, ffn_gain, mid_gain, three, rows, weight):
    slots, width = middle.shape
    units = up.shape[1]
    step = units * TILE // slots
    if rows is None:
        outer_shape = (jax.ShapeDtypeStruct((width, units), jnp.float32),)
        outer_specs = (pl.BlockSpec((width, step), lambda block: (0, block)),)
    else:
        outer_shape = (jax.ShapeDtypeStruct((width // (2 * rows), rows, units), jnp.bfloat16),) * 2
        outer_specs = (pl.BlockSpec((width // (2 * rows), rows, step), lambda block: (0, 0, block)),) * 2
    return pl.pallas_call(
        functools.partial(settle_kernel, len(weight), rows),
        grid=(slots // TILE,),
        out_shape=(
            jax.ShapeDtypeStruct((slots, width), jnp.float32),
            jax.ShapeDtypeStruct((slots, width), jnp.bfloat16),
            jax.ShapeDtypeStruct((slots, width), jnp.bfloat16),
            jax.ShapeDtypeStruct((8, width), jnp.float32),
            *outer_shape,
        ),
        in_specs=[SCALARS, rows_of(units)]
        + [rows_of(width)] * 3
        + [whole((1, width))] * 2
        + [SCALARS, whole((slots, width)), pl.BlockSpec((slots, step), lambda block: (0, block))]
        + [ANY] * len(weight),
        out_specs=(rows_of(width),) * 3 + (whole((8, width)), *outer_specs),
        scratch_shapes=[
            pltpu.VMEM((width, units), jnp.bfloat16),
            pltpu.VMEM((width, width), jnp.bfloat16),
            pltpu.VMEM((5, 8, width), jnp.float32),
            pltpu.SemaphoreType.DMA((40,)),
            pltpu.SemaphoreType.DMA((40,)),
        ],
        compiler_params=grant(58),
        cost_estimate=cost(2 * slots * width * (2 * units + width), 50 * slots * width),
        name="settle",
    )(spots, up, middle, grads, attended, ffn_gain, mid_gain, core, three, up, *weight)


def finish_kernel(count, spots_ref, q_ref, k_ref, v_ref, x_ref, total_ref, gain_ref, *refs):
    sources, (out_ref, sums_ref, weight_ref, acc, sem) = refs[:count], refs[count:]

    @pl.when(first())
    def _():
        run_all(fetch(spots_ref, sources, weight_ref, sem))
        acc[...] = jnp.zeros_like(acc)

    width = x_ref.shape[1]
    one = dot(q_ref[...], weight_ref[:, :width], NT)
    one = one + dot(k_ref[...], weight_ref[:, width : 2 * width], NT)
    one = one + dot(v_ref[...], weight_ref[:, 2 * width :], NT)
    normal, scale = standardize(wide(x_ref[...]))
    acc[0] += fold_rows(one * normal)
    acc[1] += fold_rows(one)
    acc[2] += fold_rows(wide(q_ref[...]))
    acc[3] += fold_rows(wide(v_ref[...]))
    out_ref[...] = total_ref[...] + standardize_back(one, normal, scale, gain_ref[...])

    @pl.when(pl.program_id(0) == pl.num_programs(0) - 1)
    def _():
        sums_ref[...] = jnp.zeros_like(sums_ref)
        for row in range(4):
            sums_ref[row : row + 1, :] = jnp.sum(acc[row], axis=0, keepdims=True)


def finish(spots, grad_q, grad_k, grad_v, tokens, total, gain, weight):
    slots, width = tokens.shape
    return pl.pallas_call(
        functools.partial(finish_kernel, len(weight)),
        grid=(slots // TILE,),
        out_shape=(
            jax.ShapeDtypeStruct((slots, width), jnp.float32),
            jax.ShapeDtypeStruct((8, width), jnp.float32),
        ),
        in_specs=[SCALARS]
        + [rows_of(width)] * 5
        + [whole((1, width))]
        + [ANY] * len(weight),
        out_specs=(rows_of(width), whole((8, width))),
        scratch_shapes=[
            pltpu.VMEM((width, 3 * width), jnp.bfloat16),
            pltpu.VMEM((4, 8, width), jnp.float32),
            pltpu.SemaphoreType.DMA((40,)),
        ],
        compiler_params=grant(24),
        cost_estimate=cost(6 * slots * width * width, 24 * slots * width),
        name="finish",
    )(spots, grad_q, grad_k, grad_v, tokens, total, gain, *weight)


def outer_kernel(rows, core_ref, left_ref, right_ref, *out_refs):
    product = dot(left_ref[...], right_ref[...], TN)
    if rows is None:
        out_refs[0][...] = product.astype(out_refs[0].dtype)
        return
    near = core_ref[0] == 0
    for chip in range(product.shape[0] // (2 * rows)):
        one = low(product[chip * 2 * rows : chip * 2 * rows + rows, :])
        two = low(product[chip * 2 * rows + rows : (chip + 1) * 2 * rows, :])
        out_refs[0][chip] = jnp.where(near, one, two)
        out_refs[1][chip] = jnp.where(near, two, one)


def outer(core, left, right, rows, name, dtype=jnp.float32):
    slots, height = left.shape
    columns = right.shape[1]
    step = min(height, columns)
    tall = height > columns
    left_spec = pl.BlockSpec((slots, step), (lambda block: (0, block)) if tall else (lambda block: (0, 0)))
    right_spec = pl.BlockSpec((slots, step), (lambda block: (0, 0)) if tall else (lambda block: (0, block)))
    if rows is None:
        out_shape = (jax.ShapeDtypeStruct((height, columns), dtype),)
        out_specs = (pl.BlockSpec((step, step), (lambda block: (block, 0)) if tall else (lambda block: (0, block))),)
    else:
        out_shape = (jax.ShapeDtypeStruct((height // (2 * rows), rows, columns), jnp.bfloat16),) * 2
        out_specs = (
            pl.BlockSpec(
                (step // (2 * rows), rows, step),
                (lambda block: (block, 0, 0)) if tall else (lambda block: (0, 0, block)),
            ),
        ) * 2
    return pl.pallas_call(
        functools.partial(outer_kernel, rows),
        grid=(max(height, columns) // step,),
        out_shape=out_shape,
        in_specs=[SCALARS, left_spec, right_spec],
        out_specs=out_specs,
        compiler_params=grant(58),
        cost_estimate=cost(2 * slots * height * columns, 2 * slots * (height + columns) + 4 * height * columns),
        name=name,
    )(core, left, right)


def outer_three_kernel(rows, core_ref, left_ref, q_ref, k_ref, v_ref, *out_refs):
    width = q_ref.shape[1]
    for part, right_ref in enumerate((q_ref, k_ref, v_ref)):
        columns = slice(part * width, (part + 1) * width)
        product = dot(left_ref[...], right_ref[...], TN)
        if rows is None:
            out_refs[0][:, columns] = product
            continue
        near = core_ref[0] == 0
        for chip in range(product.shape[0] // (2 * rows)):
            first_rows = low(product[chip * 2 * rows : chip * 2 * rows + rows, :])
            second_rows = low(product[chip * 2 * rows + rows : (chip + 1) * 2 * rows, :])
            out_refs[0][chip, :, columns] = jnp.where(near, first_rows, second_rows)
            out_refs[1][chip, :, columns] = jnp.where(near, second_rows, first_rows)


def outer_three(core, left, grads, rows):
    slots, width = left.shape
    if rows is None:
        out_shape = (jax.ShapeDtypeStruct((width, 3 * width), jnp.float32),)
    else:
        out_shape = (jax.ShapeDtypeStruct((width // (2 * rows), rows, 3 * width), jnp.bfloat16),) * 2
    return pl.pallas_call(
        functools.partial(outer_three_kernel, rows),
        out_shape=out_shape,
        in_specs=[SCALARS] + [pl.BlockSpec(memory_space=pltpu.VMEM)] * 4,
        out_specs=(pl.BlockSpec(memory_space=pltpu.VMEM),) * len(out_shape),
        compiler_params=grant(24),
        cost_estimate=cost(6 * slots * width * width, 8 * slots * width + 12 * width * width),
        name="outer_three",
    )(core, left, *grads)


def halves(values):
    lane = lax.broadcasted_iota(jnp.int32, values.shape, 1)
    zero = jnp.zeros_like(values)
    return jnp.where(lane < HD, values, zero), jnp.where(lane >= HD, values, zero)


def segment_starts(lengths_ref, position):
    start = jnp.zeros_like(position)
    end = jnp.int32(0)
    for index in range(lengths_ref.shape[1] - 1):
        end = end + lengths_ref[0, index]
        start = jnp.where(position >= end, end, start)
    return start


def fill_bias(tile, slots, lengths_ref, bias_ref):
    for block in range(slots // tile):
        reach = (block + 1) * tile
        spot = block * (block + 1) // 2 * tile
        query = lax.broadcasted_iota(jnp.int32, (reach, tile), 1) + block * tile
        key = lax.broadcasted_iota(jnp.int32, (reach, tile), 0)
        start = segment_starts(lengths_ref, lax.broadcasted_iota(jnp.int32, (1, tile), 1) + block * tile)
        bias_ref[spot : spot + reach, :] = jnp.where((key <= query) & (key >= start), 0.0, NEGATIVE)


def attend_kernel(tile, lengths_ref, q_ref, k_ref, v_ref, out_ref, total_ref, bias_ref):
    slots = q_ref.shape[0]

    @pl.when(pl.program_id(0) == 0)
    def _():
        fill_bias(tile, slots, lengths_ref, bias_ref)

    values = halves(v_ref[...])
    steps = [(block, head) for block in range(slots // tile) for head in range(2)]

    def score(block, head):
        reach = (block + 1) * tile
        spot = block * (block + 1) // 2 * tile
        query = halves(q_ref[block * tile : reach, :] * jnp.bfloat16(1.0 / math.sqrt(HD)))[head]
        return dot(k_ref[:reach, :], query, NT) + bias_ref[spot : spot + reach, :]

    ahead = score(*steps[0])
    for number, (block, head) in enumerate(steps):
        reach = (block + 1) * tile
        rows = slice(block * tile, reach)
        scores = ahead
        if number + 1 < len(steps):
            ahead = score(*steps[number + 1])
        top = jnp.max(scores, axis=0, keepdims=True)
        fresh = jnp.exp(scores - top)
        mass = jnp.sum(fresh, axis=0, keepdims=True)
        part = dot(values[head][:reach, :], fresh.astype(jnp.bfloat16), TN) * (1.0 / mass)
        mixed = part if head == 0 else mixed + part
        total_ref[0, head : head + 1, rows] = top + jnp.log(mass)
        if head:
            out_ref[rows, :] = mixed.T


def attend_forward(lengths, projected, begin, pairs, tile=256):
    slots, every = projected.shape[0], projected.shape[1] // (6 * HD)
    blocks = slots // tile
    column = lambda offset: pl.BlockSpec((slots, 2 * HD), lambda pair: (0, offset + pair))
    return pl.pallas_call(
        functools.partial(attend_kernel, tile),
        grid=(pairs,),
        out_shape=(
            jax.ShapeDtypeStruct((slots, 2 * HD * pairs), jnp.float32),
            jax.ShapeDtypeStruct((pairs, 8, slots), jnp.float32),
        ),
        in_specs=[pl.BlockSpec(memory_space=pltpu.SMEM), *[column(begin + part * every) for part in range(3)]],
        out_specs=(column(0), pl.BlockSpec((1, 8, slots), lambda pair: (pair, 0, 0))),
        scratch_shapes=[pltpu.VMEM((tile * blocks * (blocks + 1) // 2, tile), jnp.float32)],
        compiler_params=grant(24),
        cost_estimate=cost(20 * 10**9, 8 * 10**6),
        name="attend_forward",
    )(lengths, projected, projected, projected)


def attend_back_kernel(tile, lengths_ref, q_ref, k_ref, v_ref, g_ref, out_ref, total_ref, gq_ref, gk_ref, gv_ref, bias_ref, gk_acc, gv_acc):
    slots = q_ref.shape[0]

    @pl.when(pl.program_id(0) == 0)
    def _():
        fill_bias(tile, slots, lengths_ref, bias_ref)

    weighed = (g_ref[...].astype(jnp.float32) * out_ref[...]).T
    deltas = [
        jnp.sum(weighed[:HD, :], axis=0, keepdims=True),
        jnp.sum(weighed[HD:, :], axis=0, keepdims=True),
    ]
    keys = halves(k_ref[...])
    steps = [(block, head) for block in reversed(range(slots // tile)) for head in range(2)]

    def begin(block, head):
        reach = (block + 1) * tile
        spot = block * (block + 1) // 2 * tile
        rows = slice(block * tile, reach)
        query = halves(q_ref[rows, :] * jnp.bfloat16(1.0 / math.sqrt(HD)))[head]
        grad = halves(g_ref[rows, :])[head]
        scores = dot(k_ref[:reach, :], query, NT) + bias_ref[spot : spot + reach, :]
        return query, grad, scores, dot(v_ref[:reach, :], grad, NT)

    ahead = begin(*steps[0])
    for number, (block, head) in enumerate(steps):
        reach = (block + 1) * tile
        rows = slice(block * tile, reach)
        query, grad, scores, grad_soft = ahead
        if number + 1 < len(steps):
            ahead = begin(*steps[number + 1])
        soft = jnp.exp(scores - total_ref[0, head : head + 1, rows])
        grad_scores = (soft * (grad_soft - deltas[head][:, rows])).astype(jnp.bfloat16)
        gv = dot(soft.astype(jnp.bfloat16), grad)
        gk = dot(grad_scores, query)
        if number == 0:
            gk_acc[...] = gk
            gv_acc[...] = gv
        else:
            gk_acc[:reach, :] += gk
            gv_acc[:reach, :] += gv
        part = dot(keys[head][:reach, :], grad_scores, TN)
        gq = part if head == 0 else gq + part
        if head:
            gq_ref[rows, :] = (gq.T * (1.0 / math.sqrt(HD))).astype(jnp.bfloat16)
    gk_ref[...] = gk_acc[...].astype(jnp.bfloat16)
    gv_ref[...] = gv_acc[...].astype(jnp.bfloat16)


def attend_backward(lengths, projected, grad_out, attended, totals, begin, tile=256):
    slots, width = attended.shape
    pairs, every = width // (2 * HD), projected.shape[1] // (6 * HD)
    blocks = slots // tile
    column = lambda offset: pl.BlockSpec((slots, 2 * HD), lambda pair: (0, offset + pair))
    return pl.pallas_call(
        functools.partial(attend_back_kernel, tile),
        grid=(pairs,),
        out_shape=(jax.ShapeDtypeStruct((slots, width), jnp.bfloat16),) * 3,
        in_specs=[
            pl.BlockSpec(memory_space=pltpu.SMEM),
            *[column(begin + part * every) for part in range(3)],
            column(begin),
            column(0),
            pl.BlockSpec((1, 8, slots), lambda pair: (pair, 0, 0)),
        ],
        out_specs=(column(0),) * 3,
        scratch_shapes=[
            pltpu.VMEM((tile * blocks * (blocks + 1) // 2, tile), jnp.float32),
            pltpu.VMEM((slots, 2 * HD), jnp.float32),
            pltpu.VMEM((slots, 2 * HD), jnp.float32),
        ],
        compiler_params=grant(28),
        cost_estimate=cost(28 * 10**9, 12 * 10**6),
        name="attend_backward",
    )(lengths, projected, projected, projected, grad_out, attended, totals)


AXES = ("dp", "fsdp")


def place():
    outer_index, inner_index = lax.axis_index("dp"), lax.axis_index("fsdp")
    return outer_index // 2, outer_index % 2, inner_index // 2, inner_index % 2


def send(values, dz=0, dx=0, dy=0, dc=0):
    pairs = []
    for z in range(4):
        for x in range(2):
            for y in range(2):
                for c in range(2):
                    here = ((z * 2 + x) * 2 + y) * 2 + c
                    there = ((((z + dz) % 4) * 2 + (x ^ dx)) * 2 + (y ^ dy)) * 2 + (c ^ dc)
                    pairs.append((here, there))
    return lax.ppermute(values, AXES, pairs)


def index_of(z, x, y, c):
    return ((z * 2 + x) * 2 + y) * 2 + c


CHIPS = [[index_of(z, x, y, c) for z in range(4) for x in range(2) for y in range(2)] for c in range(2)]
COLUMNS_Z = [[index_of(z, x, y, c) for z in range(4)] for x in range(2) for y in range(2) for c in range(2)]


def part_spots():
    z, x, y, c = place()
    spots = []
    for part in range(8):
        dx, dy, dc = part >> 2 & 1, part >> 1 & 1, part & 1
        for step in range(4):
            spots.append(((((z - step) % 4) * 2 + (x ^ dx)) * 2 + (y ^ dy)) * 2 + (c ^ dc))
    return jnp.stack(spots).astype(jnp.int32)


def after(value, *others):
    return lax.optimization_barrier((value, *others))[0]


def send_z(shard):
    return [shard] + [send(shard, dz=step) for step in (1, 2, 3)]


def gather_z(shards, *gate):
    return jnp.stack(after(shards, *gate))


def gather_near(own):
    return own, send(own, dy=1), send(own, dx=1), send(own, dx=1, dy=1)


def gather_core(parts):
    both = []
    for part in parts:
        both += [part, send(part, dc=1)]
    return both


def chips_kernel(way, place_ref, *refs):
    x, y = place_ref[1], place_ref[2]
    count = 4 if way == "both" else 2
    sources, out_refs = refs[:-count], refs[-count:]
    start = 0
    for kept_ref, got_ref in zip(sources[::2], sources[1::2]):
        columns = slice(start, start + kept_ref.shape[2])
        start = columns.stop
        total = lambda z, x, y: low(wide(kept_ref[(z * 2 + x) * 2 + y]) + wide(got_ref[(z * 2 + x) * 2 + y]))
        for z in range(4):
            for flip, out_ref in enumerate(out_refs):
                if way == "x":
                    for other in range(2):
                        out_ref[z * 2 + other, :, columns] = total(z, x ^ flip, other)
                elif way == "y":
                    for other in range(2):
                        out_ref[z * 2 + other, :, columns] = total(z, other, y ^ flip)
                else:
                    out_ref[z, :, columns] = total(z, x ^ (flip >> 1), y ^ (flip & 1))


def planes_kernel(count, place_ref, *refs):
    sources, mine_ref, out_refs = refs[:count], refs[count], refs[count + 1 :]
    for step in range(4):
        z = (place_ref[0] + step) & 3
        total = wide(sources[0][z])
        for source in sources[1:]:
            total = total + wide(source[z])
        if step == 0:
            mine_ref[...] = total
        else:
            out_refs[step - 1][...] = low(total)


def plane_kernel(count, place_ref, *refs):
    sources, out_ref = refs[:count], refs[count]
    for z in range(4):
        total = wide(sources[0][z])
        for source in sources[1:]:
            total = total + wide(source[z])
        out_ref[z] = low(total)


def small_call(kernel, spot, arrays, out_shapes, name):
    vmem = pl.BlockSpec(memory_space=pltpu.VMEM)
    moved = sum(math.prod(a.shape) * a.dtype.itemsize for a in (*arrays, *out_shapes))
    return pl.pallas_call(
        kernel,
        out_shape=tuple(out_shapes),
        in_specs=[SCALARS] + [vmem] * len(arrays),
        out_specs=(vmem,) * len(out_shapes),
        compiler_params=grant(20),
        cost_estimate=cost(0, moved),
        name=name,
    )(spot, *arrays)


class Sum:
    def __init__(self, spot, kept, given, way, name):
        self.spot, self.way, self.name = spot, way, name
        self.rows, self.columns = kept.shape[1], 0
        self.arrays = []
        self.add(kept, given)

    def add(self, kept, given):
        self.kept = kept
        self.columns += kept.shape[2]
        self.arrays += [kept, send(given, dc=1)]

    def shapes(self, blocks, count):
        return [jax.ShapeDtypeStruct((blocks, self.rows, self.columns), jnp.bfloat16)] * count

    def chips(self, *gate):
        kernel = functools.partial(chips_kernel, self.way)
        out = self.shapes(4, 4) if self.way == "both" else self.shapes(8, 2)
        out = small_call(kernel, self.spot, (after(self.arrays[0], *gate), *self.arrays[1:]), out, "chips_" + self.name)
        if self.way == "both":
            own, to_y, to_x, to_xy = out
            self.parts = [own, send(to_y, dy=1), send(to_x, dx=1), send(to_xy, dx=1, dy=1)]
        else:
            self.pair = out[0], send(out[1], dx=int(self.way == "x"), dy=int(self.way == "y"))
        return out[0]

    def planes(self, *gate):
        self.parts[0] = after(self.parts[0], *gate)
        shape = (self.rows, self.columns)
        out = [jax.ShapeDtypeStruct(shape, jnp.float32)] + [jax.ShapeDtypeStruct(shape, jnp.bfloat16)] * 3
        kernel = functools.partial(planes_kernel, len(self.parts))
        mine, *others = small_call(kernel, self.spot, self.parts, out, "planes_" + self.name)
        self.others = [send(other, dz=step + 1) for step, other in enumerate(others)]
        self.mine = mine
        return mine

    def done(self):
        return self.mine + sum(wide(other) for other in self.others)

    def plane(self, *gate):
        self.parts[0] = after(self.parts[0], *gate)
        kernel = functools.partial(plane_kernel, len(self.parts))
        (total,) = small_call(kernel, self.spot, self.parts, self.shapes(4, 1), "plane_" + self.name)
        flat = total.reshape(4 * self.rows, self.columns)
        mine = lax.psum_scatter(flat, AXES, scatter_dimension=0, axis_index_groups=COLUMNS_Z, tiled=True)
        return total, wide(mine)


WIDE = ("mid_gain", "mid_bias", "out_bias", "ffn_gain", "ffn_bias", "down_bias", "in_gain", "in_bias")
DEEP = ("up_bias", "hid_gain", "hid_bias")


def spread_row(packed, width, count):
    lane = lax.broadcasted_iota(jnp.int32, (1, count), 1)
    owner = jnp.zeros_like(lane)
    for device in range(1, 32):
        owner = owner + (lane >= device * width).astype(jnp.int32)
    inside = lane - owner * width
    pick = lax.broadcasted_iota(jnp.int32, (128, count), 0) == inside
    everyone = dot(packed, low(jnp.where(pick, 1.0, 0.0)))
    owned = lax.broadcasted_iota(jnp.int32, (32, count), 0) == owner
    return jnp.sum(jnp.where(owned, everyone, 0.0), axis=0, keepdims=True)


def vectors_kernel(spots_ref, *refs):
    sources, (wide_ref, qkv_ref, deep_ref, weight_ref, landed, everything, sem, weight_sem) = refs[:8], refs[8:]
    lanes = landed.shape[3]
    copies = [
        pltpu.make_async_copy(
            source.at[:, :, pl.ds(source.shape[2] - lanes, lanes)], landed.at[part], sem.at[part]
        )
        for part, source in enumerate(sources)
    ]
    laid = [
        pltpu.make_async_copy(
            source.at[step, :, pl.ds(0, weight_ref.shape[2])],
            weight_ref.at[spots_ref[part * 4 + step]],
            weight_sem.at[part * 4 + step],
        )
        for part, source in enumerate(sources)
        for step in range(4)
    ]
    for copy in laid:
        copy.start()
    run_all(copies)
    for part in range(8):
        for step in range(4):
            everything[spots_ref[part * 4 + step]] = wide(landed[part, step])
    row = lambda number: low(everything[:, number, :])
    width = wide_ref.shape[1]
    for number in range(8):
        wide_ref[number : number + 1, :] = spread_row(row(number), width // 32, width)
    both = spread_row(row(8), width // 16, 2 * width)
    qkv_ref[:, :width] = both[:, :width]
    qkv_ref[:, width : 2 * width] = jnp.zeros((1, width), jnp.float32)
    qkv_ref[:, 2 * width :] = both[:, width:]
    units = deep_ref.shape[2]
    for number in range(3):
        deep_ref[number] = spread_row(row(9 + number), units // 32, units)
    for copy in laid:
        copy.wait()


def pack_vectors(shards, rows):
    listed = [shards[name] for name in WIDE + ("qv_bias",) + DEEP]
    packed = jnp.stack([jnp.pad(entry, (0, 128 - entry.shape[0])) for entry in listed])
    return jnp.pad(packed, ((0, rows - packed.shape[0]), (0, 0)))


def unpack_first(spots, parts, width, units):
    vmem = pl.BlockSpec(memory_space=pltpu.VMEM)
    rows = parts[0].shape[1]
    *vectors, weight = pl.pallas_call(
        vectors_kernel,
        out_shape=(
            jax.ShapeDtypeStruct((8, width), jnp.float32),
            jax.ShapeDtypeStruct((1, 3 * width), jnp.float32),
            jax.ShapeDtypeStruct((3, 1, units), jnp.float32),
            jax.ShapeDtypeStruct((32, rows, 3 * width), jnp.bfloat16),
        ),
        in_specs=[SCALARS] + [ANY] * 8,
        out_specs=(vmem,) * 4,
        scratch_shapes=[
            pltpu.VMEM((8, 4, rows, 128), jnp.bfloat16),
            pltpu.VMEM((32, rows, 128), jnp.float32),
            pltpu.SemaphoreType.DMA((8,)),
            pltpu.SemaphoreType.DMA((32,)),
        ],
        compiler_params=grant(16),
        cost_estimate=cost(10**8, 10**7),
        name="unpack",
    )(spots, *parts)
    return vectors, weight.reshape(32 * rows, 3 * width)


def sum_rows_core(rows):
    return rows + send(rows, dc=1)


def sum_rows_near(rows):
    return rows + send(rows, dy=1) + (send(rows, dx=1) + send(rows, dx=1, dy=1))


def sum_rows_z(rows):
    return rows + send(rows, dz=1) + (send(rows, dz=2) + send(rows, dz=3))


def owners_kernel(core_ref, deep_ref, mid_ref, end_ref, *out_refs):
    near = core_ref[0] == 0
    width = mid_ref.shape[1]
    per = (deep_ref.shape[0] - 1) // 3
    row = lambda ref, number: ref[number : number + 1, :]
    narrow = [row(deep_ref, 3 * per)] + [row(mid_ref, number) for number in range(5)] + [row(end_ref, number) for number in range(2)]
    broad = [
        jnp.concatenate([row(deep_ref, number * per + part) for part in range(per)], axis=1) for number in range(3)
    ]
    pair = [jnp.concatenate([row(end_ref, 2), row(end_ref, 3)], axis=1)]
    start = 0
    for group in (narrow, broad, pair):
        group = group + [jnp.zeros_like(group[0])] * (8 - len(group))
        stacked = jnp.concatenate(group, axis=0)
        share = stacked.shape[1] // 32
        stacked = jnp.concatenate([stacked, jnp.zeros((8, 128), jnp.float32)], axis=1)
        blocks = [stacked[:, owner * share : owner * share + 128] for owner in range(32)]
        for chip in range(16):
            one, two = blocks[2 * chip], blocks[2 * chip + 1]
            out_refs[0][chip, start : start + 8, :] = jnp.where(near, one, two)
            out_refs[1][chip, start : start + 8, :] = jnp.where(near, two, one)
        start += 8


SUMMED = {
    "down_bias": 0,
    "ffn_gain": 1,
    "ffn_bias": 2,
    "out_bias": 3,
    "mid_gain": 4,
    "mid_bias": 5,
    "in_gain": 6,
    "in_bias": 7,
    "hid_gain": 8,
    "hid_bias": 9,
    "up_bias": 10,
    "qv_bias": 16,
}


def lay_vectors(core, deep, mid, end):
    vmem = pl.BlockSpec(memory_space=pltpu.VMEM)
    return pl.pallas_call(
        owners_kernel,
        out_shape=(jax.ShapeDtypeStruct((16, 24, 128), jnp.float32),) * 2,
        in_specs=[SCALARS] + [vmem] * 3,
        out_specs=(vmem,) * 2,
        compiler_params=grant(8),
        cost_estimate=cost(0, 10**6),
        name="owners",
    )(core, deep, mid, end)


def sum_vectors(kept, got):
    parts = lax.all_to_all(kept + got, AXES, 0, 0, tiled=True, axis_index_groups=CHIPS)
    return jnp.sum(parts, axis=0)


WEIGHTS = ("qkv_weight", "out_weight", "up_weight", "down_weight")
PARAMS = (
    "in_gain",
    "in_bias",
    "qkv_weight",
    "qv_bias",
    "mid_gain",
    "mid_bias",
    "out_weight",
    "out_bias",
    "ffn_gain",
    "ffn_bias",
    "up_weight",
    "up_bias",
    "hid_gain",
    "hid_bias",
    "down_weight",
    "down_bias",
)


def forward_staged(spots, tokens, lengths, shards):
    width = tokens.shape[1]
    units = 32 * shards["up_bias"].shape[0]
    rows = shards["qkv_weight"].shape[0]
    whole_piece = lambda shard: [lax.all_gather(shard, AXES, axis=0, tiled=True)]
    second_piece = whole_piece(jnp.concatenate([shards["out_weight"], shards["up_weight"]], axis=1))
    own = gather_z(send_z(shards["qkv_weight"]))
    own_vectors = gather_z(send_z(pack_vectors(shards, rows)))
    near_first = gather_near(jnp.concatenate([own, own_vectors], axis=2))
    vectors, weight = unpack_first(spots, gather_core(near_first), width, units)
    third_piece = send_z(after(shards["down_weight"], near_first))
    return ([weight], second_piece, third_piece), vectors


def forward_plain(spots, tokens, lengths, shards):
    width = tokens.shape[1]
    full = {name: lax.all_gather(shards[name], AXES, axis=0, tiled=True) for name in PARAMS}
    pieces = (
        [full["qkv_weight"]],
        [jnp.concatenate([full["out_weight"], full["up_weight"]], axis=1)],
        [full["down_weight"]],
    )
    full = {name: wide(full[name]) for name in PARAMS if name not in WEIGHTS}
    rows = jnp.stack([full[name] for name in WIDE])
    bias = full["qv_bias"]
    qkv_bias = jnp.concatenate([bias[:width], jnp.zeros((width,), jnp.float32), bias[width:]])[None]
    return pieces, (rows, qkv_bias, jnp.stack([full[name][None] for name in DEEP]))


def body(staged, tokens, lengths, cotangent, *params):
    shards = dict(zip(PARAMS, params))
    width = tokens.shape[1]
    pairs = width // (2 * HD)
    if staged:
        spot = jnp.stack(place()).astype(jnp.int32)
        core, spots = spot[3:4], part_spots()
    else:
        spots = core = jnp.zeros((1,), jnp.int32)
    run = forward_staged if staged else forward_plain
    pieces, (rows, qkv_bias, deep) = run(spots, tokens, lengths, shards)
    owned = {name: shards[name].shape[0] if staged else None for name in WEIGHTS}

    one, projected = project(spots, tokens, rows, qkv_bias, pieces[0])
    attended, totals = attend_forward(lengths, projected, 0, pairs)
    third_piece = pieces[2]
    if staged:
        third_piece = gather_z(third_piece, attended)
        near_third = gather_near(third_piece)
        attended = after(attended, third_piece)
    two, middle, three, four, normal, slope, scale = lift(
        spots, attended, tokens, rows, deep[0], deep[1], deep[2], pieces[1]
    )
    if staged:
        third_piece = gather_core(after(near_third, four))
        four = after(four, near_third)
    (down,) = outer(core, four, cotangent, None, "outer_down", jnp.bfloat16)
    if staged:
        middle = after(middle, down)
    out_tokens, up, deep_sums = drop(
        spots, middle, four, normal, slope, scale, cotangent, deep[1], rows[5:6], third_piece
    )
    total, branch, back, mid_sums, *up_sum = settle(
        spots, core, up, middle, cotangent, attended, rows[3:4], rows[0:1], three, owned["up_weight"], pieces[1]
    )
    if staged:
        up_sum = Sum(spot, *up_sum, "both", "up")
        two = after(two, up_sum.kept)
    out_sum = outer(core, two, branch, owned["out_weight"], "outer_out")
    if staged:
        up_sum.add(*out_sum)
        back = after(back, up_sum.chips(back))
    grads = attend_backward(lengths, projected, back, attended, totals, 0)
    qkv_sum = outer_three(core, one, grads, owned["qkv_weight"])
    if staged:
        kept, given = qkv_sum
        flag, up_total = up_sum.plane(kept)
        qkv_sum = Sum(spot, kept, after(given, flag), "both", "qkv")
        total = after(total, qkv_sum.chips())
    grad_tokens, end_sums = finish(spots, *grads, tokens, total, rows[6:7], pieces[0])
    down = lax.psum_scatter(down, AXES, scatter_dimension=0, tiled=True)
    summed = {"down_weight": wide(down)}
    if staged:
        units = 32 * shards["up_bias"].shape[0]
        kept, given = lay_vectors(core, deep_sums, mid_sums, end_sums)
        got = send(given, dc=1)
        flag = qkv_sum.planes(kept, down)
        summed["qkv_weight"] = qkv_sum.done()
        block = sum_vectors(kept, after(got, flag))
        up_total = after(up_total, block)
        summed["up_weight"], summed["out_weight"] = jnp.split(up_total, (units,), axis=1)
        summed.update({name: block[row, : shards[name].shape[0]] for name, row in SUMMED.items()})
    else:
        deep_rows = 3 * deep.shape[2] // width
        flat = deep_sums[:deep_rows].reshape(3, -1)
        vectors = dict(zip(("hid_gain", "hid_bias", "up_bias"), flat))
        vectors["down_bias"] = deep_sums[deep_rows]
        vectors.update(zip(("ffn_gain", "ffn_bias", "out_bias", "mid_gain", "mid_bias"), mid_sums))
        vectors.update(in_gain=end_sums[0], in_bias=end_sums[1], qv_bias=end_sums[2:4].reshape(-1))
        vectors.update(up_weight=up_sum[0], out_weight=out_sum[0], qkv_weight=qkv_sum[0])
        for name, vector in vectors.items():
            summed[name] = lax.psum_scatter(vector, AXES, scatter_dimension=0, tiled=True)
    return (out_tokens, grad_tokens) + tuple(summed[name] for name in PARAMS)


def solution(mesh):
    staged = (mesh.shape["dp"], mesh.shape["fsdp"]) == (8, 4)
    matrix, vector = P(AXES, None), P(AXES)
    placed = tuple(matrix if name in WEIGHTS else vector for name in PARAMS)
    return jax.shard_map(
        functools.partial(body, staged),
        mesh=mesh,
        in_specs=(matrix,) * 3 + placed,
        out_specs=(matrix,) * 2 + placed,
        check_vma=False,
    )
```

```python
import functools
import math

import jax
import jax.numpy as jnp
from jax import lax
from jax.experimental import pallas as pl
from jax.experimental.pallas import tpu as pltpu
from jax.sharding import PartitionSpec as P

HD = 64
EPSILON = 1e-05
NEGATIVE = -1e30
TILE = 256
CHUNK = 512
NT = (((1,), (1,)), ((), ()))
TN = (((0,), (0,)), ((), ()))
NN = (((1,), (0,)), ((), ()))
ANY = pl.BlockSpec(memory_space=pl.ANY)
SCALARS = pl.BlockSpec(memory_space=pltpu.SMEM)
def grant(size):
    return pltpu.CompilerParams(vmem_limit_bytes=size << 20)


def dot(left, right, dims=NN):
    return lax.dot_general(left, right, dims, preferred_element_type=jnp.float32)


def wide(values):
    return values.astype(jnp.float32)


def low(values):
    return values.astype(jnp.bfloat16)


def cost(flops, size):
    return pl.CostEstimate(flops=int(0.4 * flops), transcendentals=0, bytes_accessed=int(0.4 * size))


def standardize(values):
    center = values - jnp.mean(values, axis=1, keepdims=True)
    scale = lax.rsqrt(jnp.mean(center * center, axis=1, keepdims=True) + EPSILON)
    return center * scale, scale


def standardize_back(grads, normal, scale, gain):
    inner = grads * gain
    return (
        inner
        - jnp.mean(inner, axis=1, keepdims=True)
        - normal * jnp.mean(inner * normal, axis=1, keepdims=True)
    ) * scale


def fold_rows(values):
    return jnp.sum(values.reshape(-1, 8, values.shape[1]), axis=0)


def fetch(spots_ref, sources, target, sem, start=0):
    stop = start + target.shape[1]
    if len(sources) == 1:
        return [pltpu.make_async_copy(sources[0].at[:, pl.ds(start, stop - start)], target, sem.at[0])]
    rows = sources[0].shape[1]
    left = sources[6].shape[2] if len(sources) > 8 else 0
    copies = []
    for part, source in enumerate(sources):
        begin = left if part >= 8 else 0
        low_end, high_end = max(start, begin), min(stop, begin + source.shape[2])
        if low_end >= high_end:
            continue
        for step in range(4):
            spot = pl.multiple_of(spots_ref[(part - 2 if part >= 8 else part) * 4 + step] * rows, math.gcd(rows, 128))
            copies.append(
                pltpu.make_async_copy(
                    source.at[step, :, pl.ds(low_end - begin, high_end - low_end)],
                    target.at[pl.ds(spot, rows), pl.ds(low_end - start, high_end - low_end)],
                    sem.at[len(copies)],
                )
            )
    return copies


def run_all(copies):
    for copy in copies:
        copy.start()
    for copy in copies:
        copy.wait()


def first():
    return pl.program_id(0) == 0


def rows_of(columns):
    return pl.BlockSpec((TILE, columns), lambda block: (block, 0))


def whole(shape):
    return pl.BlockSpec(shape, lambda block: (0,) * len(shape))


def project_kernel(count, spots_ref, x_ref, vectors_ref, bias_ref, *refs):
    sources, (hidden_ref, out_ref, weight_ref, sem) = refs[:count], refs[count:]

    @pl.when(first())
    def _():
        run_all(fetch(spots_ref, sources, weight_ref, sem))

    normal, _ = standardize(wide(x_ref[...]))
    hidden = low(normal * vectors_ref[6:7, :] + vectors_ref[7:8, :])
    hidden_ref[...] = hidden
    width = hidden.shape[1]
    for part in range(3):
        columns = slice(part * width, (part + 1) * width)
        out_ref[:, columns] = low(dot(hidden, weight_ref[:, columns]) + bias_ref[:, columns])


def project(spots, tokens, vectors, bias, weight):
    slots, width = tokens.shape
    return pl.pallas_call(
        functools.partial(project_kernel, len(weight)),
        grid=(slots // TILE,),
        out_shape=(
            jax.ShapeDtypeStruct((slots, width), jnp.bfloat16),
            jax.ShapeDtypeStruct((slots, 3 * width), jnp.bfloat16),
        ),
        in_specs=[SCALARS, rows_of(width), whole(vectors.shape), whole((1, 3 * width))]
        + [ANY] * len(weight),
        out_specs=(rows_of(width), rows_of(3 * width)),
        scratch_shapes=[pltpu.VMEM((width, 3 * width), jnp.bfloat16), pltpu.SemaphoreType.DMA((40,))],
        compiler_params=grant(20),
        cost_estimate=cost(6 * slots * width * width, 20 * slots * width),
        name="project",
    )(spots, tokens, vectors, bias, *weight)


def bell(values):
    square = jnp.exp(values * values * -0.5)
    step = 1.0 / (1.0 + jnp.abs(values) * (0.3275911 * math.sqrt(0.5)))
    series = step * (
        0.5 * 0.254829592
        + step
        * (
            0.5 * -0.284496736
            + step * (0.5 * 1.421413741 + step * (0.5 * -1.453152027 + step * (0.5 * 1.061405429)))
        )
    )
    tail = series * square
    below = jnp.where(values > 0, 1.0 - tail, tail)
    return values * below, below + values * square * (1.0 / math.sqrt(2.0 * math.pi))


def lift_kernel(count, spots_ref, attended_ref, x_ref, vectors_ref, up_bias_ref, gain_ref, shift_ref, *refs):
    sources = refs[:count]
    (two_ref, middle_ref, three_ref, four_ref, normal_ref, slope_ref, scale_ref, out_ref, up_ref, active, out_sem, up_sem) = refs[count:]

    copies = fetch(spots_ref, sources, out_ref, out_sem) + fetch(spots_ref, sources, up_ref, up_sem, out_ref.shape[1])

    @pl.when(first())
    def _():
        for copy in copies:
            copy.start()
        copies[0].wait()

    mid_gain, mid_bias, out_bias, ffn_gain, ffn_bias = [vectors_ref[row : row + 1, :] for row in range(5)]
    normal, _ = standardize(attended_ref[...])
    two = low(normal * mid_gain + mid_bias)
    two_ref[...] = two
    middle = wide(x_ref[...]) + dot(two, out_ref[...]) + out_bias
    middle_ref[...] = middle
    normal, _ = standardize(middle)
    three = low(normal * ffn_gain + ffn_bias)
    three_ref[...] = three

    @pl.when(first())
    def _():
        copies[1].wait()

    units = up_ref.shape[1]
    spans = [slice(start, start + CHUNK) for start in range(0, units, CHUNK)]
    raise_up = lambda span: dot(three, up_ref[:, span]) + up_bias_ref[:, span]
    ahead = raise_up(spans[0])
    total = jnp.zeros((TILE, 1), jnp.float32)
    slopes = []
    for number, span in enumerate(spans):
        upward = ahead
        if number + 1 < len(spans):
            ahead = raise_up(spans[number + 1])
        value, slope = bell(upward)
        active[:, span] = value
        slope_ref[:, span] = low(slope)
        total = total + jnp.sum(value, axis=1, keepdims=True)
    mean = total * (1.0 / units)
    spread = jnp.zeros((TILE, 1), jnp.float32)
    for span in spans:
        center = active[:, span] - mean
        spread = spread + jnp.sum(center * center, axis=1, keepdims=True)
    scale = lax.rsqrt(spread * (1.0 / units) + EPSILON)
    scale_ref[...] = jnp.broadcast_to(scale, scale_ref.shape)
    for span in spans:
        normal = (active[:, span] - mean) * scale
        normal_ref[:, span] = low(normal)
        four_ref[:, span] = low(normal * gain_ref[:, span] + shift_ref[:, span])


def lift(spots, attended, tokens, vectors, up_bias, gain, shift, weight):
    slots, width = tokens.shape
    units = up_bias.shape[1]
    shape = jax.ShapeDtypeStruct
    return pl.pallas_call(
        functools.partial(lift_kernel, len(weight)),
        grid=(slots // TILE,),
        out_shape=(
            shape((slots, width), jnp.bfloat16),
            shape((slots, width), jnp.float32),
            shape((slots, width), jnp.bfloat16),
            shape((slots, units), jnp.bfloat16),
            shape((slots, units), jnp.bfloat16),
            shape((slots, units), jnp.bfloat16),
            shape((slots, 128), jnp.float32),
        ),
        in_specs=[SCALARS, rows_of(width), rows_of(width), whole(vectors.shape)]
        + [whole((1, units))] * 3
        + [ANY] * len(weight),
        out_specs=(rows_of(width),) * 3 + (rows_of(units),) * 3 + (rows_of(128),),
        scratch_shapes=[
            pltpu.VMEM((width, width), jnp.bfloat16),
            pltpu.VMEM((width, units), jnp.bfloat16),
            pltpu.VMEM((TILE, units), jnp.float32),
            pltpu.SemaphoreType.DMA((40,)),
            pltpu.SemaphoreType.DMA((40,)),
        ],
        compiler_params=grant(58),
        cost_estimate=cost(2 * slots * width * (width + units), 40 * slots * width),
        name="lift",
    )(spots, attended, tokens, vectors, up_bias, gain, shift, *weight)


def drop_kernel(count, spots_ref, middle_ref, four_ref, normal_ref, slope_ref, scale_ref, grad_ref, gain_ref, bias_ref, *refs):
    sources = refs[:count]
    out_ref, up_ref, sums_ref, weight_ref, keep, gain_acc, shift_acc, up_acc, down_acc, sem = refs[count:]

    @pl.when(first())
    def _():
        run_all(fetch(spots_ref, sources, weight_ref, sem))
        for acc in (gain_acc, shift_acc, up_acc, down_acc):
            acc[...] = jnp.zeros_like(acc)

    units = four_ref.shape[1]
    width = middle_ref.shape[1]
    grads = grad_ref[...]
    spans = [slice(start, start + CHUNK) for start in range(0, units, CHUNK)]
    back = lambda span: dot(grads, weight_ref[span, :], NT)
    scale = scale_ref[:, :1]
    ahead = back(spans[0])
    total = jnp.zeros((TILE, 1), jnp.float32)
    cross = jnp.zeros((TILE, 1), jnp.float32)
    for number, span in enumerate(spans):
        hidden = ahead
        if number + 1 < len(spans):
            ahead = back(spans[number + 1])
        normal = wide(normal_ref[:, span])
        shift_acc[:, span] += fold_rows(hidden)
        gain_acc[:, span] += fold_rows(hidden * normal)
        inner = hidden * gain_ref[:, span] * scale
        keep[:, span] = inner
        total = total + jnp.sum(inner, axis=1, keepdims=True)
        cross = cross + jnp.sum(inner * normal, axis=1, keepdims=True)
    out_ref[...] = low(middle_ref[...] + dot(four_ref[...], weight_ref[...]) + bias_ref[...])
    total = total * (1.0 / units)
    cross = cross * (1.0 / units)
    for span in spans:
        up = (keep[:, span] - total - wide(normal_ref[:, span]) * cross) * wide(slope_ref[:, span])
        up = low(up)
        up_ref[:, span] = up
        up_acc[:, span] += fold_rows(wide(up))
    down_acc[...] += fold_rows(wide(grads))

    @pl.when(pl.program_id(0) == pl.num_programs(0) - 1)
    def _():
        sums_ref[...] = jnp.zeros_like(sums_ref)
        row = 0
        for acc in (gain_acc, shift_acc, up_acc, down_acc):
            for start in range(0, acc.shape[1], width):
                sums_ref[row : row + 1, :] = jnp.sum(acc[:, start : start + width], axis=0, keepdims=True)
                row += 1


def drop(spots, middle, four, normal, slope, scale, grads, gain, bias, weight):
    slots, width = middle.shape
    units = four.shape[1]
    rows = 3 * units // width + 1
    return pl.pallas_call(
        functools.partial(drop_kernel, len(weight)),
        grid=(slots // TILE,),
        out_shape=(
            jax.ShapeDtypeStruct((slots, width), jnp.bfloat16),
            jax.ShapeDtypeStruct((slots, units), jnp.bfloat16),
            jax.ShapeDtypeStruct((rows, width), jnp.float32),
        ),
        in_specs=[SCALARS, rows_of(width)]
        + [rows_of(units)] * 3
        + [rows_of(128), rows_of(width), whole((1, units)), whole((1, width))]
        + [ANY] * len(weight),
        out_specs=(rows_of(width), rows_of(units), whole((rows, width))),
        scratch_shapes=[
            pltpu.VMEM((units, width), jnp.bfloat16),
            pltpu.VMEM((TILE, units), jnp.float32),
            pltpu.VMEM((8, units), jnp.float32),
            pltpu.VMEM((8, units), jnp.float32),
            pltpu.VMEM((8, units), jnp.float32),
            pltpu.VMEM((8, width), jnp.float32),
            pltpu.SemaphoreType.DMA((40,)),
        ],
        compiler_params=grant(58),
        cost_estimate=cost(4 * slots * width * units, 40 * slots * width),
        name="drop",
    )(spots, middle, four, normal, slope, scale, grads, gain, bias, *weight)


def settle_kernel(count, rows, spots_ref, up_ref, middle_ref, grad_ref, attended_ref, ffn_gain_ref, mid_gain_ref, core_ref, three_ref, columns_ref, *refs):
    sources = refs[:count]
    (total_ref, branch_ref, back_ref, sums_ref), refs = refs[count : count + 4], refs[count + 4 :]
    outer_refs, (up_weight, out_weight, acc, up_sem, out_sem) = refs[:-5], refs[-5:]

    @pl.when(first())
    def _():
        run_all(
            fetch(spots_ref, sources, out_weight, out_sem)
            + fetch(spots_ref, sources, up_weight, up_sem, out_weight.shape[1])
        )
        acc[...] = jnp.zeros_like(acc)

    three = dot(up_ref[...], up_weight[...], NT)
    outer_kernel(rows, core_ref, three_ref, columns_ref, *outer_refs)
    normal, scale = standardize(middle_ref[...])
    acc[0] += fold_rows(three * normal)
    acc[1] += fold_rows(three)
    total = wide(grad_ref[...]) + standardize_back(three, normal, scale, ffn_gain_ref[...])
    total_ref[...] = total
    branch = low(total)
    branch_ref[...] = branch
    acc[2] += fold_rows(wide(branch))
    two = dot(branch, out_weight[...], NT)
    normal, scale = standardize(attended_ref[...])
    acc[3] += fold_rows(two * normal)
    acc[4] += fold_rows(two)
    back_ref[...] = low(standardize_back(two, normal, scale, mid_gain_ref[...]))

    @pl.when(pl.program_id(0) == pl.num_programs(0) - 1)
    def _():
        sums_ref[...] = jnp.zeros_like(sums_ref)
        for row in range(5):
            sums_ref[row : row + 1, :] = jnp.sum(acc[row], axis=0, keepdims=True)


def settle(spots, core, up, middle, grads, attended, ffn_gain, mid_gain, three, rows, weight):
    slots, width = middle.shape
    units = up.shape[1]
    step = units * TILE // slots
    if rows is None:
        outer_shape = (jax.ShapeDtypeStruct((width, units), jnp.float32),)
        outer_specs = (pl.BlockSpec((width, step), lambda block: (0, block)),)
    else:
        outer_shape = (jax.ShapeDtypeStruct((width // (2 * rows), rows, units), jnp.bfloat16),) * 2
        outer_specs = (pl.BlockSpec((width // (2 * rows), rows, step), lambda block: (0, 0, block)),) * 2
    return pl.pallas_call(
        functools.partial(settle_kernel, len(weight), rows),
        grid=(slots // TILE,),
        out_shape=(
            jax.ShapeDtypeStruct((slots, width), jnp.float32),
            jax.ShapeDtypeStruct((slots, width), jnp.bfloat16),
            jax.ShapeDtypeStruct((slots, width), jnp.bfloat16),
            jax.ShapeDtypeStruct((8, width), jnp.float32),
            *outer_shape,
        ),
        in_specs=[SCALARS, rows_of(units)]
        + [rows_of(width)] * 3
        + [whole((1, width))] * 2
        + [SCALARS, whole((slots, width)), pl.BlockSpec((slots, step), lambda block: (0, block))]
        + [ANY] * len(weight),
        out_specs=(rows_of(width),) * 3 + (whole((8, width)), *outer_specs),
        scratch_shapes=[
            pltpu.VMEM((width, units), jnp.bfloat16),
            pltpu.VMEM((width, width), jnp.bfloat16),
            pltpu.VMEM((5, 8, width), jnp.float32),
            pltpu.SemaphoreType.DMA((40,)),
            pltpu.SemaphoreType.DMA((40,)),
        ],
        compiler_params=grant(58),
        cost_estimate=cost(2 * slots * width * (2 * units + width), 50 * slots * width),
        name="settle",
    )(spots, up, middle, grads, attended, ffn_gain, mid_gain, core, three, up, *weight)


def finish_kernel(count, spots_ref, q_ref, k_ref, v_ref, x_ref, total_ref, gain_ref, *refs):
    sources, (out_ref, sums_ref, weight_ref, acc, sem) = refs[:count], refs[count:]

    @pl.when(first())
    def _():
        run_all(fetch(spots_ref, sources, weight_ref, sem))
        acc[...] = jnp.zeros_like(acc)

    width = x_ref.shape[1]
    one = dot(q_ref[...], weight_ref[:, :width], NT)
    one = one + dot(k_ref[...], weight_ref[:, width : 2 * width], NT)
    one = one + dot(v_ref[...], weight_ref[:, 2 * width :], NT)
    normal, scale = standardize(wide(x_ref[...]))
    acc[0] += fold_rows(one * normal)
    acc[1] += fold_rows(one)
    acc[2] += fold_rows(wide(q_ref[...]))
    acc[3] += fold_rows(wide(v_ref[...]))
    out_ref[...] = total_ref[...] + standardize_back(one, normal, scale, gain_ref[...])

    @pl.when(pl.program_id(0) == pl.num_programs(0) - 1)
    def _():
        sums_ref[...] = jnp.zeros_like(sums_ref)
        for row in range(4):
            sums_ref[row : row + 1, :] = jnp.sum(acc[row], axis=0, keepdims=True)


def finish(spots, grad_q, grad_k, grad_v, tokens, total, gain, weight):
    slots, width = tokens.shape
    return pl.pallas_call(
        functools.partial(finish_kernel, len(weight)),
        grid=(slots // TILE,),
        out_shape=(
            jax.ShapeDtypeStruct((slots, width), jnp.float32),
            jax.ShapeDtypeStruct((8, width), jnp.float32),
        ),
        in_specs=[SCALARS]
        + [rows_of(width)] * 5
        + [whole((1, width))]
        + [ANY] * len(weight),
        out_specs=(rows_of(width), whole((8, width))),
        scratch_shapes=[
            pltpu.VMEM((width, 3 * width), jnp.bfloat16),
            pltpu.VMEM((4, 8, width), jnp.float32),
            pltpu.SemaphoreType.DMA((40,)),
        ],
        compiler_params=grant(58),
        cost_estimate=cost(6 * slots * width * width, 24 * slots * width),
        name="finish",
    )(spots, grad_q, grad_k, grad_v, tokens, total, gain, *weight)


def outer_kernel(rows, core_ref, left_ref, right_ref, *out_refs):
    product = dot(left_ref[...], right_ref[...], TN)
    if rows is None:
        out_refs[0][...] = product.astype(out_refs[0].dtype)
        return
    near = core_ref[0] == 0
    for chip in range(product.shape[0] // (2 * rows)):
        one = low(product[chip * 2 * rows : chip * 2 * rows + rows, :])
        two = low(product[chip * 2 * rows + rows : (chip + 1) * 2 * rows, :])
        out_refs[0][chip] = jnp.where(near, one, two)
        out_refs[1][chip] = jnp.where(near, two, one)


def outer(core, left, right, rows, name, dtype=jnp.float32):
    slots, height = left.shape
    columns = right.shape[1]
    step = min(height, columns)
    tall = height > columns
    left_spec = pl.BlockSpec((slots, step), (lambda block: (0, block)) if tall else (lambda block: (0, 0)))
    right_spec = pl.BlockSpec((slots, step), (lambda block: (0, 0)) if tall else (lambda block: (0, block)))
    if rows is None:
        out_shape = (jax.ShapeDtypeStruct((height, columns), dtype),)
        out_specs = (pl.BlockSpec((step, step), (lambda block: (block, 0)) if tall else (lambda block: (0, block))),)
    else:
        out_shape = (jax.ShapeDtypeStruct((height // (2 * rows), rows, columns), jnp.bfloat16),) * 2
        out_specs = (
            pl.BlockSpec(
                (step // (2 * rows), rows, step),
                (lambda block: (block, 0, 0)) if tall else (lambda block: (0, 0, block)),
            ),
        ) * 2
    return pl.pallas_call(
        functools.partial(outer_kernel, rows),
        grid=(max(height, columns) // step,),
        out_shape=out_shape,
        in_specs=[SCALARS, left_spec, right_spec],
        out_specs=out_specs,
        compiler_params=grant(58),
        cost_estimate=cost(2 * slots * height * columns, 2 * slots * (height + columns) + 4 * height * columns),
        name=name,
    )(core, left, right)


def outer_three_kernel(rows, core_ref, left_ref, q_ref, k_ref, v_ref, *out_refs):
    width = q_ref.shape[1]
    for part, right_ref in enumerate((q_ref, k_ref, v_ref)):
        columns = slice(part * width, (part + 1) * width)
        product = dot(left_ref[...], right_ref[...], TN)
        if rows is None:
            out_refs[0][:, columns] = product
            continue
        near = core_ref[0] == 0
        for chip in range(product.shape[0] // (2 * rows)):
            first_rows = low(product[chip * 2 * rows : chip * 2 * rows + rows, :])
            second_rows = low(product[chip * 2 * rows + rows : (chip + 1) * 2 * rows, :])
            out_refs[0][chip, :, columns] = jnp.where(near, first_rows, second_rows)
            out_refs[1][chip, :, columns] = jnp.where(near, second_rows, first_rows)


def outer_three(core, left, grads, rows):
    slots, width = left.shape
    if rows is None:
        out_shape = (jax.ShapeDtypeStruct((width, 3 * width), jnp.float32),)
    else:
        out_shape = (jax.ShapeDtypeStruct((width // (2 * rows), rows, 3 * width), jnp.bfloat16),) * 2
    return pl.pallas_call(
        functools.partial(outer_three_kernel, rows),
        out_shape=out_shape,
        in_specs=[SCALARS] + [pl.BlockSpec(memory_space=pltpu.VMEM)] * 4,
        out_specs=(pl.BlockSpec(memory_space=pltpu.VMEM),) * len(out_shape),
        compiler_params=grant(24),
        cost_estimate=cost(6 * slots * width * width, 8 * slots * width + 12 * width * width),
        name="outer_three",
    )(core, left, *grads)


def halves(values):
    lane = lax.broadcasted_iota(jnp.int32, values.shape, 1)
    zero = jnp.zeros_like(values)
    return jnp.where(lane < HD, values, zero), jnp.where(lane >= HD, values, zero)


def segment_starts(lengths_ref, position):
    start = jnp.zeros_like(position)
    end = jnp.int32(0)
    for index in range(lengths_ref.shape[1] - 1):
        end = end + lengths_ref[0, index]
        start = jnp.where(position >= end, end, start)
    return start


def fill_bias(tile, slots, lengths_ref, bias_ref):
    for block in range(slots // tile):
        reach = (block + 1) * tile
        spot = block * (block + 1) // 2 * tile
        query = lax.broadcasted_iota(jnp.int32, (reach, tile), 1) + block * tile
        key = lax.broadcasted_iota(jnp.int32, (reach, tile), 0)
        start = segment_starts(lengths_ref, lax.broadcasted_iota(jnp.int32, (1, tile), 1) + block * tile)
        bias_ref[spot : spot + reach, :] = jnp.where((key <= query) & (key >= start), 0.0, NEGATIVE)


def attend_kernel(tile, lengths_ref, q_ref, k_ref, v_ref, out_ref, total_ref, bias_ref):
    slots = q_ref.shape[0]

    @pl.when(pl.program_id(0) == 0)
    def _():
        fill_bias(tile, slots, lengths_ref, bias_ref)

    values = halves(v_ref[...])
    steps = [(block, head) for block in range(slots // tile) for head in range(2)]

    def score(block, head):
        reach = (block + 1) * tile
        spot = block * (block + 1) // 2 * tile
        query = halves(q_ref[block * tile : reach, :] * jnp.bfloat16(1.0 / math.sqrt(HD)))[head]
        return dot(k_ref[:reach, :], query, NT) + bias_ref[spot : spot + reach, :]

    ahead = score(*steps[0])
    for number, (block, head) in enumerate(steps):
        reach = (block + 1) * tile
        rows = slice(block * tile, reach)
        scores = ahead
        if number + 1 < len(steps):
            ahead = score(*steps[number + 1])
        top = jnp.max(scores, axis=0, keepdims=True)
        fresh = jnp.exp(scores - top)
        mass = jnp.sum(fresh, axis=0, keepdims=True)
        part = dot(values[head][:reach, :], fresh.astype(jnp.bfloat16), TN) * (1.0 / mass)
        mixed = part if head == 0 else mixed + part
        total_ref[0, head : head + 1, rows] = top + jnp.log(mass)
        if head:
            out_ref[rows, :] = mixed.T


def attend_forward(lengths, projected, begin, pairs, tile=256):
    slots, every = projected.shape[0], projected.shape[1] // (6 * HD)
    blocks = slots // tile
    column = lambda offset: pl.BlockSpec((slots, 2 * HD), lambda pair: (0, offset + pair))
    return pl.pallas_call(
        functools.partial(attend_kernel, tile),
        grid=(pairs,),
        out_shape=(
            jax.ShapeDtypeStruct((slots, 2 * HD * pairs), jnp.float32),
            jax.ShapeDtypeStruct((pairs, 8, slots), jnp.float32),
        ),
        in_specs=[pl.BlockSpec(memory_space=pltpu.SMEM), *[column(begin + part * every) for part in range(3)]],
        out_specs=(column(0), pl.BlockSpec((1, 8, slots), lambda pair: (pair, 0, 0))),
        scratch_shapes=[pltpu.VMEM((tile * blocks * (blocks + 1) // 2, tile), jnp.float32)],
        compiler_params=grant(24),
        cost_estimate=cost(20 * 10**9, 8 * 10**6),
        name="attend_forward",
    )(lengths, projected, projected, projected)


def attend_back_kernel(tile, lengths_ref, q_ref, k_ref, v_ref, g_ref, out_ref, total_ref, gq_ref, gk_ref, gv_ref, bias_ref, gk_acc, gv_acc):
    slots = q_ref.shape[0]

    @pl.when(pl.program_id(0) == 0)
    def _():
        fill_bias(tile, slots, lengths_ref, bias_ref)

    weighed = (g_ref[...].astype(jnp.float32) * out_ref[...]).T
    deltas = [
        jnp.sum(weighed[:HD, :], axis=0, keepdims=True),
        jnp.sum(weighed[HD:, :], axis=0, keepdims=True),
    ]
    keys = halves(k_ref[...])
    steps = [(block, head) for block in reversed(range(slots // tile)) for head in range(2)]

    def begin(block, head):
        reach = (block + 1) * tile
        spot = block * (block + 1) // 2 * tile
        rows = slice(block * tile, reach)
        query = halves(q_ref[rows, :] * jnp.bfloat16(1.0 / math.sqrt(HD)))[head]
        grad = halves(g_ref[rows, :])[head]
        scores = dot(k_ref[:reach, :], query, NT) + bias_ref[spot : spot + reach, :]
        return query, grad, scores, dot(v_ref[:reach, :], grad, NT)

    ahead = begin(*steps[0])
    for number, (block, head) in enumerate(steps):
        reach = (block + 1) * tile
        rows = slice(block * tile, reach)
        query, grad, scores, grad_soft = ahead
        if number + 1 < len(steps):
            ahead = begin(*steps[number + 1])
        soft = jnp.exp(scores - total_ref[0, head : head + 1, rows])
        grad_scores = (soft * (grad_soft - deltas[head][:, rows])).astype(jnp.bfloat16)
        gv = dot(soft.astype(jnp.bfloat16), grad)
        gk = dot(grad_scores, query)
        if number == 0:
            gk_acc[...] = gk
            gv_acc[...] = gv
        else:
            gk_acc[:reach, :] += gk
            gv_acc[:reach, :] += gv
        part = dot(keys[head][:reach, :], grad_scores, TN)
        gq = part if head == 0 else gq + part
        if head:
            gq_ref[rows, :] = (gq.T * (1.0 / math.sqrt(HD))).astype(jnp.bfloat16)
    gk_ref[...] = gk_acc[...].astype(jnp.bfloat16)
    gv_ref[...] = gv_acc[...].astype(jnp.bfloat16)


def attend_backward(lengths, projected, grad_out, attended, totals, begin, tile=256):
    slots, width = attended.shape
    pairs, every = width // (2 * HD), projected.shape[1] // (6 * HD)
    blocks = slots // tile
    column = lambda offset: pl.BlockSpec((slots, 2 * HD), lambda pair: (0, offset + pair))
    return pl.pallas_call(
        functools.partial(attend_back_kernel, tile),
        grid=(pairs,),
        out_shape=(jax.ShapeDtypeStruct((slots, width), jnp.bfloat16),) * 3,
        in_specs=[
            pl.BlockSpec(memory_space=pltpu.SMEM),
            *[column(begin + part * every) for part in range(3)],
            column(begin),
            column(0),
            pl.BlockSpec((1, 8, slots), lambda pair: (pair, 0, 0)),
        ],
        out_specs=(column(0),) * 3,
        scratch_shapes=[
            pltpu.VMEM((tile * blocks * (blocks + 1) // 2, tile), jnp.float32),
            pltpu.VMEM((slots, 2 * HD), jnp.float32),
            pltpu.VMEM((slots, 2 * HD), jnp.float32),
        ],
        compiler_params=grant(28),
        cost_estimate=cost(28 * 10**9, 12 * 10**6),
        name="attend_backward",
    )(lengths, projected, projected, projected, grad_out, attended, totals)


AXES = ("dp", "fsdp")


def place():
    outer_index, inner_index = lax.axis_index("dp"), lax.axis_index("fsdp")
    return outer_index // 2, outer_index % 2, inner_index // 2, inner_index % 2


def send(values, dz=0, dx=0, dy=0, dc=0):
    pairs = []
    for z in range(4):
        for x in range(2):
            for y in range(2):
                for c in range(2):
                    here = ((z * 2 + x) * 2 + y) * 2 + c
                    there = ((((z + dz) % 4) * 2 + (x ^ dx)) * 2 + (y ^ dy)) * 2 + (c ^ dc)
                    pairs.append((here, there))
    return lax.ppermute(values, AXES, pairs)


def index_of(z, x, y, c):
    return ((z * 2 + x) * 2 + y) * 2 + c


CHIPS = [[index_of(z, x, y, c) for z in range(4) for x in range(2) for y in range(2)] for c in range(2)]
COLUMNS_Z = [[index_of(z, x, y, c) for z in range(4)] for x in range(2) for y in range(2) for c in range(2)]


def part_spots():
    z, x, y, c = place()
    spots = []
    for part in range(8):
        dx, dy, dc = part >> 2 & 1, part >> 1 & 1, part & 1
        for step in range(4):
            spots.append(((((z - step) % 4) * 2 + (x ^ dx)) * 2 + (y ^ dy)) * 2 + (c ^ dc))
    return jnp.stack(spots).astype(jnp.int32)


def after(value, *others):
    return lax.optimization_barrier((value, *others))[0]


def send_z(shard):
    return [shard] + [send(shard, dz=step) for step in (1, 2, 3)]


def gather_z(shards, *gate):
    return jnp.stack(after(shards, *gate))


def gather_near(own):
    return own, send(own, dy=1), send(own, dx=1), send(own, dx=1, dy=1)


def gather_core(parts):
    both = []
    for part in parts:
        both += [part, send(part, dc=1)]
    return both


def chips_kernel(way, place_ref, *refs):
    x, y = place_ref[1], place_ref[2]
    count = 4 if way == "both" else 2
    sources, out_refs = refs[:-count], refs[-count:]
    start = 0
    for kept_ref, got_ref in zip(sources[::2], sources[1::2]):
        columns = slice(start, start + kept_ref.shape[2])
        start = columns.stop
        total = lambda z, x, y: low(wide(kept_ref[(z * 2 + x) * 2 + y]) + wide(got_ref[(z * 2 + x) * 2 + y]))
        for z in range(4):
            for flip, out_ref in enumerate(out_refs):
                if way == "x":
                    for other in range(2):
                        out_ref[z * 2 + other, :, columns] = total(z, x ^ flip, other)
                elif way == "y":
                    for other in range(2):
                        out_ref[z * 2 + other, :, columns] = total(z, other, y ^ flip)
                else:
                    out_ref[z, :, columns] = total(z, x ^ (flip >> 1), y ^ (flip & 1))


def planes_kernel(count, place_ref, *refs):
    sources, mine_ref, out_refs = refs[:count], refs[count], refs[count + 1 :]
    for step in range(4):
        z = (place_ref[0] + step) & 3
        total = wide(sources[0][z])
        for source in sources[1:]:
            total = total + wide(source[z])
        if step == 0:
            mine_ref[...] = total
        else:
            out_refs[step - 1][...] = low(total)


def plane_kernel(count, place_ref, *refs):
    sources, out_ref = refs[:count], refs[count]
    for z in range(4):
        total = wide(sources[0][z])
        for source in sources[1:]:
            total = total + wide(source[z])
        out_ref[z] = low(total)


def small_call(kernel, spot, arrays, out_shapes, name):
    vmem = pl.BlockSpec(memory_space=pltpu.VMEM)
    moved = sum(math.prod(a.shape) * a.dtype.itemsize for a in (*arrays, *out_shapes))
    return pl.pallas_call(
        kernel,
        out_shape=tuple(out_shapes),
        in_specs=[SCALARS] + [vmem] * len(arrays),
        out_specs=(vmem,) * len(out_shapes),
        compiler_params=grant(20),
        cost_estimate=cost(0, moved),
        name=name,
    )(spot, *arrays)


class Sum:
    def __init__(self, spot, kept, given, way, name):
        self.spot, self.way, self.name = spot, way, name
        self.rows, self.columns = kept.shape[1], 0
        self.arrays = []
        self.add(kept, given)

    def add(self, kept, given):
        self.kept = kept
        self.columns += kept.shape[2]
        self.arrays += [kept, send(given, dc=1)]

    def shapes(self, blocks, count):
        return [jax.ShapeDtypeStruct((blocks, self.rows, self.columns), jnp.bfloat16)] * count

    def chips(self, *gate):
        kernel = functools.partial(chips_kernel, self.way)
        out = self.shapes(4, 4) if self.way == "both" else self.shapes(8, 2)
        out = small_call(kernel, self.spot, (after(self.arrays[0], *gate), *self.arrays[1:]), out, "chips_" + self.name)
        if self.way == "both":
            own, to_y, to_x, to_xy = out
            self.parts = [own, send(to_y, dy=1), send(to_x, dx=1), send(to_xy, dx=1, dy=1)]
        else:
            self.pair = out[0], send(out[1], dx=int(self.way == "x"), dy=int(self.way == "y"))
        return out[0]

    def planes(self, *gate):
        self.parts[0] = after(self.parts[0], *gate)
        shape = (self.rows, self.columns)
        out = [jax.ShapeDtypeStruct(shape, jnp.float32)] + [jax.ShapeDtypeStruct(shape, jnp.bfloat16)] * 3
        kernel = functools.partial(planes_kernel, len(self.parts))
        mine, *others = small_call(kernel, self.spot, self.parts, out, "planes_" + self.name)
        self.others = [send(other, dz=step + 1) for step, other in enumerate(others)]
        self.mine = mine
        return mine

    def done(self):
        return self.mine + sum(wide(other) for other in self.others)

    def plane(self, *gate):
        self.parts[0] = after(self.parts[0], *gate)
        kernel = functools.partial(plane_kernel, len(self.parts))
        (total,) = small_call(kernel, self.spot, self.parts, self.shapes(4, 1), "plane_" + self.name)
        parts = lax.all_to_all(total, AXES, 0, 0, tiled=True, axis_index_groups=COLUMNS_Z)
        return total, jnp.sum(wide(parts), axis=0)


WIDE = ("mid_gain", "mid_bias", "out_bias", "ffn_gain", "ffn_bias", "down_bias", "in_gain", "in_bias")
DEEP = ("up_bias", "hid_gain", "hid_bias")


def spread_row(packed, width, count):
    lane = lax.broadcasted_iota(jnp.int32, (1, count), 1)
    owner = jnp.zeros_like(lane)
    for device in range(1, 32):
        owner = owner + (lane >= device * width).astype(jnp.int32)
    inside = lane - owner * width
    pick = lax.broadcasted_iota(jnp.int32, (128, count), 0) == inside
    everyone = dot(packed, low(jnp.where(pick, 1.0, 0.0)))
    owned = lax.broadcasted_iota(jnp.int32, (32, count), 0) == owner
    return jnp.sum(jnp.where(owned, everyone, 0.0), axis=0, keepdims=True)


def vectors_kernel(spots_ref, *refs):
    sources, (wide_ref, qkv_ref, deep_ref, weight_ref, landed, everything, sem, weight_sem) = refs[:8], refs[8:]
    lanes = landed.shape[3]
    copies = [
        pltpu.make_async_copy(
            source.at[:, :, pl.ds(source.shape[2] - lanes, lanes)], landed.at[part], sem.at[part]
        )
        for part, source in enumerate(sources)
    ]
    laid = [
        pltpu.make_async_copy(
            source.at[step, :, pl.ds(0, weight_ref.shape[2])],
            weight_ref.at[spots_ref[part * 4 + step]],
            weight_sem.at[part * 4 + step],
        )
        for part, source in enumerate(sources)
        for step in range(4)
    ]
    for copy in laid:
        copy.start()
    run_all(copies)
    for part in range(8):
        for step in range(4):
            everything[spots_ref[part * 4 + step]] = wide(landed[part, step])
    row = lambda number: low(everything[:, number, :])
    width = wide_ref.shape[1]
    for number in range(8):
        wide_ref[number : number + 1, :] = spread_row(row(number), width // 32, width)
    both = spread_row(row(8), width // 16, 2 * width)
    qkv_ref[:, :width] = both[:, :width]
    qkv_ref[:, width : 2 * width] = jnp.zeros((1, width), jnp.float32)
    qkv_ref[:, 2 * width :] = both[:, width:]
    units = deep_ref.shape[2]
    for number in range(3):
        deep_ref[number] = spread_row(row(9 + number), units // 32, units)
    for copy in laid:
        copy.wait()


def pack_vectors(shards, rows):
    listed = [shards[name] for name in WIDE + ("qv_bias",) + DEEP]
    packed = jnp.stack([jnp.pad(entry, (0, 128 - entry.shape[0])) for entry in listed])
    return jnp.pad(packed, ((0, rows - packed.shape[0]), (0, 0)))


def unpack_first(spots, parts, width, units):
    vmem = pl.BlockSpec(memory_space=pltpu.VMEM)
    rows = parts[0].shape[1]
    *vectors, weight = pl.pallas_call(
        vectors_kernel,
        out_shape=(
            jax.ShapeDtypeStruct((8, width), jnp.float32),
            jax.ShapeDtypeStruct((1, 3 * width), jnp.float32),
            jax.ShapeDtypeStruct((3, 1, units), jnp.float32),
            jax.ShapeDtypeStruct((32, rows, 3 * width), jnp.bfloat16),
        ),
        in_specs=[SCALARS] + [ANY] * 8,
        out_specs=(vmem,) * 4,
        scratch_shapes=[
            pltpu.VMEM((8, 4, rows, 128), jnp.bfloat16),
            pltpu.VMEM((32, rows, 128), jnp.float32),
            pltpu.SemaphoreType.DMA((8,)),
            pltpu.SemaphoreType.DMA((32,)),
        ],
        compiler_params=grant(16),
        cost_estimate=cost(10**8, 10**7),
        name="unpack",
    )(spots, *parts)
    return vectors, weight.reshape(32 * rows, 3 * width)


def sum_rows_core(rows):
    return rows + send(rows, dc=1)


def sum_rows_near(rows):
    return rows + send(rows, dy=1) + (send(rows, dx=1) + send(rows, dx=1, dy=1))


def sum_rows_z(rows):
    return rows + send(rows, dz=1) + (send(rows, dz=2) + send(rows, dz=3))


def owners_kernel(core_ref, deep_ref, mid_ref, end_ref, *out_refs):
    near = core_ref[0] == 0
    width = mid_ref.shape[1]
    per = (deep_ref.shape[0] - 1) // 3
    row = lambda ref, number: ref[number : number + 1, :]
    narrow = [row(deep_ref, 3 * per)] + [row(mid_ref, number) for number in range(5)] + [row(end_ref, number) for number in range(2)]
    broad = [
        jnp.concatenate([row(deep_ref, number * per + part) for part in range(per)], axis=1) for number in range(3)
    ]
    pair = [jnp.concatenate([row(end_ref, 2), row(end_ref, 3)], axis=1)]
    start = 0
    for group in (narrow, broad, pair):
        group = group + [jnp.zeros_like(group[0])] * (8 - len(group))
        stacked = jnp.concatenate(group, axis=0)
        share = stacked.shape[1] // 32
        stacked = jnp.concatenate([stacked, jnp.zeros((8, 128), jnp.float32)], axis=1)
        blocks = [stacked[:, owner * share : owner * share + 128] for owner in range(32)]
        for chip in range(16):
            one, two = blocks[2 * chip], blocks[2 * chip + 1]
            out_refs[0][chip, start : start + 8, :] = jnp.where(near, one, two)
            out_refs[1][chip, start : start + 8, :] = jnp.where(near, two, one)
        start += 8


SUMMED = {
    "down_bias": 0,
    "ffn_gain": 1,
    "ffn_bias": 2,
    "out_bias": 3,
    "mid_gain": 4,
    "mid_bias": 5,
    "in_gain": 6,
    "in_bias": 7,
    "hid_gain": 8,
    "hid_bias": 9,
    "up_bias": 10,
    "qv_bias": 16,
}


def lay_vectors(core, deep, mid, end):
    vmem = pl.BlockSpec(memory_space=pltpu.VMEM)
    return pl.pallas_call(
        owners_kernel,
        out_shape=(jax.ShapeDtypeStruct((16, 24, 128), jnp.float32),) * 2,
        in_specs=[SCALARS] + [vmem] * 3,
        out_specs=(vmem,) * 2,
        compiler_params=grant(8),
        cost_estimate=cost(0, 10**6),
        name="owners",
    )(core, deep, mid, end)


def sum_vectors(kept, got):
    parts = lax.all_to_all(kept + got, AXES, 0, 0, tiled=True, axis_index_groups=CHIPS)
    return jnp.sum(parts, axis=0)


WEIGHTS = ("qkv_weight", "out_weight", "up_weight", "down_weight")
PARAMS = (
    "in_gain",
    "in_bias",
    "qkv_weight",
    "qv_bias",
    "mid_gain",
    "mid_bias",
    "out_weight",
    "out_bias",
    "ffn_gain",
    "ffn_bias",
    "up_weight",
    "up_bias",
    "hid_gain",
    "hid_bias",
    "down_weight",
    "down_bias",
)


def forward_staged(spots, tokens, lengths, shards):
    width = tokens.shape[1]
    units = 32 * shards["up_bias"].shape[0]
    rows = shards["qkv_weight"].shape[0]
    whole_piece = lambda shard: [lax.all_gather(shard, AXES, axis=0, tiled=True)]
    second_piece = whole_piece(jnp.concatenate([shards["out_weight"], shards["up_weight"]], axis=1))
    own = gather_z(send_z(shards["qkv_weight"]))
    own_vectors = gather_z(send_z(pack_vectors(shards, rows)))
    near_first = gather_near(jnp.concatenate([own, own_vectors], axis=2))
    vectors, weight = unpack_first(spots, gather_core(near_first), width, units)
    third_piece = send_z(after(shards["down_weight"], near_first))
    return ([weight], second_piece, third_piece), vectors


def forward_plain(spots, tokens, lengths, shards):
    width = tokens.shape[1]
    full = {name: lax.all_gather(shards[name], AXES, axis=0, tiled=True) for name in PARAMS}
    pieces = (
        [full["qkv_weight"]],
        [jnp.concatenate([full["out_weight"], full["up_weight"]], axis=1)],
        [full["down_weight"]],
    )
    full = {name: wide(full[name]) for name in PARAMS if name not in WEIGHTS}
    rows = jnp.stack([full[name] for name in WIDE])
    bias = full["qv_bias"]
    qkv_bias = jnp.concatenate([bias[:width], jnp.zeros((width,), jnp.float32), bias[width:]])[None]
    return pieces, (rows, qkv_bias, jnp.stack([full[name][None] for name in DEEP]))


def body(staged, tokens, lengths, cotangent, *params):
    shards = dict(zip(PARAMS, params))
    width = tokens.shape[1]
    pairs = width // (2 * HD)
    if staged:
        spot = jnp.stack(place()).astype(jnp.int32)
        core, spots = spot[3:4], part_spots()
    else:
        spots = core = jnp.zeros((1,), jnp.int32)
    run = forward_staged if staged else forward_plain
    pieces, (rows, qkv_bias, deep) = run(spots, tokens, lengths, shards)
    owned = {name: shards[name].shape[0] if staged else None for name in WEIGHTS}

    one, projected = project(spots, tokens, rows, qkv_bias, pieces[0])
    attended, totals = attend_forward(lengths, projected, 0, pairs)
    third_piece = pieces[2]
    if staged:
        third_piece = gather_z(third_piece, attended)
        near_third = gather_near(third_piece)
        attended = after(attended, third_piece)
    two, middle, three, four, normal, slope, scale = lift(
        spots, attended, tokens, rows, deep[0], deep[1], deep[2], pieces[1]
    )
    if staged:
        third_piece = gather_core(after(near_third, four))
        four = after(four, near_third)
    (down,) = outer(core, four, cotangent, None, "outer_down", jnp.bfloat16)
    if staged:
        middle = after(middle, down)
    out_tokens, up, deep_sums = drop(
        spots, middle, four, normal, slope, scale, cotangent, deep[1], rows[5:6], third_piece
    )
    total, branch, back, mid_sums, *up_sum = settle(
        spots, core, up, middle, cotangent, attended, rows[3:4], rows[0:1], three, owned["up_weight"], pieces[1]
    )
    if staged:
        up_sum = Sum(spot, *up_sum, "both", "up")
        two = after(two, up_sum.kept)
    out_sum = outer(core, two, branch, owned["out_weight"], "outer_out")
    if staged:
        up_sum.add(*out_sum)
        back = after(back, up_sum.chips(back))
    grads = attend_backward(lengths, projected, back, attended, totals, 0)
    qkv_sum = outer_three(core, one, grads, owned["qkv_weight"])
    if staged:
        kept, given = qkv_sum
        flag, up_total = up_sum.plane(kept)
        qkv_sum = Sum(spot, kept, after(given, flag), "both", "qkv")
        total = after(total, qkv_sum.chips())
    grad_tokens, end_sums = finish(spots, *grads, tokens, total, rows[6:7], pieces[0])
    down = lax.psum_scatter(down, AXES, scatter_dimension=0, tiled=True)
    summed = {"down_weight": wide(down)}
    if staged:
        units = 32 * shards["up_bias"].shape[0]
        kept, given = lay_vectors(core, deep_sums, mid_sums, end_sums)
        got = send(given, dc=1)
        flag = qkv_sum.planes(kept, up_total, down)
        summed["qkv_weight"] = qkv_sum.done()
        block = sum_vectors(kept, after(got, flag))
        summed["up_weight"], summed["out_weight"] = jnp.split(up_total, (units,), axis=1)
        summed.update({name: block[row, : shards[name].shape[0]] for name, row in SUMMED.items()})
    else:
        deep_rows = 3 * deep.shape[2] // width
        flat = deep_sums[:deep_rows].reshape(3, -1)
        vectors = dict(zip(("hid_gain", "hid_bias", "up_bias"), flat))
        vectors["down_bias"] = deep_sums[deep_rows]
        vectors.update(zip(("ffn_gain", "ffn_bias", "out_bias", "mid_gain", "mid_bias"), mid_sums))
        vectors.update(in_gain=end_sums[0], in_bias=end_sums[1], qv_bias=end_sums[2:4].reshape(-1))
        vectors.update(up_weight=up_sum[0], out_weight=out_sum[0], qkv_weight=qkv_sum[0])
        for name, vector in vectors.items():
            summed[name] = lax.psum_scatter(vector, AXES, scatter_dimension=0, tiled=True)
    return (out_tokens, grad_tokens) + tuple(summed[name] for name in PARAMS)


def solution(mesh):
    staged = (mesh.shape["dp"], mesh.shape["fsdp"]) == (8, 4)
    matrix, vector = P(AXES, None), P(AXES)
    placed = tuple(matrix if name in WEIGHTS else vector for name in PARAMS)
    return jax.shard_map(
        functools.partial(body, staged),
        mesh=mesh,
        in_specs=(matrix,) * 3 + placed,
        out_specs=(matrix,) * 2 + placed,
        check_vma=False,
    )
```

```python
import functools
import math

import jax
import jax.numpy as jnp
from jax import lax
from jax.experimental import pallas as pl
from jax.experimental.pallas import tpu as pltpu
from jax.sharding import PartitionSpec as P

HD = 64
EPSILON = 1e-05
NEGATIVE = -1e30
TILE = 256
CHUNK = 512
NT = (((1,), (1,)), ((), ()))
TN = (((0,), (0,)), ((), ()))
NN = (((1,), (0,)), ((), ()))
ANY = pl.BlockSpec(memory_space=pl.ANY)
SCALARS = pl.BlockSpec(memory_space=pltpu.SMEM)
def grant(size):
    return pltpu.CompilerParams(vmem_limit_bytes=size << 20)


def dot(left, right, dims=NN):
    return lax.dot_general(left, right, dims, preferred_element_type=jnp.float32)


def wide(values):
    return values.astype(jnp.float32)


def low(values):
    return values.astype(jnp.bfloat16)


def cost(flops, size):
    return pl.CostEstimate(flops=int(0.4 * flops), transcendentals=0, bytes_accessed=int(0.4 * size))


def standardize(values):
    center = values - jnp.mean(values, axis=1, keepdims=True)
    scale = lax.rsqrt(jnp.mean(center * center, axis=1, keepdims=True) + EPSILON)
    return center * scale, scale


def standardize_back(grads, normal, scale, gain):
    inner = grads * gain
    return (
        inner
        - jnp.mean(inner, axis=1, keepdims=True)
        - normal * jnp.mean(inner * normal, axis=1, keepdims=True)
    ) * scale


def fold_rows(values):
    return jnp.sum(values.reshape(-1, 8, values.shape[1]), axis=0)


def fetch(spots_ref, sources, target, sem, start=0):
    stop = start + target.shape[1]
    if len(sources) == 1:
        return [pltpu.make_async_copy(sources[0].at[:, pl.ds(start, stop - start)], target, sem.at[0])]
    rows = sources[0].shape[1]
    left = sources[6].shape[2] if len(sources) > 8 else 0
    copies = []
    for part, source in enumerate(sources):
        begin = left if part >= 8 else 0
        low_end, high_end = max(start, begin), min(stop, begin + source.shape[2])
        if low_end >= high_end:
            continue
        for step in range(4):
            spot = pl.multiple_of(spots_ref[(part - 2 if part >= 8 else part) * 4 + step] * rows, math.gcd(rows, 128))
            copies.append(
                pltpu.make_async_copy(
                    source.at[step, :, pl.ds(low_end - begin, high_end - low_end)],
                    target.at[pl.ds(spot, rows), pl.ds(low_end - start, high_end - low_end)],
                    sem.at[len(copies)],
                )
            )
    return copies


def run_all(copies):
    for copy in copies:
        copy.start()
    for copy in copies:
        copy.wait()


def first():
    return pl.program_id(0) == 0


def rows_of(columns):
    return pl.BlockSpec((TILE, columns), lambda block: (block, 0))


def whole(shape):
    return pl.BlockSpec(shape, lambda block: (0,) * len(shape))


def project_kernel(count, spots_ref, x_ref, vectors_ref, bias_ref, *refs):
    sources, (hidden_ref, out_ref, weight_ref, sem) = refs[:count], refs[count:]

    @pl.when(first())
    def _():
        run_all(fetch(spots_ref, sources, weight_ref, sem))

    normal, _ = standardize(wide(x_ref[...]))
    hidden = low(normal * vectors_ref[6:7, :] + vectors_ref[7:8, :])
    hidden_ref[...] = hidden
    width = hidden.shape[1]
    for part in range(3):
        columns = slice(part * width, (part + 1) * width)
        out_ref[:, columns] = low(dot(hidden, weight_ref[:, columns]) + bias_ref[:, columns])


def project(spots, tokens, vectors, bias, weight):
    slots, width = tokens.shape
    return pl.pallas_call(
        functools.partial(project_kernel, len(weight)),
        grid=(slots // TILE,),
        out_shape=(
            jax.ShapeDtypeStruct((slots, width), jnp.bfloat16),
            jax.ShapeDtypeStruct((slots, 3 * width), jnp.bfloat16),
        ),
        in_specs=[SCALARS, rows_of(width), whole(vectors.shape), whole((1, 3 * width))]
        + [ANY] * len(weight),
        out_specs=(rows_of(width), rows_of(3 * width)),
        scratch_shapes=[pltpu.VMEM((width, 3 * width), jnp.bfloat16), pltpu.SemaphoreType.DMA((40,))],
        compiler_params=grant(20),
        cost_estimate=cost(6 * slots * width * width, 20 * slots * width),
        name="project",
    )(spots, tokens, vectors, bias, *weight)


def bell(values):
    square = jnp.exp(values * values * -0.5)
    step = 1.0 / (1.0 + jnp.abs(values) * (0.3275911 * math.sqrt(0.5)))
    series = step * (
        0.5 * 0.254829592
        + step
        * (
            0.5 * -0.284496736
            + step * (0.5 * 1.421413741 + step * (0.5 * -1.453152027 + step * (0.5 * 1.061405429)))
        )
    )
    tail = series * square
    below = jnp.where(values > 0, 1.0 - tail, tail)
    return values * below, below + values * square * (1.0 / math.sqrt(2.0 * math.pi))


def lift_kernel(count, spots_ref, attended_ref, x_ref, vectors_ref, up_bias_ref, gain_ref, shift_ref, *refs):
    sources = refs[:count]
    (two_ref, middle_ref, three_ref, four_ref, normal_ref, slope_ref, scale_ref, out_ref, up_ref, active, out_sem, up_sem) = refs[count:]

    copies = fetch(spots_ref, sources, out_ref, out_sem) + fetch(spots_ref, sources, up_ref, up_sem, out_ref.shape[1])

    @pl.when(first())
    def _():
        for copy in copies:
            copy.start()
        copies[0].wait()

    mid_gain, mid_bias, out_bias, ffn_gain, ffn_bias = [vectors_ref[row : row + 1, :] for row in range(5)]
    normal, _ = standardize(attended_ref[...])
    two = low(normal * mid_gain + mid_bias)
    two_ref[...] = two
    middle = wide(x_ref[...]) + dot(two, out_ref[...]) + out_bias
    middle_ref[...] = middle
    normal, _ = standardize(middle)
    three = low(normal * ffn_gain + ffn_bias)
    three_ref[...] = three

    @pl.when(first())
    def _():
        copies[1].wait()

    units = up_ref.shape[1]
    spans = [slice(start, start + CHUNK) for start in range(0, units, CHUNK)]
    raise_up = lambda span: dot(three, up_ref[:, span]) + up_bias_ref[:, span]
    ahead = raise_up(spans[0])
    total = jnp.zeros((TILE, 1), jnp.float32)
    slopes = []
    for number, span in enumerate(spans):
        upward = ahead
        if number + 1 < len(spans):
            ahead = raise_up(spans[number + 1])
        value, slope = bell(upward)
        active[:, span] = value
        slope_ref[:, span] = low(slope)
        total = total + jnp.sum(value, axis=1, keepdims=True)
    mean = total * (1.0 / units)
    spread = jnp.zeros((TILE, 1), jnp.float32)
    for span in spans:
        center = active[:, span] - mean
        spread = spread + jnp.sum(center * center, axis=1, keepdims=True)
    scale = lax.rsqrt(spread * (1.0 / units) + EPSILON)
    scale_ref[...] = jnp.broadcast_to(scale, scale_ref.shape)
    for span in spans:
        normal = (active[:, span] - mean) * scale
        normal_ref[:, span] = low(normal)
        four_ref[:, span] = low(normal * gain_ref[:, span] + shift_ref[:, span])


def lift(spots, attended, tokens, vectors, up_bias, gain, shift, weight):
    slots, width = tokens.shape
    units = up_bias.shape[1]
    shape = jax.ShapeDtypeStruct
    return pl.pallas_call(
        functools.partial(lift_kernel, len(weight)),
        grid=(slots // TILE,),
        out_shape=(
            shape((slots, width), jnp.bfloat16),
            shape((slots, width), jnp.float32),
            shape((slots, width), jnp.bfloat16),
            shape((slots, units), jnp.bfloat16),
            shape((slots, units), jnp.bfloat16),
            shape((slots, units), jnp.bfloat16),
            shape((slots, 128), jnp.float32),
        ),
        in_specs=[SCALARS, rows_of(width), rows_of(width), whole(vectors.shape)]
        + [whole((1, units))] * 3
        + [ANY] * len(weight),
        out_specs=(rows_of(width),) * 3 + (rows_of(units),) * 3 + (rows_of(128),),
        scratch_shapes=[
            pltpu.VMEM((width, width), jnp.bfloat16),
            pltpu.VMEM((width, units), jnp.bfloat16),
            pltpu.VMEM((TILE, units), jnp.float32),
            pltpu.SemaphoreType.DMA((40,)),
            pltpu.SemaphoreType.DMA((40,)),
        ],
        compiler_params=grant(58),
        cost_estimate=cost(2 * slots * width * (width + units), 40 * slots * width),
        name="lift",
    )(spots, attended, tokens, vectors, up_bias, gain, shift, *weight)


def drop_kernel(count, spots_ref, middle_ref, four_ref, normal_ref, slope_ref, scale_ref, grad_ref, gain_ref, bias_ref, *refs):
    sources = refs[:count]
    out_ref, up_ref, sums_ref, weight_ref, keep, gain_acc, shift_acc, up_acc, down_acc, sem = refs[count:]

    @pl.when(first())
    def _():
        run_all(fetch(spots_ref, sources, weight_ref, sem))
        for acc in (gain_acc, shift_acc, up_acc, down_acc):
            acc[...] = jnp.zeros_like(acc)

    units = four_ref.shape[1]
    width = middle_ref.shape[1]
    grads = grad_ref[...]
    spans = [slice(start, start + CHUNK) for start in range(0, units, CHUNK)]
    back = lambda span: dot(grads, weight_ref[span, :], NT)
    scale = scale_ref[:, :1]
    ahead = back(spans[0])
    total = jnp.zeros((TILE, 1), jnp.float32)
    cross = jnp.zeros((TILE, 1), jnp.float32)
    for number, span in enumerate(spans):
        hidden = ahead
        if number + 1 < len(spans):
            ahead = back(spans[number + 1])
        normal = wide(normal_ref[:, span])
        shift_acc[:, span] += fold_rows(hidden)
        gain_acc[:, span] += fold_rows(hidden * normal)
        inner = hidden * gain_ref[:, span] * scale
        keep[:, span] = inner
        total = total + jnp.sum(inner, axis=1, keepdims=True)
        cross = cross + jnp.sum(inner * normal, axis=1, keepdims=True)
    out_ref[...] = low(middle_ref[...] + dot(four_ref[...], weight_ref[...]) + bias_ref[...])
    total = total * (1.0 / units)
    cross = cross * (1.0 / units)
    for span in spans:
        up = (keep[:, span] - total - wide(normal_ref[:, span]) * cross) * wide(slope_ref[:, span])
        up = low(up)
        up_ref[:, span] = up
        up_acc[:, span] += fold_rows(wide(up))
    down_acc[...] += fold_rows(wide(grads))

    @pl.when(pl.program_id(0) == pl.num_programs(0) - 1)
    def _():
        sums_ref[...] = jnp.zeros_like(sums_ref)
        row = 0
        for acc in (gain_acc, shift_acc, up_acc, down_acc):
            for start in range(0, acc.shape[1], width):
                sums_ref[row : row + 1, :] = jnp.sum(acc[:, start : start + width], axis=0, keepdims=True)
                row += 1


def drop(spots, middle, four, normal, slope, scale, grads, gain, bias, weight):
    slots, width = middle.shape
    units = four.shape[1]
    rows = 3 * units // width + 1
    return pl.pallas_call(
        functools.partial(drop_kernel, len(weight)),
        grid=(slots // TILE,),
        out_shape=(
            jax.ShapeDtypeStruct((slots, width), jnp.bfloat16),
            jax.ShapeDtypeStruct((slots, units), jnp.bfloat16),
            jax.ShapeDtypeStruct((rows, width), jnp.float32),
        ),
        in_specs=[SCALARS, rows_of(width)]
        + [rows_of(units)] * 3
        + [rows_of(128), rows_of(width), whole((1, units)), whole((1, width))]
        + [ANY] * len(weight),
        out_specs=(rows_of(width), rows_of(units), whole((rows, width))),
        scratch_shapes=[
            pltpu.VMEM((units, width), jnp.bfloat16),
            pltpu.VMEM((TILE, units), jnp.float32),
            pltpu.VMEM((8, units), jnp.float32),
            pltpu.VMEM((8, units), jnp.float32),
            pltpu.VMEM((8, units), jnp.float32),
            pltpu.VMEM((8, width), jnp.float32),
            pltpu.SemaphoreType.DMA((40,)),
        ],
        compiler_params=grant(58),
        cost_estimate=cost(4 * slots * width * units, 40 * slots * width),
        name="drop",
    )(spots, middle, four, normal, slope, scale, grads, gain, bias, *weight)


def settle_kernel(count, rows, spots_ref, up_ref, middle_ref, grad_ref, attended_ref, ffn_gain_ref, mid_gain_ref, core_ref, three_ref, columns_ref, *refs):
    sources = refs[:count]
    (total_ref, branch_ref, back_ref, sums_ref), refs = refs[count : count + 4], refs[count + 4 :]
    outer_refs, (up_weight, out_weight, acc, up_sem, out_sem) = refs[:-5], refs[-5:]

    @pl.when(first())
    def _():
        run_all(
            fetch(spots_ref, sources, out_weight, out_sem)
            + fetch(spots_ref, sources, up_weight, up_sem, out_weight.shape[1])
        )
        acc[...] = jnp.zeros_like(acc)

    three = dot(up_ref[...], up_weight[...], NT)
    outer_kernel(rows, core_ref, three_ref, columns_ref, *outer_refs)
    normal, scale = standardize(middle_ref[...])
    acc[0] += fold_rows(three * normal)
    acc[1] += fold_rows(three)
    total = wide(grad_ref[...]) + standardize_back(three, normal, scale, ffn_gain_ref[...])
    total_ref[...] = total
    branch = low(total)
    branch_ref[...] = branch
    acc[2] += fold_rows(wide(branch))
    two = dot(branch, out_weight[...], NT)
    normal, scale = standardize(attended_ref[...])
    acc[3] += fold_rows(two * normal)
    acc[4] += fold_rows(two)
    back_ref[...] = low(standardize_back(two, normal, scale, mid_gain_ref[...]))

    @pl.when(pl.program_id(0) == pl.num_programs(0) - 1)
    def _():
        sums_ref[...] = jnp.zeros_like(sums_ref)
        for row in range(5):
            sums_ref[row : row + 1, :] = jnp.sum(acc[row], axis=0, keepdims=True)


def settle(spots, core, up, middle, grads, attended, ffn_gain, mid_gain, three, rows, weight):
    slots, width = middle.shape
    units = up.shape[1]
    step = units * TILE // slots
    if rows is None:
        outer_shape = (jax.ShapeDtypeStruct((width, units), jnp.float32),)
        outer_specs = (pl.BlockSpec((width, step), lambda block: (0, block)),)
    else:
        outer_shape = (jax.ShapeDtypeStruct((width // (2 * rows), rows, units), jnp.bfloat16),) * 2
        outer_specs = (pl.BlockSpec((width // (2 * rows), rows, step), lambda block: (0, 0, block)),) * 2
    return pl.pallas_call(
        functools.partial(settle_kernel, len(weight), rows),
        grid=(slots // TILE,),
        out_shape=(
            jax.ShapeDtypeStruct((slots, width), jnp.float32),
            jax.ShapeDtypeStruct((slots, width), jnp.bfloat16),
            jax.ShapeDtypeStruct((slots, width), jnp.bfloat16),
            jax.ShapeDtypeStruct((8, width), jnp.float32),
            *outer_shape,
        ),
        in_specs=[SCALARS, rows_of(units)]
        + [rows_of(width)] * 3
        + [whole((1, width))] * 2
        + [SCALARS, whole((slots, width)), pl.BlockSpec((slots, step), lambda block: (0, block))]
        + [ANY] * len(weight),
        out_specs=(rows_of(width),) * 3 + (whole((8, width)), *outer_specs),
        scratch_shapes=[
            pltpu.VMEM((width, units), jnp.bfloat16),
            pltpu.VMEM((width, width), jnp.bfloat16),
            pltpu.VMEM((5, 8, width), jnp.float32),
            pltpu.SemaphoreType.DMA((40,)),
            pltpu.SemaphoreType.DMA((40,)),
        ],
        compiler_params=grant(46),
        cost_estimate=cost(2 * slots * width * (2 * units + width), 50 * slots * width),
        name="settle",
    )(spots, up, middle, grads, attended, ffn_gain, mid_gain, core, three, up, *weight)


def finish_kernel(count, spots_ref, q_ref, k_ref, v_ref, x_ref, total_ref, gain_ref, *refs):
    sources, (out_ref, sums_ref, weight_ref, acc, sem) = refs[:count], refs[count:]

    @pl.when(first())
    def _():
        run_all(fetch(spots_ref, sources, weight_ref, sem))
        acc[...] = jnp.zeros_like(acc)

    width = x_ref.shape[1]
    one = dot(q_ref[...], weight_ref[:, :width], NT)
    one = one + dot(k_ref[...], weight_ref[:, width : 2 * width], NT)
    one = one + dot(v_ref[...], weight_ref[:, 2 * width :], NT)
    normal, scale = standardize(wide(x_ref[...]))
    acc[0] += fold_rows(one * normal)
    acc[1] += fold_rows(one)
    acc[2] += fold_rows(wide(q_ref[...]))
    acc[3] += fold_rows(wide(v_ref[...]))
    out_ref[...] = total_ref[...] + standardize_back(one, normal, scale, gain_ref[...])

    @pl.when(pl.program_id(0) == pl.num_programs(0) - 1)
    def _():
        sums_ref[...] = jnp.zeros_like(sums_ref)
        for row in range(4):
            sums_ref[row : row + 1, :] = jnp.sum(acc[row], axis=0, keepdims=True)


def finish(spots, grad_q, grad_k, grad_v, tokens, total, gain, weight):
    slots, width = tokens.shape
    return pl.pallas_call(
        functools.partial(finish_kernel, len(weight)),
        grid=(slots // TILE,),
        out_shape=(
            jax.ShapeDtypeStruct((slots, width), jnp.float32),
            jax.ShapeDtypeStruct((8, width), jnp.float32),
        ),
        in_specs=[SCALARS]
        + [rows_of(width)] * 5
        + [whole((1, width))]
        + [ANY] * len(weight),
        out_specs=(rows_of(width), whole((8, width))),
        scratch_shapes=[
            pltpu.VMEM((width, 3 * width), jnp.bfloat16),
            pltpu.VMEM((4, 8, width), jnp.float32),
            pltpu.SemaphoreType.DMA((40,)),
        ],
        compiler_params=grant(58),
        cost_estimate=cost(6 * slots * width * width, 24 * slots * width),
        name="finish",
    )(spots, grad_q, grad_k, grad_v, tokens, total, gain, *weight)


def outer_kernel(rows, core_ref, left_ref, right_ref, *out_refs):
    product = dot(left_ref[...], right_ref[...], TN)
    if rows is None:
        out_refs[0][...] = product.astype(out_refs[0].dtype)
        return
    near = core_ref[0] == 0
    for chip in range(product.shape[0] // (2 * rows)):
        one = low(product[chip * 2 * rows : chip * 2 * rows + rows, :])
        two = low(product[chip * 2 * rows + rows : (chip + 1) * 2 * rows, :])
        out_refs[0][chip] = jnp.where(near, one, two)
        out_refs[1][chip] = jnp.where(near, two, one)


def outer(core, left, right, rows, name, dtype=jnp.float32):
    slots, height = left.shape
    columns = right.shape[1]
    step = min(height, columns)
    tall = height > columns
    left_spec = pl.BlockSpec((slots, step), (lambda block: (0, block)) if tall else (lambda block: (0, 0)))
    right_spec = pl.BlockSpec((slots, step), (lambda block: (0, 0)) if tall else (lambda block: (0, block)))
    if rows is None:
        out_shape = (jax.ShapeDtypeStruct((height, columns), dtype),)
        out_specs = (pl.BlockSpec((step, step), (lambda block: (block, 0)) if tall else (lambda block: (0, block))),)
    else:
        out_shape = (jax.ShapeDtypeStruct((height // (2 * rows), rows, columns), jnp.bfloat16),) * 2
        out_specs = (
            pl.BlockSpec(
                (step // (2 * rows), rows, step),
                (lambda block: (block, 0, 0)) if tall else (lambda block: (0, 0, block)),
            ),
        ) * 2
    return pl.pallas_call(
        functools.partial(outer_kernel, rows),
        grid=(max(height, columns) // step,),
        out_shape=out_shape,
        in_specs=[SCALARS, left_spec, right_spec],
        out_specs=out_specs,
        compiler_params=grant(40),
        cost_estimate=cost(2 * slots * height * columns, 2 * slots * (height + columns) + 4 * height * columns),
        name=name,
    )(core, left, right)


def outer_three_kernel(rows, core_ref, left_ref, q_ref, k_ref, v_ref, *out_refs):
    width = q_ref.shape[1]
    for part, right_ref in enumerate((q_ref, k_ref, v_ref)):
        columns = slice(part * width, (part + 1) * width)
        product = dot(left_ref[...], right_ref[...], TN)
        if rows is None:
            out_refs[0][:, columns] = product
            continue
        near = core_ref[0] == 0
        for chip in range(product.shape[0] // (2 * rows)):
            first_rows = low(product[chip * 2 * rows : chip * 2 * rows + rows, :])
            second_rows = low(product[chip * 2 * rows + rows : (chip + 1) * 2 * rows, :])
            out_refs[0][chip, :, columns] = jnp.where(near, first_rows, second_rows)
            out_refs[1][chip, :, columns] = jnp.where(near, second_rows, first_rows)


def outer_three(core, left, grads, rows):
    slots, width = left.shape
    if rows is None:
        out_shape = (jax.ShapeDtypeStruct((width, 3 * width), jnp.float32),)
    else:
        out_shape = (jax.ShapeDtypeStruct((width // (2 * rows), rows, 3 * width), jnp.bfloat16),) * 2
    return pl.pallas_call(
        functools.partial(outer_three_kernel, rows),
        out_shape=out_shape,
        in_specs=[SCALARS] + [pl.BlockSpec(memory_space=pltpu.VMEM)] * 4,
        out_specs=(pl.BlockSpec(memory_space=pltpu.VMEM),) * len(out_shape),
        compiler_params=grant(24),
        cost_estimate=cost(6 * slots * width * width, 8 * slots * width + 12 * width * width),
        name="outer_three",
    )(core, left, *grads)


def halves(values):
    lane = lax.broadcasted_iota(jnp.int32, values.shape, 1)
    zero = jnp.zeros_like(values)
    return jnp.where(lane < HD, values, zero), jnp.where(lane >= HD, values, zero)


def segment_starts(lengths_ref, position):
    start = jnp.zeros_like(position)
    end = jnp.int32(0)
    for index in range(lengths_ref.shape[1] - 1):
        end = end + lengths_ref[0, index]
        start = jnp.where(position >= end, end, start)
    return start


def fill_bias(tile, slots, lengths_ref, bias_ref):
    for block in range(slots // tile):
        reach = (block + 1) * tile
        spot = block * (block + 1) // 2 * tile
        query = lax.broadcasted_iota(jnp.int32, (reach, tile), 1) + block * tile
        key = lax.broadcasted_iota(jnp.int32, (reach, tile), 0)
        start = segment_starts(lengths_ref, lax.broadcasted_iota(jnp.int32, (1, tile), 1) + block * tile)
        bias_ref[spot : spot + reach, :] = jnp.where((key <= query) & (key >= start), 0.0, NEGATIVE)


def attend_kernel(tile, lengths_ref, q_ref, k_ref, v_ref, out_ref, total_ref, bias_ref):
    slots = q_ref.shape[0]

    @pl.when(pl.program_id(0) == 0)
    def _():
        fill_bias(tile, slots, lengths_ref, bias_ref)

    values = halves(v_ref[...])
    steps = [(block, head) for block in range(slots // tile) for head in range(2)]

    def score(block, head):
        reach = (block + 1) * tile
        spot = block * (block + 1) // 2 * tile
        query = halves(q_ref[block * tile : reach, :] * jnp.bfloat16(1.0 / math.sqrt(HD)))[head]
        return dot(k_ref[:reach, :], query, NT) + bias_ref[spot : spot + reach, :]

    ahead = score(*steps[0])
    for number, (block, head) in enumerate(steps):
        reach = (block + 1) * tile
        rows = slice(block * tile, reach)
        scores = ahead
        if number + 1 < len(steps):
            ahead = score(*steps[number + 1])
        top = jnp.max(scores, axis=0, keepdims=True)
        fresh = jnp.exp(scores - top)
        mass = jnp.sum(fresh, axis=0, keepdims=True)
        part = dot(values[head][:reach, :], fresh.astype(jnp.bfloat16), TN) * (1.0 / mass)
        mixed = part if head == 0 else mixed + part
        total_ref[0, head : head + 1, rows] = top + jnp.log(mass)
        if head:
            out_ref[rows, :] = mixed.T


def attend_forward(lengths, projected, begin, pairs, tile=256):
    slots, every = projected.shape[0], projected.shape[1] // (6 * HD)
    blocks = slots // tile
    column = lambda offset: pl.BlockSpec((slots, 2 * HD), lambda pair: (0, offset + pair))
    return pl.pallas_call(
        functools.partial(attend_kernel, tile),
        grid=(pairs,),
        out_shape=(
            jax.ShapeDtypeStruct((slots, 2 * HD * pairs), jnp.float32),
            jax.ShapeDtypeStruct((pairs, 8, slots), jnp.float32),
        ),
        in_specs=[pl.BlockSpec(memory_space=pltpu.SMEM), *[column(begin + part * every) for part in range(3)]],
        out_specs=(column(0), pl.BlockSpec((1, 8, slots), lambda pair: (pair, 0, 0))),
        scratch_shapes=[pltpu.VMEM((tile * blocks * (blocks + 1) // 2, tile), jnp.float32)],
        compiler_params=grant(20),
        cost_estimate=cost(20 * 10**9, 8 * 10**6),
        name="attend_forward",
    )(lengths, projected, projected, projected)


def attend_back_kernel(tile, lengths_ref, q_ref, k_ref, v_ref, g_ref, out_ref, total_ref, gq_ref, gk_ref, gv_ref, bias_ref, gk_acc, gv_acc):
    slots = q_ref.shape[0]

    @pl.when(pl.program_id(0) == 0)
    def _():
        fill_bias(tile, slots, lengths_ref, bias_ref)

    weighed = (g_ref[...].astype(jnp.float32) * out_ref[...]).T
    deltas = [
        jnp.sum(weighed[:HD, :], axis=0, keepdims=True),
        jnp.sum(weighed[HD:, :], axis=0, keepdims=True),
    ]
    keys = halves(k_ref[...])
    steps = [(block, head) for block in reversed(range(slots // tile)) for head in range(2)]

    def begin(block, head):
        reach = (block + 1) * tile
        spot = block * (block + 1) // 2 * tile
        rows = slice(block * tile, reach)
        query = halves(q_ref[rows, :] * jnp.bfloat16(1.0 / math.sqrt(HD)))[head]
        grad = halves(g_ref[rows, :])[head]
        scores = dot(k_ref[:reach, :], query, NT) + bias_ref[spot : spot + reach, :]
        return query, grad, scores, dot(v_ref[:reach, :], grad, NT)

    ahead = begin(*steps[0])
    for number, (block, head) in enumerate(steps):
        reach = (block + 1) * tile
        rows = slice(block * tile, reach)
        query, grad, scores, grad_soft = ahead
        if number + 1 < len(steps):
            ahead = begin(*steps[number + 1])
        soft = jnp.exp(scores - total_ref[0, head : head + 1, rows])
        grad_scores = (soft * (grad_soft - deltas[head][:, rows])).astype(jnp.bfloat16)
        gv = dot(soft.astype(jnp.bfloat16), grad)
        gk = dot(grad_scores, query)
        if number == 0:
            gk_acc[...] = gk
            gv_acc[...] = gv
        else:
            gk_acc[:reach, :] += gk
            gv_acc[:reach, :] += gv
        part = dot(keys[head][:reach, :], grad_scores, TN)
        gq = part if head == 0 else gq + part
        if head:
            gq_ref[rows, :] = (gq.T * (1.0 / math.sqrt(HD))).astype(jnp.bfloat16)
    gk_ref[...] = gk_acc[...].astype(jnp.bfloat16)
    gv_ref[...] = gv_acc[...].astype(jnp.bfloat16)


def attend_backward(lengths, projected, grad_out, attended, totals, begin, tile=256):
    slots, width = attended.shape
    pairs, every = width // (2 * HD), projected.shape[1] // (6 * HD)
    blocks = slots // tile
    column = lambda offset: pl.BlockSpec((slots, 2 * HD), lambda pair: (0, offset + pair))
    return pl.pallas_call(
        functools.partial(attend_back_kernel, tile),
        grid=(pairs,),
        out_shape=(jax.ShapeDtypeStruct((slots, width), jnp.bfloat16),) * 3,
        in_specs=[
            pl.BlockSpec(memory_space=pltpu.SMEM),
            *[column(begin + part * every) for part in range(3)],
            column(begin),
            column(0),
            pl.BlockSpec((1, 8, slots), lambda pair: (pair, 0, 0)),
        ],
        out_specs=(column(0),) * 3,
        scratch_shapes=[
            pltpu.VMEM((tile * blocks * (blocks + 1) // 2, tile), jnp.float32),
            pltpu.VMEM((slots, 2 * HD), jnp.float32),
            pltpu.VMEM((slots, 2 * HD), jnp.float32),
        ],
        compiler_params=grant(22),
        cost_estimate=cost(28 * 10**9, 12 * 10**6),
        name="attend_backward",
    )(lengths, projected, projected, projected, grad_out, attended, totals)


AXES = ("dp", "fsdp")


def place():
    outer_index, inner_index = lax.axis_index("dp"), lax.axis_index("fsdp")
    return outer_index // 2, outer_index % 2, inner_index // 2, inner_index % 2


def send(values, dz=0, dx=0, dy=0, dc=0):
    pairs = []
    for z in range(4):
        for x in range(2):
            for y in range(2):
                for c in range(2):
                    here = ((z * 2 + x) * 2 + y) * 2 + c
                    there = ((((z + dz) % 4) * 2 + (x ^ dx)) * 2 + (y ^ dy)) * 2 + (c ^ dc)
                    pairs.append((here, there))
    return lax.ppermute(values, AXES, pairs)


def index_of(z, x, y, c):
    return ((z * 2 + x) * 2 + y) * 2 + c


CHIPS = [[index_of(z, x, y, c) for z in range(4) for x in range(2) for y in range(2)] for c in range(2)]
COLUMNS_Z = [[index_of(z, x, y, c) for z in range(4)] for x in range(2) for y in range(2) for c in range(2)]


def part_spots():
    z, x, y, c = place()
    spots = []
    for part in range(8):
        dx, dy, dc = part >> 2 & 1, part >> 1 & 1, part & 1
        for step in range(4):
            spots.append(((((z - step) % 4) * 2 + (x ^ dx)) * 2 + (y ^ dy)) * 2 + (c ^ dc))
    return jnp.stack(spots).astype(jnp.int32)


def after(value, *others):
    return lax.optimization_barrier((value, *others))[0]


def send_z(shard):
    return [shard] + [send(shard, dz=step) for step in (1, 2, 3)]


def gather_z(shards, *gate):
    return jnp.stack(after(shards, *gate))


def gather_near(own):
    return own, send(own, dy=1), send(own, dx=1), send(own, dx=1, dy=1)


def gather_core(parts):
    both = []
    for part in parts:
        both += [part, send(part, dc=1)]
    return both


def chips_kernel(way, place_ref, *refs):
    x, y = place_ref[1], place_ref[2]
    count = 4 if way == "both" else 2
    sources, out_refs = refs[:-count], refs[-count:]
    start = 0
    for kept_ref, got_ref in zip(sources[::2], sources[1::2]):
        columns = slice(start, start + kept_ref.shape[2])
        start = columns.stop
        total = lambda z, x, y: low(wide(kept_ref[(z * 2 + x) * 2 + y]) + wide(got_ref[(z * 2 + x) * 2 + y]))
        for z in range(4):
            for flip, out_ref in enumerate(out_refs):
                if way == "x":
                    for other in range(2):
                        out_ref[z * 2 + other, :, columns] = total(z, x ^ flip, other)
                elif way == "y":
                    for other in range(2):
                        out_ref[z * 2 + other, :, columns] = total(z, other, y ^ flip)
                else:
                    out_ref[z, :, columns] = total(z, x ^ (flip >> 1), y ^ (flip & 1))


def planes_kernel(count, place_ref, *refs):
    sources, mine_ref, out_refs = refs[:count], refs[count], refs[count + 1 :]
    for step in range(4):
        z = (place_ref[0] + step) & 3
        total = wide(sources[0][z])
        for source in sources[1:]:
            total = total + wide(source[z])
        if step == 0:
            mine_ref[...] = total
        else:
            out_refs[step - 1][...] = low(total)


def plane_kernel(count, place_ref, *refs):
    sources, out_ref = refs[:count], refs[count]
    for z in range(4):
        total = wide(sources[0][z])
        for source in sources[1:]:
            total = total + wide(source[z])
        out_ref[z] = low(total)


def small_call(kernel, spot, arrays, out_shapes, name):
    vmem = pl.BlockSpec(memory_space=pltpu.VMEM)
    moved = sum(math.prod(a.shape) * a.dtype.itemsize for a in (*arrays, *out_shapes))
    return pl.pallas_call(
        kernel,
        out_shape=tuple(out_shapes),
        in_specs=[SCALARS] + [vmem] * len(arrays),
        out_specs=(vmem,) * len(out_shapes),
        compiler_params=grant(20),
        cost_estimate=cost(0, moved),
        name=name,
    )(spot, *arrays)


class Sum:
    def __init__(self, spot, kept, given, way, name):
        self.spot, self.way, self.name = spot, way, name
        self.rows, self.columns = kept.shape[1], 0
        self.arrays = []
        self.add(kept, given)

    def add(self, kept, given):
        self.kept = kept
        self.columns += kept.shape[2]
        self.arrays += [kept, send(given, dc=1)]

    def shapes(self, blocks, count):
        return [jax.ShapeDtypeStruct((blocks, self.rows, self.columns), jnp.bfloat16)] * count

    def chips(self, *gate):
        kernel = functools.partial(chips_kernel, self.way)
        out = self.shapes(4, 4) if self.way == "both" else self.shapes(8, 2)
        out = small_call(kernel, self.spot, (after(self.arrays[0], *gate), *self.arrays[1:]), out, "chips_" + self.name)
        if self.way == "both":
            own, to_y, to_x, to_xy = out
            self.parts = [own, send(to_y, dy=1), send(to_x, dx=1), send(to_xy, dx=1, dy=1)]
        else:
            self.pair = out[0], send(out[1], dx=int(self.way == "x"), dy=int(self.way == "y"))
        return out[0]

    def planes(self, *gate):
        self.parts[0] = after(self.parts[0], *gate)
        shape = (self.rows, self.columns)
        out = [jax.ShapeDtypeStruct(shape, jnp.float32)] + [jax.ShapeDtypeStruct(shape, jnp.bfloat16)] * 3
        kernel = functools.partial(planes_kernel, len(self.parts))
        mine, *others = small_call(kernel, self.spot, self.parts, out, "planes_" + self.name)
        self.others = [send(other, dz=step + 1) for step, other in enumerate(others)]
        self.mine = mine
        return mine

    def done(self):
        return self.mine + sum(wide(other) for other in self.others)

    def plane(self, *gate):
        self.parts[0] = after(self.parts[0], *gate)
        kernel = functools.partial(plane_kernel, len(self.parts))
        (total,) = small_call(kernel, self.spot, self.parts, self.shapes(4, 1), "plane_" + self.name)
        parts = lax.all_to_all(total, AXES, 0, 0, tiled=True, axis_index_groups=COLUMNS_Z)
        return total, jnp.sum(wide(parts), axis=0)


WIDE = ("mid_gain", "mid_bias", "out_bias", "ffn_gain", "ffn_bias", "down_bias", "in_gain", "in_bias")
DEEP = ("up_bias", "hid_gain", "hid_bias")


def spread_row(packed, width, count):
    lane = lax.broadcasted_iota(jnp.int32, (1, count), 1)
    owner = jnp.zeros_like(lane)
    for device in range(1, 32):
        owner = owner + (lane >= device * width).astype(jnp.int32)
    inside = lane - owner * width
    pick = lax.broadcasted_iota(jnp.int32, (128, count), 0) == inside
    everyone = dot(packed, low(jnp.where(pick, 1.0, 0.0)))
    owned = lax.broadcasted_iota(jnp.int32, (32, count), 0) == owner
    return jnp.sum(jnp.where(owned, everyone, 0.0), axis=0, keepdims=True)


def vectors_kernel(spots_ref, *refs):
    sources, (wide_ref, qkv_ref, deep_ref, weight_ref, landed, everything, sem, weight_sem) = refs[:8], refs[8:]
    lanes = landed.shape[3]
    copies = [
        pltpu.make_async_copy(
            source.at[:, :, pl.ds(source.shape[2] - lanes, lanes)], landed.at[part], sem.at[part]
        )
        for part, source in enumerate(sources)
    ]
    laid = [
        pltpu.make_async_copy(
            source.at[step, :, pl.ds(0, weight_ref.shape[2])],
            weight_ref.at[spots_ref[part * 4 + step]],
            weight_sem.at[part * 4 + step],
        )
        for part, source in enumerate(sources)
        for step in range(4)
    ]
    for copy in laid:
        copy.start()
    run_all(copies)
    for part in range(8):
        for step in range(4):
            everything[spots_ref[part * 4 + step]] = wide(landed[part, step])
    row = lambda number: low(everything[:, number, :])
    width = wide_ref.shape[1]
    for number in range(8):
        wide_ref[number : number + 1, :] = spread_row(row(number), width // 32, width)
    both = spread_row(row(8), width // 16, 2 * width)
    qkv_ref[:, :width] = both[:, :width]
    qkv_ref[:, width : 2 * width] = jnp.zeros((1, width), jnp.float32)
    qkv_ref[:, 2 * width :] = both[:, width:]
    units = deep_ref.shape[2]
    for number in range(3):
        deep_ref[number] = spread_row(row(9 + number), units // 32, units)
    for copy in laid:
        copy.wait()


def pack_vectors(shards, rows):
    listed = [shards[name] for name in WIDE + ("qv_bias",) + DEEP]
    packed = jnp.stack([jnp.pad(entry, (0, 128 - entry.shape[0])) for entry in listed])
    return jnp.pad(packed, ((0, rows - packed.shape[0]), (0, 0)))


def unpack_first(spots, parts, width, units):
    vmem = pl.BlockSpec(memory_space=pltpu.VMEM)
    rows = parts[0].shape[1]
    *vectors, weight = pl.pallas_call(
        vectors_kernel,
        out_shape=(
            jax.ShapeDtypeStruct((8, width), jnp.float32),
            jax.ShapeDtypeStruct((1, 3 * width), jnp.float32),
            jax.ShapeDtypeStruct((3, 1, units), jnp.float32),
            jax.ShapeDtypeStruct((32, rows, 3 * width), jnp.bfloat16),
        ),
        in_specs=[SCALARS] + [ANY] * 8,
        out_specs=(vmem,) * 4,
        scratch_shapes=[
            pltpu.VMEM((8, 4, rows, 128), jnp.bfloat16),
            pltpu.VMEM((32, rows, 128), jnp.float32),
            pltpu.SemaphoreType.DMA((8,)),
            pltpu.SemaphoreType.DMA((32,)),
        ],
        compiler_params=grant(16),
        cost_estimate=cost(10**8, 10**7),
        name="unpack",
    )(spots, *parts)
    return vectors, weight.reshape(32 * rows, 3 * width)


def sum_rows_core(rows):
    return rows + send(rows, dc=1)


def sum_rows_near(rows):
    return rows + send(rows, dy=1) + (send(rows, dx=1) + send(rows, dx=1, dy=1))


def sum_rows_z(rows):
    return rows + send(rows, dz=1) + (send(rows, dz=2) + send(rows, dz=3))


def owners_kernel(core_ref, deep_ref, mid_ref, end_ref, *out_refs):
    near = core_ref[0] == 0
    width = mid_ref.shape[1]
    per = (deep_ref.shape[0] - 1) // 3
    row = lambda ref, number: ref[number : number + 1, :]
    narrow = [row(deep_ref, 3 * per)] + [row(mid_ref, number) for number in range(5)] + [row(end_ref, number) for number in range(2)]
    broad = [
        jnp.concatenate([row(deep_ref, number * per + part) for part in range(per)], axis=1) for number in range(3)
    ]
    pair = [jnp.concatenate([row(end_ref, 2), row(end_ref, 3)], axis=1)]
    start = 0
    for group in (narrow, broad, pair):
        group = group + [jnp.zeros_like(group[0])] * (8 - len(group))
        stacked = jnp.concatenate(group, axis=0)
        share = stacked.shape[1] // 32
        stacked = jnp.concatenate([stacked, jnp.zeros((8, 128), jnp.float32)], axis=1)
        blocks = [stacked[:, owner * share : owner * share + 128] for owner in range(32)]
        for chip in range(16):
            one, two = blocks[2 * chip], blocks[2 * chip + 1]
            out_refs[0][chip, start : start + 8, :] = jnp.where(near, one, two)
            out_refs[1][chip, start : start + 8, :] = jnp.where(near, two, one)
        start += 8


SUMMED = {
    "down_bias": 0,
    "ffn_gain": 1,
    "ffn_bias": 2,
    "out_bias": 3,
    "mid_gain": 4,
    "mid_bias": 5,
    "in_gain": 6,
    "in_bias": 7,
    "hid_gain": 8,
    "hid_bias": 9,
    "up_bias": 10,
    "qv_bias": 16,
}


def lay_vectors(core, deep, mid, end):
    vmem = pl.BlockSpec(memory_space=pltpu.VMEM)
    return pl.pallas_call(
        owners_kernel,
        out_shape=(jax.ShapeDtypeStruct((16, 24, 128), jnp.float32),) * 2,
        in_specs=[SCALARS] + [vmem] * 3,
        out_specs=(vmem,) * 2,
        compiler_params=grant(8),
        cost_estimate=cost(0, 10**6),
        name="owners",
    )(core, deep, mid, end)


def sum_vectors(kept, got):
    parts = lax.all_to_all(kept + got, AXES, 0, 0, tiled=True, axis_index_groups=CHIPS)
    return jnp.sum(parts, axis=0)


WEIGHTS = ("qkv_weight", "out_weight", "up_weight", "down_weight")
PARAMS = (
    "in_gain",
    "in_bias",
    "qkv_weight",
    "qv_bias",
    "mid_gain",
    "mid_bias",
    "out_weight",
    "out_bias",
    "ffn_gain",
    "ffn_bias",
    "up_weight",
    "up_bias",
    "hid_gain",
    "hid_bias",
    "down_weight",
    "down_bias",
)


def forward_staged(spots, tokens, lengths, shards):
    width = tokens.shape[1]
    units = 32 * shards["up_bias"].shape[0]
    rows = shards["qkv_weight"].shape[0]
    whole_piece = lambda shard: [lax.all_gather(shard, AXES, axis=0, tiled=True)]
    second_piece = whole_piece(jnp.concatenate([shards["out_weight"], shards["up_weight"]], axis=1))
    own = gather_z(send_z(shards["qkv_weight"]))
    own_vectors = gather_z(send_z(pack_vectors(shards, rows)))
    near_first = gather_near(jnp.concatenate([own, own_vectors], axis=2))
    vectors, weight = unpack_first(spots, gather_core(near_first), width, units)
    third_piece = send_z(after(shards["down_weight"], near_first))
    return ([weight], second_piece, third_piece), vectors


def forward_plain(spots, tokens, lengths, shards):
    width = tokens.shape[1]
    full = {name: lax.all_gather(shards[name], AXES, axis=0, tiled=True) for name in PARAMS}
    pieces = (
        [full["qkv_weight"]],
        [jnp.concatenate([full["out_weight"], full["up_weight"]], axis=1)],
        [full["down_weight"]],
    )
    full = {name: wide(full[name]) for name in PARAMS if name not in WEIGHTS}
    rows = jnp.stack([full[name] for name in WIDE])
    bias = full["qv_bias"]
    qkv_bias = jnp.concatenate([bias[:width], jnp.zeros((width,), jnp.float32), bias[width:]])[None]
    return pieces, (rows, qkv_bias, jnp.stack([full[name][None] for name in DEEP]))


def body(staged, tokens, lengths, cotangent, *params):
    shards = dict(zip(PARAMS, params))
    width = tokens.shape[1]
    pairs = width // (2 * HD)
    if staged:
        spot = jnp.stack(place()).astype(jnp.int32)
        core, spots = spot[3:4], part_spots()
    else:
        spots = core = jnp.zeros((1,), jnp.int32)
    run = forward_staged if staged else forward_plain
    pieces, (rows, qkv_bias, deep) = run(spots, tokens, lengths, shards)
    owned = {name: shards[name].shape[0] if staged else None for name in WEIGHTS}

    one, projected = project(spots, tokens, rows, qkv_bias, pieces[0])
    attended, totals = attend_forward(lengths, projected, 0, pairs)
    third_piece = pieces[2]
    if staged:
        third_piece = gather_z(third_piece, attended)
        near_third = gather_near(third_piece)
        attended = after(attended, third_piece)
    two, middle, three, four, normal, slope, scale = lift(
        spots, attended, tokens, rows, deep[0], deep[1], deep[2], pieces[1]
    )
    if staged:
        third_piece = gather_core(after(near_third, four))
        four = after(four, near_third)
    (down,) = outer(core, four, cotangent, None, "outer_down", jnp.bfloat16)
    if staged:
        middle = after(middle, down)
    out_tokens, up, deep_sums = drop(
        spots, middle, four, normal, slope, scale, cotangent, deep[1], rows[5:6], third_piece
    )
    total, branch, back, mid_sums, *up_sum = settle(
        spots, core, up, middle, cotangent, attended, rows[3:4], rows[0:1], three, owned["up_weight"], pieces[1]
    )
    if staged:
        up_sum = Sum(spot, *up_sum, "both", "up")
        two = after(two, up_sum.kept)
    out_sum = outer(core, two, branch, owned["out_weight"], "outer_out")
    if staged:
        up_sum.add(*out_sum)
        back = after(back, up_sum.chips(back))
    grads = attend_backward(lengths, projected, back, attended, totals, 0)
    qkv_sum = outer_three(core, one, grads, owned["qkv_weight"])
    if staged:
        kept, given = qkv_sum
        flag, up_total = up_sum.plane(kept)
        qkv_sum = Sum(spot, kept, after(given, flag), "both", "qkv")
        total = after(total, qkv_sum.chips())
    grad_tokens, end_sums = finish(spots, *grads, tokens, total, rows[6:7], pieces[0])
    down = lax.psum_scatter(down, AXES, scatter_dimension=0, tiled=True)
    summed = {"down_weight": wide(down)}
    if staged:
        units = 32 * shards["up_bias"].shape[0]
        kept, given = lay_vectors(core, deep_sums, mid_sums, end_sums)
        got = send(given, dc=1)
        flag = qkv_sum.planes(kept, up_total, down)
        summed["qkv_weight"] = qkv_sum.done()
        block = sum_vectors(kept, after(got, flag))
        summed["up_weight"], summed["out_weight"] = jnp.split(up_total, (units,), axis=1)
        summed.update({name: block[row, : shards[name].shape[0]] for name, row in SUMMED.items()})
    else:
        deep_rows = 3 * deep.shape[2] // width
        flat = deep_sums[:deep_rows].reshape(3, -1)
        vectors = dict(zip(("hid_gain", "hid_bias", "up_bias"), flat))
        vectors["down_bias"] = deep_sums[deep_rows]
        vectors.update(zip(("ffn_gain", "ffn_bias", "out_bias", "mid_gain", "mid_bias"), mid_sums))
        vectors.update(in_gain=end_sums[0], in_bias=end_sums[1], qv_bias=end_sums[2:4].reshape(-1))
        vectors.update(up_weight=up_sum[0], out_weight=out_sum[0], qkv_weight=qkv_sum[0])
        for name, vector in vectors.items():
            summed[name] = lax.psum_scatter(vector, AXES, scatter_dimension=0, tiled=True)
    return (out_tokens, grad_tokens) + tuple(summed[name] for name in PARAMS)


def solution(mesh):
    staged = (mesh.shape["dp"], mesh.shape["fsdp"]) == (8, 4)
    matrix, vector = P(AXES, None), P(AXES)
    placed = tuple(matrix if name in WEIGHTS else vector for name in PARAMS)
    return jax.shard_map(
        functools.partial(body, staged),
        mesh=mesh,
        in_specs=(matrix,) * 3 + placed,
        out_specs=(matrix,) * 2 + placed,
        check_vma=False,
    )
```
